32 devices in a mesh: ctx: 16 (over z, y, x), head: 2 (over core).
Axes of the slice: x: 2, y: 2, z: 4, core: 2. Of those that a mesh axis runs over, the one named last changes fastest.
Arguments:
- queries: bfloat16 [6144, 4096], P('ctx', 'head'), may hold values from -6 to 6
- key_heads: bfloat16 [6144, 1024], P('ctx', 'head'), may hold values from -5 to 5
- value_heads: bfloat16 [6144, 1024], P('ctx', 'head'), may hold values from -6 to 6
- doc_units: int32 [6], replicated, may hold values from 1 to 24, as said below
- w_out: bfloat16 [4096, 4096], P('head'), may hold values from -0.09375 to 0.09375
Outputs:
- layer_out: bfloat16 [6144, 4096], P(('ctx', 'head'))
The draws below stay inside these ranges and needn't reach their ends.
Inputs may be any that keep to these rules, and one draw needn't show every extreme that they name: `doc_units`: the lengths, in units of 128 tokens, of the 6 documents laid end to end; they sum to 48; exactly one document has 24 units, it covers token 3072, and every other one has at most 12.
All inputs are finite; a program needn't handle non-finite values.
Results may differ from the reference program's by a relative error of at most 0.018.
Values may be sent and summed in bfloat16 or wider, within the bound.
No kernel may reach another device: no remote copies, remote signals or barrier semaphores. Data moves between devices by JAX's collectives and lax.ppermute only.
A program may use at most 64 MiB of HBM per device.

```python
import math
import jax
import jax.numpy as jnp
from jax import lax

D = 4096
HQ = 32
KVH = 8
HD = 128
TOK_DEV = 384
UNIT = 128
SPAN = 8
TOKENS = 6144
MOST_UNITS = 24
NDOCS = 6
N_HEAD = 2


def doc_plan(key):
    total_units = TOKENS // UNIT
    longest = MOST_UNITS
    remain = total_units - longest
    grain = longest // 2
    others = NDOCS - 1
    score_key, jitter_key = jax.random.split(key)
    jitter = jax.random.randint(jitter_key, (), -(grain // 2), grain // 2 + 1, dtype=jnp.int32)
    anchor = (total_units // 2 - longest // 2 + jitter).astype(jnp.int32)
    candidate = jnp.arange(1, remain, dtype=jnp.int32)
    forced = (candidate - anchor) % grain == 0
    raw_score = jax.random.randint(score_key, (remain - 1,), 0, 4 * remain, dtype=jnp.int32)
    ranked = jnp.where(forced, 8 * remain, raw_score) * remain + candidate
    top_values, picked = lax.top_k(ranked, others - 1)
    cuts = jnp.sort(candidate[picked])
    bounds = jnp.concatenate([jnp.zeros((1,), jnp.int32), cuts, jnp.full((1,), remain, jnp.int32)])
    pieces = bounds[1:] - bounds[:-1]
    place = jnp.sum((cuts <= anchor).astype(jnp.int32)).astype(jnp.int32)
    order = jnp.arange(NDOCS, dtype=jnp.int32)
    source = jnp.clip(order - (order > place).astype(jnp.int32), 0, others - 1)
    return jnp.where(order == place, longest, pieces[source]).astype(jnp.int32)


def draw_doc_units(key, part):
    return doc_plan(jax.random.fold_in(key, 7))


def draw_queries(key, part):
    shape = (TOKENS, HQ * HD)
    base = jax.random.normal(jax.random.fold_in(key, 1), shape, jnp.float32) * 2.0
    return jnp.clip(base, -6.0, 6.0).astype(jnp.bfloat16)


def draw_key_heads(key, part):
    shape = (TOKENS, KVH * HD)
    base = jax.random.normal(jax.random.fold_in(key, 2), shape, jnp.float32)
    return jnp.clip(base, -5.0, 5.0).astype(jnp.bfloat16)


def levels(stream_key, shape, shards, smallest, largest):
    def one(position, parts):
        steps = jax.random.uniform(jax.random.fold_in(jax.random.fold_in(stream_key, 6), position), (parts,), jnp.float32, smallest / len(shards), largest / len(shards))
        return jnp.repeat(jnp.exp(steps), shape[position] // parts).reshape((-1,) + (1,) * (len(shape) - position - 1))

    level = one(*shards[0])
    for cut in shards[1:]:
        level = level * one(*cut)
    return level


def gaussian(own_key, dims, width, bound, cuts=(), kind=jnp.bfloat16):
    drawn = jax.random.normal(own_key, dims, jnp.float32) * width
    if len(cuts) > 0:
        drawn = levels(own_key, dims, cuts, -0.22, 0.18) * drawn
    return jnp.clip(drawn, min=-bound, max=bound).astype(kind)


def setup_inputs(seed: int = 0) -> dict:
    key_list = jax.random.split(jax.random.key(seed), 6)
    queries = draw_queries(jax.random.fold_in(key_list[5], 71), 0)
    key_heads = draw_key_heads(jax.random.fold_in(key_list[5], 71), 0)
    value_heads = gaussian(key_list[2], (TOKENS, KVH * HD), 1.0, 6.0, ((0, 16), (1, 2)))
    doc_units = draw_doc_units(jax.random.fold_in(key_list[5], 71), 0)
    w_out = gaussian(key_list[4], (HQ * HD, D), (HQ * HD) ** -0.5, 0.09375, ((0, 2),))
    return {"queries": queries, "key_heads": key_heads, "value_heads": value_heads, "doc_units": doc_units, "w_out": w_out}


def reference(queries, key_heads, value_heads, doc_units, w_out):
    tok_count = queries.shape[0]
    group_size = HQ // KVH
    doc_tokens = (doc_units * UNIT).astype(jnp.int32)
    doc_ends = jnp.cumsum(doc_tokens).astype(jnp.int32)
    positions = jnp.arange(tok_count, dtype=jnp.int32)
    doc_start = lax.optimization_barrier(jnp.sum(jnp.where(doc_ends[None, :] <= positions[:, None], doc_tokens[None, :], 0), axis=1)).astype(jnp.int32)
    window = SPAN * TOK_DEV
    padding = jnp.zeros((window, key_heads.shape[1]), key_heads.dtype)
    key_padded = jnp.concatenate([padding, key_heads], axis=0)
    value_padded = jnp.concatenate([padding, value_heads], axis=0)
    block_count = tok_count // TOK_DEV
    score_scale = 1.0 / math.sqrt(HD)

    def one_block(number):
        block_id = number // KVH
        head_id = number % KVH
        row_first = (block_id * TOK_DEV).astype(jnp.int32)
        query_col = (head_id * group_size * HD).astype(jnp.int32)
        key_col = (head_id * HD).astype(jnp.int32)
        query_block = lax.dynamic_slice(queries, (row_first, query_col), (TOK_DEV, group_size * HD))
        query_block = query_block.reshape(TOK_DEV, group_size, HD).astype(jnp.float32)
        key_block = lax.dynamic_slice(key_padded, (row_first, key_col), (window + TOK_DEV, HD)).astype(jnp.float32)
        value_block = lax.dynamic_slice(value_padded, (row_first, key_col), (window + TOK_DEV, HD)).astype(jnp.float32)
        key_pos = row_first - window + jnp.arange(window + TOK_DEV, dtype=jnp.int32)
        query_pos = row_first + jnp.arange(TOK_DEV, dtype=jnp.int32)
        query_start = lax.dynamic_slice(doc_start, (row_first,), (TOK_DEV,))
        scores = jnp.einsum('qgd,kd->gqk', query_block, key_block) * score_scale
        allowed = (key_pos[None, :] >= query_start[:, None]) & (key_pos[None, :] <= query_pos[:, None])
        scores = jnp.where(allowed[None], scores, -1e+30)
        row_max = lax.optimization_barrier(jnp.max(scores, axis=-1, keepdims=True))
        weights = jnp.exp(scores - row_max)
        row_sum = lax.optimization_barrier(jnp.sum(weights, axis=-1))
        rounded = lax.optimization_barrier(weights.astype(jnp.bfloat16)).astype(jnp.float32)
        mixed = jnp.einsum('gqk,kd->qgd', rounded, value_block)
        result = mixed / jnp.transpose(row_sum)[:, :, None]
        return result.astype(jnp.bfloat16).reshape(TOK_DEV, group_size * HD)
    pieces = lax.map(one_block, jnp.arange(block_count * KVH, dtype=jnp.int32))
    attention = pieces.reshape(block_count, KVH, TOK_DEV, group_size * HD)
    attention = jnp.transpose(attention, (0, 2, 1, 3)).reshape(tok_count, HQ * HD)
    share_rows = HQ * HD // N_HEAD
    summed = jnp.zeros((tok_count, D), jnp.float32)
    for number in range(N_HEAD):
        partial_value = jnp.dot(attention[:, number * share_rows:(number + 1) * share_rows], w_out[number * share_rows:(number + 1) * share_rows], preferred_element_type=jnp.float32).astype(jnp.bfloat16)
        summed = summed + lax.optimization_barrier(partial_value).astype(jnp.float32)
    return summed.astype(jnp.bfloat16)
```

```python
from functools import partial
import math

import jax
import jax.numpy as jnp
from jax import lax
from jax.experimental import pallas as pl
from jax.experimental.pallas import tpu as pltpu
from jax.sharding import PartitionSpec as P

HD = 128
UNIT = 128
CHUNK_UNITS = 4
LOW = -1e30
VMEM_LIMIT = 40 * 1024 * 1024
HBM = pl.BlockSpec(memory_space=pl.ANY)
SMEM = pl.BlockSpec(memory_space=pltpu.SMEM)


def params():
    return pltpu.CompilerParams(vmem_limit_bytes=VMEM_LIMIT)


def run_copies(copies):
    for copy in copies:
        copy.start()
    for copy in copies:
        copy.wait()


def split_kernel(group, width, source_count, *refs):
    sources = refs[:source_count]
    pieces = refs[source_count:source_count + group]
    sem = refs[-1]
    member = lax.rem(lax.axis_index("ctx"), group)
    copies = []
    for step in range(group):
        start = pl.multiple_of((member ^ step) * width, width)
        for number, source in enumerate(sources):
            copies.append(
                pltpu.make_async_copy(
                    source.at[:, pl.ds(start, width)],
                    pieces[step].at[:, pl.ds(number * width, width)],
                    sem.at[step * source_count + number],
                )
            )
    run_copies(copies)


def split_columns(sources, group):
    rows, columns = sources[0].shape
    width = columns // group
    count = len(sources)
    piece = jax.ShapeDtypeStruct((rows, width * count), sources[0].dtype)
    return pl.pallas_call(
        partial(split_kernel, group, width, count),
        out_shape=[piece] * group,
        in_specs=[HBM] * count,
        out_specs=[HBM] * group,
        scratch_shapes=[pltpu.SemaphoreType.DMA((group * count,))],
    )(*sources)


def pack_kernel(group, *refs):
    pieces, packed, sem = refs[:group], refs[group], refs[group + 1]
    rows = pieces[0].shape[0]
    member = lax.rem(lax.axis_index("ctx"), group)
    copies = []
    for step in range(group):
        start = pl.multiple_of((member ^ step) * rows, rows)
        copies.append(
            pltpu.make_async_copy(pieces[step], packed.at[pl.ds(start, rows), :], sem.at[step])
        )
    run_copies(copies)


def pack_rows(pieces):
    group = len(pieces)
    rows, columns = pieces[0].shape
    return pl.pallas_call(
        partial(pack_kernel, group),
        out_shape=jax.ShapeDtypeStruct((rows * group, columns), pieces[0].dtype),
        in_specs=[HBM] * group,
        out_specs=HBM,
        scratch_shapes=[pltpu.SemaphoreType.DMA((group,))],
    )(*pieces)


def attention_kernel(group, planes, heads, docs, *refs):
    docs_ref = refs[0]
    queries = refs[1:1 + group]
    keys = refs[1 + group:1 + group + planes]
    outs = refs[1 + group + planes:1 + 2 * group + planes]
    q_buf, kv_buf, o_buf, top, total, in_sem, out_sem = refs[1 + 2 * group + planes:]
    tokens = queries[0].shape[0]
    units = tokens // UNIT
    plane_rows = keys[0].shape[0]
    plane_units = plane_rows // UNIT
    pad_units = CHUNK_UNITS - 1
    pad = pad_units * UNIT
    chunk = CHUNK_UNITS * UNIT
    rows = heads * UNIT
    rank = lax.axis_index("ctx")
    member = lax.rem(rank, group)
    first_unit = (rank - member) * units - (planes - 1) * plane_units

    copies = [
        pltpu.make_async_copy(keys[number], kv_buf.at[pl.ds(pad + number * plane_rows, plane_rows), :], in_sem.at[number])
        for number in range(planes)
    ] + [
        pltpu.make_async_copy(queries[step], q_buf.at[step], in_sem.at[planes + step])
        for step in range(group)
    ]
    for copy in copies:
        copy.start()
    kv_buf[pl.ds(0, pad), :] = jnp.zeros((pad, 2 * HD), jnp.bfloat16)
    for copy in copies:
        copy.wait()

    scale = math.log2(math.e) / math.sqrt(HD)
    column = lax.broadcasted_iota(jnp.int32, (rows, chunk), 1)
    row = lax.broadcasted_iota(jnp.int32, (rows, chunk), 0) & (UNIT - 1)
    ones = jnp.ones((chunk, HD), jnp.bfloat16)

    def one_unit(index, carry):
        step = index // units
        unit = index - step * units
        here = (rank ^ step) * units + unit
        doc_first = jnp.int32(0)
        end = jnp.int32(0)
        for doc in range(docs):
            size = docs_ref[doc]
            end = end + size
            doc_first = jnp.where(end <= here, end, doc_first)
        last = here - first_unit + pad_units
        low = jnp.maximum(doc_first - first_unit, 0) + pad_units
        count = (last - low + CHUNK_UNITS) // CHUNK_UNITS
        tok = pl.multiple_of(unit * UNIT, UNIT)
        query = jnp.concatenate(
            [q_buf[step, pl.ds(tok, UNIT), head * HD:(head + 1) * HD] for head in range(heads)], axis=0
        )
        top[...] = jnp.full(top.shape, LOW, jnp.float32)
        total[...] = jnp.zeros(total.shape, jnp.float32)

        def visit(number, masked):
            start_unit = last + 1 - (number + 1) * CHUNK_UNITS
            start = pl.multiple_of(start_unit * UNIT, UNIT)
            key = kv_buf[pl.ds(start, chunk), :HD]
            value = jnp.concatenate([kv_buf[pl.ds(start, chunk), HD:], ones], axis=1)
            scores = lax.dot_general(query, key, (((1,), (1,)), ((), ())), preferred_element_type=jnp.float32)
            if masked:
                allowed = (column >= (low - start_unit) * UNIT) & (column - row <= (last - start_unit) * UNIT)
                scores = jnp.where(allowed, scores, LOW)
            old = top[...]
            new = jnp.maximum(old, jnp.max(scores, axis=1, keepdims=True))
            weights = jnp.exp2((scores - new[:, :1]) * scale).astype(jnp.bfloat16)
            shrink = jnp.exp2((old - new) * scale)
            update = jnp.dot(weights, value, preferred_element_type=jnp.float32)
            total[:, :HD] = total[:, :HD] * shrink + update[:, :HD]
            total[:, HD:] = total[:, HD:] * shrink + update[:, HD:]
            top[...] = new

        def chunk_step(number, inner):
            edge = (number == 0) | (number == count - 1)

            @pl.when(edge)
            def _():
                visit(number, True)

            @pl.when(jnp.logical_not(edge))
            def _():
                visit(number, False)

            return inner

        lax.fori_loop(0, count, chunk_step, 0)
        result = (total[:, :HD] / total[:, HD:]).astype(jnp.bfloat16)
        for head in range(heads):
            o_buf[step, pl.ds(tok, UNIT), head * HD:(head + 1) * HD] = result[head * UNIT:(head + 1) * UNIT]
        return carry

    lax.fori_loop(0, group * units, one_unit, 0)
    run_copies([pltpu.make_async_copy(o_buf.at[step], outs[step], out_sem.at[step]) for step in range(group)])


def attend(doc_units, query_pieces, planes):
    group = len(query_pieces)
    tokens, width = query_pieces[0].shape
    heads = width // HD
    plane_rows = planes[0].shape[0]
    rows = heads * UNIT
    pad = (CHUNK_UNITS - 1) * UNIT
    scores = tokens * group * width // HD * plane_rows * len(planes)
    return pl.pallas_call(
        partial(attention_kernel, group, len(planes), heads, doc_units.shape[0]),
        out_shape=[jax.ShapeDtypeStruct((tokens, width), jnp.bfloat16)] * group,
        in_specs=[SMEM] + [HBM] * (group + len(planes)),
        out_specs=[HBM] * group,
        scratch_shapes=[
            pltpu.VMEM((group, tokens, width), jnp.bfloat16),
            pltpu.VMEM((pad + plane_rows * len(planes), 2 * HD), jnp.bfloat16),
            pltpu.VMEM((group, tokens, width), jnp.bfloat16),
            pltpu.VMEM((rows, HD), jnp.float32),
            pltpu.VMEM((rows, 2 * HD), jnp.float32),
            pltpu.SemaphoreType.DMA((group + len(planes),)),
            pltpu.SemaphoreType.DMA((group,)),
        ],
        compiler_params=params(),
        cost_estimate=pl.CostEstimate(
            flops=2 * HD * scores, transcendentals=scores // 2, bytes_accessed=4 * tokens * group * width
        ),
    )(doc_units, *query_pieces, *planes)


def project_kernel(group, *refs):
    pieces = refs[:group]
    w_ref, give_ref, keep_ref, a_buf, sem = refs[group:]
    width = pieces[0].shape[1]
    member = lax.rem(lax.axis_index("ctx"), group)

    @pl.when(pl.program_id(0) == 0)
    def _():
        copies = []
        for step in range(group):
            start = pl.multiple_of((member ^ step) * width, width)
            copies.append(
                pltpu.make_async_copy(pieces[step], a_buf.at[:, pl.ds(start, width)], sem.at[step])
            )
        run_copies(copies)

    product = jnp.dot(a_buf[...], w_ref[...], preferred_element_type=jnp.float32).astype(jnp.bfloat16)
    parts = lax.axis_size("head")
    block = product.shape[0] // parts
    me = lax.axis_index("head")
    if parts == 2:
        mine_first = me == 0
        keep_ref[0] = jnp.where(mine_first, product[:block], product[block:])
        give_ref[0] = jnp.where(mine_first, product[block:], product[:block])
    else:
        for part in range(parts):
            give_ref[part] = product[part * block:(part + 1) * block]


def project(pieces, w_out, first, columns, tile):
    group = len(pieces)
    rows, width = pieces[0].shape
    parts = lax.axis_size("head")
    depth = w_out.shape[0]
    block = rows // parts
    outs = 1 if parts == 2 else parts
    base = first // tile
    half = jax.ShapeDtypeStruct((outs, block, columns), jnp.bfloat16)
    spec = pl.BlockSpec((outs, block, tile), lambda step: (0, 0, step))
    return pl.pallas_call(
        partial(project_kernel, group),
        out_shape=[half, half],
        grid=(columns // tile,),
        in_specs=[HBM] * group + [pl.BlockSpec((depth, tile), lambda step: (0, base + step))],
        out_specs=[spec, spec],
        scratch_shapes=[pltpu.VMEM((rows, depth), jnp.bfloat16), pltpu.SemaphoreType.DMA((group,))],
        compiler_params=params(),
        cost_estimate=pl.CostEstimate(
            flops=2 * rows * depth * columns, transcendentals=0, bytes_accessed=2 * depth * columns
        ),
    )(*pieces, w_out)


def shards(queries, key_heads, value_heads, doc_units, w_out):
    count = lax.axis_size("ctx")
    group = key_heads.shape[1] // HD
    hops = min(16, count // 2) // group

    def exchange(pieces):
        return [pieces[0]] + [
            lax.ppermute(pieces[step], "ctx", [(rank, rank ^ step) for rank in range(count)])
            for step in range(1, group)
        ]

    plane = pack_rows(exchange(split_columns([key_heads, value_heads], group)))
    query_pieces = exchange(split_columns([queries], group))
    planes = [plane]
    for hop in range(hops):
        planes.insert(
            0, lax.ppermute(planes[0], "ctx", [(rank, rank + group) for rank in range(count - group)])
        )
    attention = exchange(attend(doc_units, query_pieces, planes))
    columns = w_out.shape[1]
    parts = lax.axis_size("head")
    if parts == 2:
        halves = 2
        sums = []
        for half in range(halves):
            size = columns // halves
            give, keep = project(attention, w_out, half * size, size, 512)
            got = lax.ppermute(give[0], "head", [(0, 1), (1, 0)])
            sums.append((keep[0].astype(jnp.float32) + got.astype(jnp.float32)).astype(jnp.bfloat16))
        return jnp.concatenate(sums, axis=1)
    product, unused = project(attention, w_out, 0, columns, 512)
    return lax.psum_scatter(
        product.reshape(-1, columns), "head", scatter_dimension=0, tiled=True
    )


def solution(mesh):
    in_specs = (P("ctx", "head"), P("ctx", "head"), P("ctx", "head"), P(), P("head", None))
    out_specs = P(("ctx", "head"), None)
    return jax.shard_map(shards, mesh=mesh, in_specs=in_specs, out_specs=out_specs, check_vma=False)
```

```python
from functools import partial
import math

import jax
import jax.numpy as jnp
from jax import lax
from jax.experimental import pallas as pl
from jax.experimental.pallas import tpu as pltpu
from jax.sharding import PartitionSpec as P

HD = 128
UNIT = 128
CHUNK_UNITS = 4
LOW = -1e30
LARGE = 2.0**90
VMEM_LIMIT = 40 * 1024 * 1024
HBM = pl.BlockSpec(memory_space=pl.ANY)
SMEM = pl.BlockSpec(memory_space=pltpu.SMEM)


def params():
    return pltpu.CompilerParams(vmem_limit_bytes=VMEM_LIMIT)


def run_copies(copies):
    for copy in copies:
        copy.start()
    for copy in copies:
        copy.wait()


def attention_kernel(group, planes, heads, docs, *refs):
    docs_ref = refs[0]
    queries = refs[1:1 + group]
    keys = refs[1 + group:1 + group + planes]
    outs = refs[1 + group + planes:1 + 2 * group + planes]
    q_buf, kv_buf, o_buf, top, total, in_sem, out_sem = refs[1 + 2 * group + planes:]
    tokens = queries[0].shape[0]
    units = tokens // UNIT
    plane_rows = keys[0].shape[0]
    plane_units = plane_rows // UNIT
    pad_units = CHUNK_UNITS - 1
    pad = pad_units * UNIT
    chunk = CHUNK_UNITS * UNIT
    rows = heads * UNIT
    rank = lax.axis_index("ctx")
    member = lax.rem(rank, group)
    first_unit = (rank - member) * units - (planes - 1) * plane_units

    copies = []
    for number in range(planes):
        for step in range(group):
            place = pl.multiple_of(pad + number * plane_rows + (member ^ step) * tokens, UNIT)
            copies.append(
                pltpu.make_async_copy(
                    keys[number].at[pl.ds(step * tokens, tokens), :],
                    kv_buf.at[pl.ds(place, tokens), :],
                    in_sem.at[number * group + step],
                )
            )
    for step in range(group):
        copies.append(
            pltpu.make_async_copy(queries[step], q_buf.at[step], in_sem.at[planes * group + step])
        )
    for copy in copies:
        copy.start()
    kv_buf[pl.ds(0, pad), :] = jnp.zeros((pad, 2 * HD), jnp.bfloat16)
    for copy in copies:
        copy.wait()

    scale = math.log2(math.e) / math.sqrt(HD)
    column = lax.broadcasted_iota(jnp.int32, (rows, chunk), 1)
    row = lax.broadcasted_iota(jnp.int32, (rows, chunk), 0) & (UNIT - 1)
    ones = jnp.ones((chunk, HD), jnp.bfloat16)
    square = jnp.ones((HD, HD), jnp.bfloat16)

    def one_unit(index, carry):
        step = index // units
        unit = index - step * units
        here = (rank ^ step) * units + unit
        doc_first = jnp.int32(0)
        end = jnp.int32(0)
        for doc in range(docs):
            size = docs_ref[doc]
            end = end + size
            doc_first = jnp.where(end <= here, end, doc_first)
        last = here - first_unit + pad_units
        low = jnp.maximum(doc_first - first_unit, 0) + pad_units
        count = (last - low + CHUNK_UNITS) // CHUNK_UNITS
        tok = pl.multiple_of(unit * UNIT, UNIT)
        query = jnp.concatenate(
            [q_buf[step, pl.ds(tok, UNIT), head * HD:(head + 1) * HD] for head in range(heads)], axis=0
        )

        def scores_of(number, masked):
            start_unit = last + 1 - (number + 1) * CHUNK_UNITS
            start = pl.multiple_of(start_unit * UNIT, UNIT)
            key = kv_buf[pl.ds(start, chunk), :HD]
            value = jnp.concatenate([kv_buf[pl.ds(start, chunk), HD:], ones], axis=1)
            scores = lax.dot_general(query, key, (((1,), (1,)), ((), ())), preferred_element_type=jnp.float32)
            if masked:
                allowed = (column >= (low - start_unit) * UNIT) & (column - row <= (last - start_unit) * UNIT)
                scores = jnp.where(allowed, scores, LOW)
            return scores, value

        own_key = kv_buf[pl.ds(pl.multiple_of(last * UNIT, UNIT), UNIT), :HD]
        own = query * jnp.concatenate([own_key] * heads, axis=0)
        shift = jnp.dot(own, square, preferred_element_type=jnp.float32) * scale
        top[...] = shift

        def visit(number, masked, first=False):
            scores, value = scores_of(number, masked)
            shifts = jnp.concatenate([top[...]] * CHUNK_UNITS, axis=1)
            weights = jnp.exp2(scores * scale - shifts).astype(jnp.bfloat16)
            update = jnp.dot(weights, value, preferred_element_type=jnp.float32)
            if first:
                total[...] = update
            else:
                total[...] += update

        visit(0, True, True)

        def inside(number, inner):
            visit(number, False)
            return inner

        pairs = jnp.maximum(count - 2, 0) // 2

        def twice(number, inner):
            visit(1 + 2 * number, False)
            visit(2 + 2 * number, False)
            return inner

        lax.fori_loop(0, pairs, twice, 0)
        lax.fori_loop(1 + 2 * pairs, count - 1, inside, 0)

        @pl.when(count > 1)
        def _():
            visit(count - 1, True)

        @pl.when(jnp.logical_not(jnp.max(total[:, HD:]) < LARGE))
        def _():
            top[...] = jnp.full(top.shape, LOW, jnp.float32)
            total[...] = jnp.zeros(total.shape, jnp.float32)

            def careful(number, inner):
                scores, value = scores_of(number, True)
                old = top[...]
                new = jnp.maximum(old, jnp.max(scores, axis=1, keepdims=True))
                weights = jnp.exp2((scores - new[:, :1]) * scale).astype(jnp.bfloat16)
                shrink = jnp.exp2((old - new) * scale)
                update = jnp.dot(weights, value, preferred_element_type=jnp.float32)
                total[...] = total[...] * jnp.concatenate([shrink] * 2, axis=1) + update
                top[...] = new
                return inner

            lax.fori_loop(0, count, careful, 0)

        result = (total[:, :HD] / total[:, HD:]).astype(jnp.bfloat16)
        for head in range(heads):
            o_buf[step, pl.ds(tok, UNIT), head * HD:(head + 1) * HD] = result[head * UNIT:(head + 1) * UNIT]
        return carry

    lax.fori_loop(0, group * units, one_unit, 0)
    run_copies([pltpu.make_async_copy(o_buf.at[step], outs[step], out_sem.at[step]) for step in range(group)])


def attend(doc_units, query_pieces, planes):
    group = len(query_pieces)
    tokens, width = query_pieces[0].shape
    heads = width // HD
    plane_rows = planes[0].shape[0]
    rows = heads * UNIT
    pad = (CHUNK_UNITS - 1) * UNIT
    scores = tokens * group * width // HD * plane_rows * len(planes)
    return pl.pallas_call(
        partial(attention_kernel, group, len(planes), heads, doc_units.shape[0]),
        out_shape=[jax.ShapeDtypeStruct((tokens, width), jnp.bfloat16)] * group,
        in_specs=[SMEM] + [HBM] * (group + len(planes)),
        out_specs=[HBM] * group,
        scratch_shapes=[
            pltpu.VMEM((group, tokens, width), jnp.bfloat16),
            pltpu.VMEM((pad + plane_rows * len(planes), 2 * HD), jnp.bfloat16),
            pltpu.VMEM((group, tokens, width), jnp.bfloat16),
            pltpu.VMEM((rows, HD), jnp.float32),
            pltpu.VMEM((rows, 2 * HD), jnp.float32),
            pltpu.SemaphoreType.DMA((group + group * len(planes),)),
            pltpu.SemaphoreType.DMA((group,)),
        ],
        compiler_params=params(),
        cost_estimate=pl.CostEstimate(
            flops=2 * HD * scores, transcendentals=scores // 2, bytes_accessed=4 * tokens * group * width
        ),
    )(doc_units, *query_pieces, *planes)


def project_kernel(group, first, tile, *refs):
    pieces = refs[:group]
    w_ref, give_ref, keep_ref, a_buf, sem = refs[group:]
    width = pieces[0].shape[1]
    member = lax.rem(lax.axis_index("ctx"), group)

    @pl.when(pl.program_id(0) == 0)
    def _():
        copies = []
        for step in range(group):
            start = pl.multiple_of((member ^ step) * width, width)
            copies.append(
                pltpu.make_async_copy(pieces[step], a_buf.at[:, pl.ds(start, width)], sem.at[step])
            )
        run_copies(copies)

    start = pl.multiple_of(first + pl.program_id(0) * tile, tile)
    product = jnp.dot(a_buf[...], w_ref[:, pl.ds(start, tile)], preferred_element_type=jnp.float32)
    product = product.astype(jnp.bfloat16)
    block = product.shape[0] // 2
    low_first = lax.axis_index("head") == 0
    keep_ref[...] = jnp.where(low_first, product[:block], product[block:])
    give_ref[...] = jnp.where(low_first, product[block:], product[:block])


def project(pieces, w_out, first, columns, tile):
    group = len(pieces)
    rows, width = pieces[0].shape
    depth = w_out.shape[0]
    half = jax.ShapeDtypeStruct((rows // 2, columns), jnp.bfloat16)
    spec = pl.BlockSpec((rows // 2, tile), lambda step: (0, step))
    return pl.pallas_call(
        partial(project_kernel, group, first, tile),
        out_shape=[half, half],
        grid=(columns // tile,),
        in_specs=[HBM] * group + [pl.BlockSpec(memory_space=pltpu.VMEM)],
        out_specs=[spec, spec],
        scratch_shapes=[pltpu.VMEM((rows, depth), jnp.bfloat16), pltpu.SemaphoreType.DMA((group,))],
        compiler_params=params(),
        cost_estimate=pl.CostEstimate(
            flops=2 * rows * depth * columns, transcendentals=0, bytes_accessed=4 * rows * columns
        ),
    )(*pieces, w_out)


def sum_kernel(*refs):
    out_ref = refs[-1]
    halves = (len(refs) - 1) // 2
    columns = refs[0].shape[1]
    for half in range(halves):
        summed = refs[half][...].astype(jnp.float32) + refs[halves + half][...].astype(jnp.float32)
        out_ref[:, half * columns:(half + 1) * columns] = summed.astype(jnp.bfloat16)


def shards(queries, key_heads, value_heads, doc_units, w_out):
    count = lax.axis_size("ctx")
    group = key_heads.shape[1] // HD
    hops = min(16, count // 2) // group
    tokens, depth = queries.shape
    width = depth // group
    rank = lax.axis_index("ctx")
    member = lax.rem(rank, group)

    def column_block(value, step, size):
        return lax.dynamic_slice(value, (0, (member ^ step) * size), (tokens, size))

    def exchange(pieces):
        return [pieces[0]] + [
            lax.ppermute(pieces[step], "ctx", [(source, source ^ step) for source in range(count)])
            for step in range(1, group)
        ]

    kv_pieces = exchange([
        jnp.concatenate([column_block(key_heads, step, HD), column_block(value_heads, step, HD)], axis=1)
        for step in range(group)
    ])
    query_pieces = exchange([column_block(queries, step, width) for step in range(group)])
    planes = [jnp.concatenate(kv_pieces, axis=0)]
    for hop in range(hops):
        planes.insert(
            0, lax.ppermute(planes[0], "ctx", [(source, source + group) for source in range(count - group)])
        )
    attention = exchange(attend(doc_units, query_pieces, planes))
    columns = w_out.shape[1]
    if lax.axis_size("head") == 2:
        w_here = pltpu.with_memory_space_constraint(w_out, pltpu.VMEM)
        size = columns // 2
        keeps, gots = [], []
        for half in range(2):
            give, keep = project(attention, w_here, half * size, size, 512)
            keeps.append(keep)
            gots.append(lax.ppermute(give, "head", [(0, 1), (1, 0)]))
        return pl.pallas_call(
            sum_kernel,
            out_shape=jax.ShapeDtypeStruct((tokens // 2, columns), jnp.bfloat16),
            compiler_params=params(),
        )(*keeps, *gots)
    product = sum(
        jnp.dot(
            attention[step],
            lax.dynamic_slice(w_out, ((member ^ step) * width, 0), (width, columns)),
            preferred_element_type=jnp.float32,
        )
        for step in range(group)
    )
    return lax.psum_scatter(product.astype(jnp.bfloat16), "head", scatter_dimension=0, tiled=True)


def solution(mesh):
    in_specs = (P("ctx", "head"), P("ctx", "head"), P("ctx", "head"), P(), P("head", None))
    out_specs = P(("ctx", "head"), None)
    return jax.shard_map(shards, mesh=mesh, in_specs=in_specs, out_specs=out_specs, check_vma=False)
```

```python
from functools import partial
import math

import jax
import jax.numpy as jnp
from jax import lax
from jax.experimental import pallas as pl
from jax.experimental.pallas import tpu as pltpu
from jax.sharding import PartitionSpec as P

HD = 128
UNIT = 128
CHUNK_UNITS = 4
LOW = -1e30
LARGE = 2.0**90
VMEM_LIMIT = 24 * 1024 * 1024
HBM = pl.BlockSpec(memory_space=pl.ANY)
SMEM = pl.BlockSpec(memory_space=pltpu.SMEM)


def params():
    return pltpu.CompilerParams(vmem_limit_bytes=VMEM_LIMIT)


def run_copies(copies):
    for copy in copies:
        copy.start()
    for copy in copies:
        copy.wait()


def attention_kernel(mode, steps, group, planes, heads, docs, *refs):
    refs = list(refs)

    def take(number):
        taken = refs[:number]
        del refs[:number]
        return taken

    pieces = len(steps)
    early, late = mode == "early", mode == "late"
    (docs_ref,) = take(1)
    queries = take(pieces)
    keys = take(planes)
    if early:
        (w_from,) = take(1)
    if late:
        (state,) = take(1)
        take(pieces)
    outs = take(pieces)
    if early:
        state, w_to = take(2)
    q_buf, kv_buf, o_buf, top, total, in_sem, out_sem = refs
    tokens = queries[0].shape[0]
    units = tokens // UNIT
    plane_rows = keys[0].shape[0]
    plane_units = plane_rows // UNIT
    pad_units = CHUNK_UNITS - 1
    pad = pad_units * UNIT
    chunk = CHUNK_UNITS * UNIT
    rows = heads * UNIT
    rank = lax.axis_index("ctx")
    member = lax.rem(rank, group)
    first_unit = (rank - member) * units - (planes - 1) * plane_units
    unseen = pad_units + max(planes - 2, 0) * plane_units
    scale = math.log2(math.e) / math.sqrt(HD)

    def place(index):
        piece = index // units
        unit = index - piece * units
        here = (rank ^ (steps[0] - piece)) * units + unit
        doc_first = jnp.int32(0)
        end = jnp.int32(0)
        for doc in range(docs):
            end = end + docs_ref[doc]
            doc_first = jnp.where(end <= here, end, doc_first)
        last = here - first_unit + pad_units
        start = doc_first - first_unit + pad_units
        return piece, pl.multiple_of(unit * UNIT, UNIT), last, start

    def load():
        copies = []
        for number in range(planes):
            for step in range(group):
                to = pl.multiple_of(pad + number * plane_rows + (member ^ step) * tokens, UNIT)
                copies.append(
                    pltpu.make_async_copy(
                        keys[number].at[pl.ds(step * tokens, tokens), :],
                        kv_buf.at[pl.ds(to, tokens), :],
                        in_sem.at[number * group + step],
                    )
                )
        for piece in range(pieces):
            copies.append(
                pltpu.make_async_copy(queries[piece], q_buf.at[piece], in_sem.at[planes * group + piece])
            )
        for copy in copies:
            copy.start()
        kv_buf[pl.ds(0, pad), :] = jnp.zeros((pad, 2 * HD), jnp.bfloat16)
        for copy in copies:
            copy.wait()

    def one_unit(index):
        column = lax.broadcasted_iota(jnp.int32, (rows, chunk), 1)
        row = lax.broadcasted_iota(jnp.int32, (rows, chunk), 0) & (UNIT - 1)
        ones = jnp.ones((chunk, HD), jnp.bfloat16)
        square = jnp.ones((HD, HD), jnp.bfloat16)
        piece, tok, last, start_unit = place(index)
        low = jnp.maximum(start_unit, pad_units)
        stop = jnp.int32(unseen) if late else last + 1
        count = (stop - low + CHUNK_UNITS - 1) // CHUNK_UNITS
        query = jnp.concatenate(
            [q_buf[piece, pl.ds(tok, UNIT), head * HD:(head + 1) * HD] for head in range(heads)], axis=0
        )

        def scores_of(end, number, masked):
            begin_unit = end - (number + 1) * CHUNK_UNITS
            begin = pl.multiple_of(begin_unit * UNIT, UNIT)
            key = kv_buf[pl.ds(begin, chunk), :HD]
            value = jnp.concatenate([kv_buf[pl.ds(begin, chunk), HD:], ones], axis=1)
            scores = lax.dot_general(query, key, (((1,), (1,)), ((), ())), preferred_element_type=jnp.float32)
            if masked:
                allowed = (column >= (low - begin_unit) * UNIT) & (column - row <= (last - begin_unit) * UNIT)
                scores = jnp.where(allowed, scores, LOW)
            return scores, value

        own_key = kv_buf[pl.ds(pl.multiple_of(last * UNIT, UNIT), UNIT), :HD]
        own = query * jnp.concatenate([own_key] * heads, axis=0)
        top[...] = jnp.dot(own, square, preferred_element_type=jnp.float32) * scale

        def visit(number, masked, first=False):
            scores, value = scores_of(stop, number, masked)
            shifts = jnp.concatenate([top[...]] * CHUNK_UNITS, axis=1)
            weights = jnp.exp2(scores * scale - shifts).astype(jnp.bfloat16)
            update = jnp.dot(weights, value, preferred_element_type=jnp.float32)
            if first:
                total[...] = update
            else:
                total[...] += update

        if late:
            copy = pltpu.make_async_copy(state.at[index], total, out_sem.at[0])
            copy.start()
            copy.wait()
        visit(0, True, not late)
        pairs = jnp.maximum(count - 2, 0) // 2

        def twice(number, inner):
            visit(1 + 2 * number, False)
            visit(2 + 2 * number, False)
            return inner

        def once(number, inner):
            visit(number, False)
            return inner

        lax.fori_loop(0, pairs, twice, 0)
        lax.fori_loop(1 + 2 * pairs, count - 1, once, 0)

        @pl.when(count > 1)
        def _():
            visit(count - 1, True)

        overflow = jnp.logical_not(jnp.max(total[:, HD:]) < LARGE)
        if early:
            unfinished = start_unit < pad_units
            overflow = overflow & jnp.logical_not(unfinished)

            @pl.when(unfinished)
            def _():
                copy = pltpu.make_async_copy(total, state.at[index], out_sem.at[0])
                copy.start()
                copy.wait()

        @pl.when(overflow)
        def _():
            top[...] = jnp.full(top.shape, LOW, jnp.float32)
            total[...] = jnp.zeros(total.shape, jnp.float32)

            def careful(number, inner):
                scores, value = scores_of(last + 1, number, True)
                old = top[...]
                new = jnp.maximum(old, jnp.max(scores, axis=1, keepdims=True))
                weights = jnp.exp2((scores - new[:, :1]) * scale).astype(jnp.bfloat16)
                shrink = jnp.exp2((old - new) * scale)
                update = jnp.dot(weights, value, preferred_element_type=jnp.float32)
                total[...] = total[...] * jnp.concatenate([shrink] * 2, axis=1) + update
                top[...] = new
                return inner

            lax.fori_loop(0, (last + CHUNK_UNITS - low) // CHUNK_UNITS, careful, 0)

        result = (total[:, :HD] / total[:, HD:]).astype(jnp.bfloat16)
        for head in range(heads):
            o_buf[piece, pl.ds(tok, UNIT), head * HD:(head + 1) * HD] = result[head * UNIT:(head + 1) * UNIT]
        return piece, tok

    if late:
        needed = jnp.bool_(False)
        for index in range(pieces * units):
            needed = needed | (place(jnp.int32(index))[3] < unseen)

        @pl.when(needed)
        def _():
            load()

            def maybe(index, carry):
                @pl.when(place(index)[3] < unseen)
                def _():
                    piece, tok = one_unit(index)
                    for number in range(pieces):

                        @pl.when(piece == number)
                        def _():
                            copy = pltpu.make_async_copy(
                                o_buf.at[number, pl.ds(tok, UNIT), :],
                                outs[number].at[pl.ds(tok, UNIT), :],
                                out_sem.at[0],
                            )
                            copy.start()
                            copy.wait()

                return carry

            lax.fori_loop(0, pieces * units, maybe, 0)
    else:
        if early:
            w_copy = pltpu.make_async_copy(w_from, w_to, out_sem.at[pieces])
            w_copy.start()
        load()

        def always(index, carry):
            one_unit(index)
            return carry

        lax.fori_loop(0, pieces * units, always, 0)
        run_copies([
            pltpu.make_async_copy(o_buf.at[piece], outs[piece], out_sem.at[piece]) for piece in range(pieces)
        ])
        if early:
            w_copy.wait()


def attend(mode, steps, doc_units, queries, planes, w_out=None, state=None, outs=None):
    pieces = len(steps)
    group = planes[0].shape[0] // queries[0].shape[0]
    tokens, width = queries[0].shape
    heads = width // HD
    plane_rows = planes[0].shape[0]
    rows = heads * UNIT
    pad = (CHUNK_UNITS - 1) * UNIT
    scores = tokens * pieces * heads * plane_rows * (1 if mode == "late" else len(planes)) // 2
    operands = [doc_units, *queries, *planes]
    out_shape = [jax.ShapeDtypeStruct((tokens, width), jnp.bfloat16)] * pieces
    out_specs = [HBM] * pieces
    aliases = {}
    moved = 4 * tokens * pieces * width
    if mode == "early":
        operands += [w_out]
        out_shape += [
            jax.ShapeDtypeStruct((pieces * tokens // UNIT, rows, 2 * HD), jnp.float32),
            pltpu.VMEM(w_out.shape, w_out.dtype),
        ]
        out_specs += [HBM, pl.BlockSpec(memory_space=pltpu.VMEM)]
        moved += 2 * w_out.size
    if mode == "late":
        aliases = {len(operands) + 1 + piece: piece for piece in range(pieces)}
        operands += [state, *outs]
    return pl.pallas_call(
        partial(attention_kernel, mode, steps, group, len(planes), heads, doc_units.shape[0]),
        out_shape=out_shape,
        in_specs=[SMEM] + [HBM] * (len(operands) - 1),
        out_specs=out_specs,
        scratch_shapes=[
            pltpu.VMEM((pieces, tokens, width), jnp.bfloat16),
            pltpu.VMEM((pad + plane_rows * len(planes), 2 * HD), jnp.bfloat16),
            pltpu.VMEM((pieces, tokens, width), jnp.bfloat16),
            pltpu.VMEM((rows, HD), jnp.float32),
            pltpu.VMEM((rows, 2 * HD), jnp.float32),
            pltpu.SemaphoreType.DMA((pieces + group * len(planes),)),
            pltpu.SemaphoreType.DMA((pieces + 1,)),
        ],
        input_output_aliases=aliases,
        compiler_params=params(),
        cost_estimate=pl.CostEstimate(flops=4 * HD * scores, transcendentals=scores, bytes_accessed=moved),
    )(*operands)


def project_kernel(group, first, tile, *refs):
    pieces = refs[:group]
    w_ref, give_ref, keep_ref, a_buf, sem = refs[group:]
    width = pieces[0].shape[1]
    member = lax.rem(lax.axis_index("ctx"), group)

    @pl.when(pl.program_id(0) == 0)
    def _():
        copies = []
        for step in range(group):
            start = pl.multiple_of((member ^ step) * width, width)
            copies.append(
                pltpu.make_async_copy(pieces[step], a_buf.at[:, pl.ds(start, width)], sem.at[step])
            )
        run_copies(copies)

    start = pl.multiple_of(first + pl.program_id(0) * tile, tile)
    product = jnp.dot(a_buf[...], w_ref[:, pl.ds(start, tile)], preferred_element_type=jnp.float32)
    product = product.astype(jnp.bfloat16)
    block = product.shape[0] // 2
    low_first = lax.axis_index("head") == 0
    keep_ref[...] = jnp.where(low_first, product[:block], product[block:])
    give_ref[...] = jnp.where(low_first, product[block:], product[:block])


def project(pieces, w_out, first, columns, tile):
    group = len(pieces)
    rows, width = pieces[0].shape
    depth = w_out.shape[0]
    half = jax.ShapeDtypeStruct((rows // 2, columns), jnp.bfloat16)
    spec = pl.BlockSpec((rows // 2, tile), lambda step: (0, step))
    return pl.pallas_call(
        partial(project_kernel, group, first, tile),
        out_shape=[half, half],
        grid=(columns // tile,),
        in_specs=[HBM] * group + [pl.BlockSpec(memory_space=pltpu.VMEM)],
        out_specs=[spec, spec],
        scratch_shapes=[pltpu.VMEM((rows, depth), jnp.bfloat16), pltpu.SemaphoreType.DMA((group,))],
        compiler_params=params(),
        cost_estimate=pl.CostEstimate(
            flops=2 * rows * depth * columns, transcendentals=0, bytes_accessed=4 * rows * columns
        ),
    )(*pieces, w_out)


def sum_kernel(*refs):
    out_ref = refs[-1]
    halves = (len(refs) - 1) // 2
    columns = refs[0].shape[1]
    for half in range(halves):
        summed = refs[half][...].astype(jnp.float32) + refs[halves + half][...].astype(jnp.float32)
        out_ref[:, half * columns:(half + 1) * columns] = summed.astype(jnp.bfloat16)


def shards(queries, key_heads, value_heads, doc_units, w_out):
    count = lax.axis_size("ctx")
    group = key_heads.shape[1] // HD
    hops = min(16, count // 2) // group
    tokens, depth = queries.shape
    width = depth // group
    rank = lax.axis_index("ctx")
    member = lax.rem(rank, group)

    def column_block(value, step, size):
        return lax.dynamic_slice(value, (0, (member ^ step) * size), (tokens, size))

    def swap(value, step):
        if step == 0:
            return value
        return lax.ppermute(value, "ctx", [(source, source ^ step) for source in range(count)])

    def next_plane(value):
        return lax.ppermute(value, "ctx", [(source, source + group) for source in range(count - group)])

    kv_pieces = [
        swap(
            jnp.concatenate([column_block(key_heads, step, HD), column_block(value_heads, step, HD)], axis=1), step
        )
        for step in range(group)
    ]
    planes = [jnp.concatenate(kv_pieces, axis=0)]
    queries, planes = lax.optimization_barrier((queries, planes))
    query_pieces = [swap(column_block(queries, step, width), step) for step in range(group)]
    planes = [next_plane(planes[0])] + planes
    planes, query_pieces = lax.optimization_barrier((planes, query_pieces))
    for hop in range(hops - 1):
        planes = [next_plane(planes[0])] + planes
    w_here = w_out
    attention = [None] * group
    far = tuple(range(group - 1, 1, -1))
    if far:
        far_queries = [query_pieces[step] for step in far]
        *partials, state, w_here = attend("early", far, doc_units, far_queries, planes[-2:], w_out=w_out)
        finals = attend("late", far, doc_units, far_queries, planes, state=state, outs=partials)
        for step, final in zip(far, finals):
            attention[step] = swap(final, step)
    for step in range(min(group, 2) - 1, -1, -1):
        (final,) = attend("full", (step,), doc_units, [query_pieces[step]], planes)
        attention[step] = swap(final, step)
    columns = w_out.shape[1]
    if lax.axis_size("head") == 2:
        w_here = pltpu.with_memory_space_constraint(w_here, pltpu.VMEM)
        size = columns // 2
        keeps, gots = [], []
        for half in range(2):
            give, keep = project(attention, w_here, half * size, size, 512)
            keeps.append(keep)
            gots.append(lax.ppermute(give, "head", [(0, 1), (1, 0)]))
        return pl.pallas_call(
            sum_kernel,
            out_shape=jax.ShapeDtypeStruct((tokens // 2, columns), jnp.bfloat16),
            compiler_params=params(),
        )(*keeps, *gots)
    product = sum(
        jnp.dot(
            attention[step],
            lax.dynamic_slice(w_out, ((member ^ step) * width, 0), (width, columns)),
            preferred_element_type=jnp.float32,
        )
        for step in range(group)
    )
    return lax.psum_scatter(product.astype(jnp.bfloat16), "head", scatter_dimension=0, tiled=True)


def solution(mesh):
    in_specs = (P("ctx", "head"), P("ctx", "head"), P("ctx", "head"), P(), P("head", None))
    out_specs = P(("ctx", "head"), None)
    return jax.shard_map(shards, mesh=mesh, in_specs=in_specs, out_specs=out_specs, check_vma=False)
```

```python
from functools import partial
import math

import jax
import jax.numpy as jnp
from jax import lax
from jax.experimental import pallas as pl
from jax.experimental.pallas import tpu as pltpu
from jax.sharding import PartitionSpec as P

HD = 128
UNIT = 128
CHUNK_UNITS = 4
LOW = -1e30
LARGE = 2.0**90
VMEM_LIMIT = 24 * 1024 * 1024
HBM = pl.BlockSpec(memory_space=pl.ANY)
SMEM = pl.BlockSpec(memory_space=pltpu.SMEM)
VMEM = pl.BlockSpec(memory_space=pltpu.VMEM)


def params():
    return pltpu.CompilerParams(vmem_limit_bytes=VMEM_LIMIT)


def run_copies(copies):
    for copy in copies:
        copy.start()
    for copy in copies:
        copy.wait()


def attention_kernel(mode, steps, group, planes, heads, docs, *refs):
    refs = list(refs)

    def take(number):
        taken = refs[:number]
        del refs[:number]
        return taken

    pieces = len(steps)
    early, late = mode == "early", mode == "late"
    (docs_ref,) = take(1)
    queries = take(pieces)
    keys = take(planes)
    if early:
        (w_from,) = take(1)
    if late:
        (state,) = take(1)
        take(pieces)
    outs = take(pieces)
    if early:
        state, w_to = take(2)
    q_buf, kv_buf, o_buf, shift, total, in_sem, out_sem = refs
    tokens = queries[0].shape[0]
    units = tokens // UNIT
    plane_rows = keys[0].shape[0]
    plane_units = plane_rows // UNIT
    pad_units = CHUNK_UNITS - 1
    pad = pad_units * UNIT
    chunk = CHUNK_UNITS * UNIT
    rank = lax.axis_index("ctx")
    member = lax.rem(rank, group)
    first_unit = (rank - member) * units - (planes - 1) * plane_units
    unseen = pad_units + max(planes - 2, 0) * plane_units
    scale = math.log2(math.e) / math.sqrt(HD)

    def place(piece):
        here = (rank ^ (steps[0] - piece)) * units
        starts = []
        for unit in range(units):
            doc_first = jnp.int32(0)
            end = jnp.int32(0)
            for doc in range(docs):
                end = end + docs_ref[doc]
                doc_first = jnp.where(end <= here + unit, end, doc_first)
            starts.append(doc_first - first_unit + pad_units)
        return here - first_unit + pad_units, starts

    def load():
        copies = []
        for number in range(planes):
            for step in range(group):
                to = pl.multiple_of(pad + number * plane_rows + (member ^ step) * tokens, UNIT)
                copies.append(
                    pltpu.make_async_copy(
                        keys[number].at[pl.ds(step * tokens, tokens), :],
                        kv_buf.at[pl.ds(to, tokens), :],
                        in_sem.at[number * group + step],
                    )
                )
        for piece in range(pieces):
            copies.append(
                pltpu.make_async_copy(queries[piece], q_buf.at[piece], in_sem.at[planes * group + piece])
            )
        for copy in copies:
            copy.start()
        kv_buf[pl.ds(0, pad), :] = jnp.zeros((pad, 2 * HD), jnp.bfloat16)
        for copy in copies:
            copy.wait()

    def one_piece(piece):
        ones = jnp.ones((chunk, HD), jnp.bfloat16)
        square = jnp.ones((HD, HD), jnp.bfloat16)
        first_row, starts = place(piece)
        lows = [jnp.maximum(start, pad_units) for start in starts]
        low, high = lows[0], lows[-1]
        stop = jnp.int32(unseen) if late else first_row + units
        count = (stop - low + CHUNK_UNITS - 1) // CHUNK_UNITS
        whole = jnp.maximum((stop - high) // CHUNK_UNITS, 0 if late else 1)
        query = jnp.concatenate([q_buf[piece, :, head * HD:(head + 1) * HD] for head in range(heads)], axis=0)

        def scores_of(end, number, masked):
            begin_unit = end - (number + 1) * CHUNK_UNITS
            begin = pl.multiple_of(begin_unit * UNIT, UNIT)
            key = kv_buf[pl.ds(begin, chunk), :HD]
            value = jnp.concatenate([kv_buf[pl.ds(begin, chunk), HD:], ones], axis=1)
            scores = lax.dot_general(query, key, (((1,), (1,)), ((), ())), preferred_element_type=jnp.float32)
            if masked:
                column = lax.broadcasted_iota(jnp.int32, (UNIT, chunk), 1)
                ahead = column - lax.broadcasted_iota(jnp.int32, (UNIT, chunk), 0)
                allowed = [
                    (column >= (lows[unit] - begin_unit) * UNIT) & (ahead <= (first_row + unit - begin_unit) * UNIT)
                    for unit in range(units)
                ]
                scores = jnp.concatenate([
                    jnp.where(allowed[number % units], scores[number * UNIT:(number + 1) * UNIT], LOW)
                    for number in range(heads * units)
                ], axis=0)
            return scores, value

        own_key = kv_buf[pl.ds(pl.multiple_of(first_row * UNIT, UNIT), tokens), :HD]
        own = query * jnp.concatenate([own_key] * heads, axis=0)
        shift[...] = jnp.dot(own, square, preferred_element_type=jnp.float32) * scale

        def visit(number, masked, fresh=False):
            scores, value = scores_of(stop, number, masked)
            shifts = jnp.concatenate([shift[...]] * CHUNK_UNITS, axis=1)
            weights = jnp.exp2(scores * scale - shifts).astype(jnp.bfloat16)
            update = jnp.dot(weights, value, preferred_element_type=jnp.float32)
            if fresh:
                total[...] = update
            else:
                total[...] += update

        def masked_visit(number, inner):
            visit(number, True)
            return inner

        def plain_visit(number, inner):
            visit(number, False)
            return inner

        if late:
            total[...] = state[piece]
        else:
            visit(0, True, True)
        lax.fori_loop(0 if late else 1, whole, plain_visit, 0)
        lax.fori_loop(whole, count, masked_visit, 0)

        overflow = jnp.logical_not(jnp.max(total[:, HD:]) < LARGE)
        if early:
            unfinished = starts[0] < pad_units
            overflow = overflow & jnp.logical_not(unfinished)

            @pl.when(unfinished)
            def _():
                state[piece] = total[...]

        @pl.when(overflow)
        def _():
            shift[...] = jnp.full(shift.shape, LOW, jnp.float32)
            total[...] = jnp.zeros(total.shape, jnp.float32)

            def careful(number, inner):
                scores, value = scores_of(first_row + units, number, True)
                old = shift[...]
                new = jnp.maximum(old, jnp.max(scores, axis=1, keepdims=True))
                weights = jnp.exp2((scores - new[:, :1]) * scale).astype(jnp.bfloat16)
                shrink = jnp.exp2((old - new) * scale)
                update = jnp.dot(weights, value, preferred_element_type=jnp.float32)
                total[...] = total[...] * jnp.concatenate([shrink] * 2, axis=1) + update
                shift[...] = new
                return inner

            lax.fori_loop(0, (first_row + units - low + CHUNK_UNITS - 1) // CHUNK_UNITS, careful, 0)

        result = (total[:, :HD] / total[:, HD:]).astype(jnp.bfloat16)
        for head in range(heads):
            o_buf[piece, :, head * HD:(head + 1) * HD] = result[head * tokens:(head + 1) * tokens]

    if late:
        needed = [place(jnp.int32(piece))[1][0] < unseen for piece in range(pieces)]

        @pl.when(sum(need.astype(jnp.int32) for need in needed) > 0)
        def _():
            load()
            for piece in range(pieces):

                @pl.when(needed[piece])
                def _():
                    one_piece(piece)
                    copy = pltpu.make_async_copy(o_buf.at[piece], outs[piece], out_sem.at[piece])
                    copy.start()
                    copy.wait()
    else:
        if early:
            w_copy = pltpu.make_async_copy(w_from, w_to, out_sem.at[pieces])
            w_copy.start()
        load()

        def always(piece, carry):
            one_piece(piece)
            return carry

        lax.fori_loop(0, pieces, always, 0)
        run_copies([
            pltpu.make_async_copy(o_buf.at[piece], outs[piece], out_sem.at[piece]) for piece in range(pieces)
        ])
        if early:
            w_copy.wait()


def attend(mode, steps, doc_units, queries, planes, w_out=None, state=None, outs=None):
    pieces = len(steps)
    group = planes[0].shape[0] // queries[0].shape[0]
    tokens, width = queries[0].shape
    heads = width // HD
    plane_rows = planes[0].shape[0]
    rows = heads * tokens
    pad = (CHUNK_UNITS - 1) * UNIT
    scores = tokens * pieces * heads * plane_rows * (1 if mode == "late" else len(planes)) // 2
    operands = [doc_units, *queries, *planes]
    in_specs = [SMEM] + [HBM] * (len(operands) - 1)
    out_shape = [jax.ShapeDtypeStruct((tokens, width), jnp.bfloat16)] * pieces
    out_specs = [HBM] * pieces
    aliases = {}
    moved = 4 * tokens * pieces * width
    if mode == "early":
        operands += [w_out]
        in_specs += [HBM]
        out_shape += [pltpu.VMEM((pieces, rows, 2 * HD), jnp.float32), pltpu.VMEM(w_out.shape, w_out.dtype)]
        out_specs += [VMEM, VMEM]
        moved += 2 * w_out.size
    if mode == "late":
        aliases = {len(operands) + 1 + piece: piece for piece in range(pieces)}
        operands += [pltpu.with_memory_space_constraint(state, pltpu.VMEM), *outs]
        in_specs += [VMEM] + [HBM] * pieces
    return pl.pallas_call(
        partial(attention_kernel, mode, steps, group, len(planes), heads, doc_units.shape[0]),
        out_shape=out_shape,
        in_specs=in_specs,
        out_specs=out_specs,
        scratch_shapes=[
            pltpu.VMEM((pieces, tokens, width), jnp.bfloat16),
            pltpu.VMEM((pad + plane_rows * len(planes), 2 * HD), jnp.bfloat16),
            pltpu.VMEM((pieces, tokens, width), jnp.bfloat16),
            pltpu.VMEM((rows, HD), jnp.float32),
            pltpu.VMEM((rows, 2 * HD), jnp.float32),
            pltpu.SemaphoreType.DMA((pieces + group * len(planes),)),
            pltpu.SemaphoreType.DMA((pieces + 1,)),
        ],
        input_output_aliases=aliases,
        compiler_params=params(),
        cost_estimate=pl.CostEstimate(flops=4 * HD * scores, transcendentals=scores, bytes_accessed=moved),
    )(*operands)


def project_kernel(group, first, tile, *refs):
    pieces = refs[:group]
    w_ref, give_ref, keep_ref, a_buf, sem = refs[group:]
    width = pieces[0].shape[1]
    member = lax.rem(lax.axis_index("ctx"), group)

    @pl.when(pl.program_id(0) == 0)
    def _():
        copies = []
        for step in range(group):
            start = pl.multiple_of((member ^ step) * width, width)
            copies.append(
                pltpu.make_async_copy(pieces[step], a_buf.at[:, pl.ds(start, width)], sem.at[step])
            )
        run_copies(copies)

    start = pl.multiple_of(first + pl.program_id(0) * tile, tile)
    product = jnp.dot(a_buf[...], w_ref[:, pl.ds(start, tile)], preferred_element_type=jnp.float32)
    product = product.astype(jnp.bfloat16)
    block = product.shape[0] // 2
    low_first = lax.axis_index("head") == 0
    keep_ref[...] = jnp.where(low_first, product[:block], product[block:])
    give_ref[...] = jnp.where(low_first, product[block:], product[:block])


def project(pieces, w_out, first, columns, tile):
    group = len(pieces)
    rows, width = pieces[0].shape
    depth = w_out.shape[0]
    half = jax.ShapeDtypeStruct((rows // 2, columns), jnp.bfloat16)
    spec = pl.BlockSpec((rows // 2, tile), lambda step: (0, step))
    return pl.pallas_call(
        partial(project_kernel, group, first, tile),
        out_shape=[half, half],
        grid=(columns // tile,),
        in_specs=[HBM] * group + [pl.BlockSpec(memory_space=pltpu.VMEM)],
        out_specs=[spec, spec],
        scratch_shapes=[pltpu.VMEM((rows, depth), jnp.bfloat16), pltpu.SemaphoreType.DMA((group,))],
        compiler_params=params(),
        cost_estimate=pl.CostEstimate(
            flops=2 * rows * depth * columns, transcendentals=0, bytes_accessed=4 * rows * columns
        ),
    )(*pieces, w_out)


def sum_kernel(*refs):
    out_ref = refs[-1]
    halves = (len(refs) - 1) // 2
    columns = refs[0].shape[1]
    for half in range(halves):
        summed = refs[half][...].astype(jnp.float32) + refs[halves + half][...].astype(jnp.float32)
        out_ref[:, half * columns:(half + 1) * columns] = summed.astype(jnp.bfloat16)


def shards(queries, key_heads, value_heads, doc_units, w_out):
    count = lax.axis_size("ctx")
    group = key_heads.shape[1] // HD
    hops = min(16, count // 2) // group
    tokens, depth = queries.shape
    width = depth // group
    rank = lax.axis_index("ctx")
    member = lax.rem(rank, group)

    def column_block(value, step, size):
        return lax.dynamic_slice(value, (0, (member ^ step) * size), (tokens, size))

    def swap(value, step):
        if step == 0:
            return value
        return lax.ppermute(value, "ctx", [(source, source ^ step) for source in range(count)])

    def next_plane(value):
        return lax.ppermute(value, "ctx", [(source, source + group) for source in range(count - group)])

    kv_pieces = [
        swap(
            jnp.concatenate([column_block(key_heads, step, HD), column_block(value_heads, step, HD)], axis=1), step
        )
        for step in range(group)
    ]
    planes = [jnp.concatenate(kv_pieces, axis=0)]
    queries, planes = lax.optimization_barrier((queries, planes))
    query_pieces = [swap(column_block(queries, step, width), step) for step in range(group)]
    planes = [next_plane(planes[0])] + planes
    planes, query_pieces = lax.optimization_barrier((planes, query_pieces))
    for hop in range(hops - 1):
        planes = [next_plane(planes[0])] + planes
    w_here = w_out
    attention = [None] * group
    far = tuple(range(group - 1, 1, -1))
    if far:
        far_queries = [query_pieces[step] for step in far]
        *partials, state, w_here = attend("early", far, doc_units, far_queries, planes[-2:], w_out=w_out)
        finals = attend("late", far, doc_units, far_queries, planes, state=state, outs=partials)
        for step, final in zip(far, finals):
            attention[step] = swap(final, step)
        query_pieces, finals = lax.optimization_barrier((query_pieces, finals))
    for step in range(min(group, 2) - 1, -1, -1):
        (final,) = attend("full", (step,), doc_units, [query_pieces[step]], planes)
        attention[step] = swap(final, step)
        query_pieces, final = lax.optimization_barrier((query_pieces, final))
    columns = w_out.shape[1]
    if lax.axis_size("head") == 2:
        w_here = pltpu.with_memory_space_constraint(w_here, pltpu.VMEM)
        size = columns // 2
        keeps, gots = [], []
        for half in range(2):
            give, keep = project(attention, w_here, half * size, size, 512)
            keeps.append(keep)
            gots.append(lax.ppermute(give, "head", [(0, 1), (1, 0)]))
        return pl.pallas_call(
            sum_kernel,
            out_shape=jax.ShapeDtypeStruct((tokens // 2, columns), jnp.bfloat16),
            compiler_params=params(),
        )(*keeps, *gots)
    product = sum(
        jnp.dot(
            attention[step],
            lax.dynamic_slice(w_out, ((member ^ step) * width, 0), (width, columns)),
            preferred_element_type=jnp.float32,
        )
        for step in range(group)
    )
    return lax.psum_scatter(product.astype(jnp.bfloat16), "head", scatter_dimension=0, tiled=True)


def solution(mesh):
    in_specs = (P("ctx", "head"), P("ctx", "head"), P("ctx", "head"), P(), P("head", None))
    out_specs = P(("ctx", "head"), None)
    return jax.shard_map(shards, mesh=mesh, in_specs=in_specs, out_specs=out_specs, check_vma=False)
```

```python
from functools import partial
import math

import jax
import jax.numpy as jnp
from jax import lax
from jax.experimental import pallas as pl
from jax.experimental.pallas import tpu as pltpu
from jax.sharding import PartitionSpec as P

HD = 128
UNIT = 128
CHUNK_UNITS = 4
LOW = -1e30
LARGE = 2.0**90
VMEM_LIMIT = 24 * 1024 * 1024
HBM = pl.BlockSpec(memory_space=pl.ANY)
SMEM = pl.BlockSpec(memory_space=pltpu.SMEM)
VMEM = pl.BlockSpec(memory_space=pltpu.VMEM)


def params():
    return pltpu.CompilerParams(vmem_limit_bytes=VMEM_LIMIT)


def run_copies(copies):
    for copy in copies:
        copy.start()
    for copy in copies:
        copy.wait()


def attention_kernel(mode, steps, group, planes, heads, docs, *refs):
    refs = list(refs)

    def take(number):
        taken = refs[:number]
        del refs[:number]
        return taken

    pieces = len(steps)
    early, late = mode == "early", mode == "late"
    (docs_ref,) = take(1)
    queries = take(pieces)
    keys = take(planes)
    values = take(planes)
    if early:
        (w_from,) = take(1)
    if late:
        (state,) = take(1)
        take(pieces)
    outs = take(pieces)
    if early:
        state, w_to = take(2)
    q_buf, k_buf, v_buf, o_buf, shift, total, in_sem, out_sem = refs
    tokens = queries[0].shape[0]
    units = tokens // UNIT
    plane_rows = keys[0].shape[0]
    plane_units = plane_rows // UNIT
    pad_units = CHUNK_UNITS - 1
    pad = pad_units * UNIT
    chunk = CHUNK_UNITS * UNIT
    rank = lax.axis_index("ctx")
    member = lax.rem(rank, group)
    first_unit = (rank - member) * units - (planes - 1) * plane_units
    unseen = pad_units + max(planes - 2, 0) * plane_units
    scale = math.log2(math.e) / math.sqrt(HD)

    def place(piece):
        here = (rank ^ (steps[0] - piece)) * units
        starts = []
        for unit in range(units):
            doc_first = jnp.int32(0)
            end = jnp.int32(0)
            for doc in range(docs):
                end = end + docs_ref[doc]
                doc_first = jnp.where(end <= here + unit, end, doc_first)
            starts.append(doc_first - first_unit + pad_units)
        return here - first_unit + pad_units, starts

    def load():
        copies = []
        for number in range(planes):
            for step in range(group):
                to = pl.multiple_of(pad + number * plane_rows + (member ^ step) * tokens, UNIT)
                for part, (source, target) in enumerate(((keys, k_buf), (values, v_buf))):
                    copies.append(
                        pltpu.make_async_copy(
                            source[number].at[pl.ds(step * tokens, tokens), :],
                            target.at[pl.ds(to, tokens), :],
                            in_sem.at[2 * (number * group + step) + part],
                        )
                    )
        for piece in range(pieces):
            copies.append(
                pltpu.make_async_copy(queries[piece], q_buf.at[piece], in_sem.at[2 * planes * group + piece])
            )
        for copy in copies:
            copy.start()
        k_buf[pl.ds(0, pad), :] = jnp.zeros((pad, HD), jnp.bfloat16)
        v_buf[pl.ds(0, pad), :] = jnp.zeros((pad, HD), jnp.bfloat16)
        for copy in copies:
            copy.wait()

    def one_piece(piece):
        ones = jnp.ones((chunk, HD), jnp.bfloat16)
        square = jnp.ones((HD, HD), jnp.bfloat16)
        first_row, starts = place(piece)
        lows = [jnp.maximum(start, pad_units) for start in starts]
        low, high = lows[0], lows[-1]
        stop = jnp.int32(unseen) if late else first_row + units
        count = (stop - low + CHUNK_UNITS - 1) // CHUNK_UNITS
        whole = jnp.maximum((stop - high) // CHUNK_UNITS, 0 if late else 1)
        query = jnp.concatenate([q_buf[piece, :, head * HD:(head + 1) * HD] for head in range(heads)], axis=0)

        def scores_of(end, number, masked):
            begin_unit = end - (number + 1) * CHUNK_UNITS
            begin = pl.multiple_of(begin_unit * UNIT, UNIT)
            key = k_buf[pl.ds(begin, chunk), :]
            value = jnp.concatenate([v_buf[pl.ds(begin, chunk), :], ones], axis=1)
            scores = lax.dot_general(query, key, (((1,), (1,)), ((), ())), preferred_element_type=jnp.float32)
            if masked:
                column = lax.broadcasted_iota(jnp.int32, (UNIT, chunk), 1)
                ahead = column - lax.broadcasted_iota(jnp.int32, (UNIT, chunk), 0)
                allowed = [
                    (column >= (lows[unit] - begin_unit) * UNIT) & (ahead <= (first_row + unit - begin_unit) * UNIT)
                    for unit in range(units)
                ]
                scores = jnp.concatenate([
                    jnp.where(allowed[number % units], scores[number * UNIT:(number + 1) * UNIT], LOW)
                    for number in range(heads * units)
                ], axis=0)
            return scores, value

        own_key = k_buf[pl.ds(pl.multiple_of(first_row * UNIT, UNIT), tokens), :]
        own = query * jnp.concatenate([own_key] * heads, axis=0)
        shift[...] = jnp.dot(own, square, preferred_element_type=jnp.float32) * scale

        def visit(number, masked, fresh=False):
            scores, value = scores_of(stop, number, masked)
            shifts = jnp.concatenate([shift[...]] * CHUNK_UNITS, axis=1)
            weights = jnp.exp2(scores * scale - shifts).astype(jnp.bfloat16)
            update = jnp.dot(weights, value, preferred_element_type=jnp.float32)
            if fresh:
                total[...] = update
            else:
                total[...] += update

        def masked_visit(number, inner):
            visit(number, True)
            return inner

        def plain_visit(number, inner):
            visit(number, False)
            return inner

        if late:
            total[...] = state[piece]
        else:
            visit(0, True, True)
        lax.fori_loop(0 if late else 1, whole, plain_visit, 0)
        lax.fori_loop(whole, count, masked_visit, 0)

        overflow = jnp.logical_not(jnp.max(total[:, HD:]) < LARGE)
        if early:
            unfinished = starts[0] < pad_units
            overflow = overflow & jnp.logical_not(unfinished)

            @pl.when(unfinished)
            def _():
                state[piece] = total[...]

        @pl.when(overflow)
        def _():
            shift[...] = jnp.full(shift.shape, LOW, jnp.float32)
            total[...] = jnp.zeros(total.shape, jnp.float32)

            def careful(number, inner):
                scores, value = scores_of(first_row + units, number, True)
                old = shift[...]
                new = jnp.maximum(old, jnp.max(scores, axis=1, keepdims=True))
                weights = jnp.exp2((scores - new[:, :1]) * scale).astype(jnp.bfloat16)
                shrink = jnp.exp2((old - new) * scale)
                update = jnp.dot(weights, value, preferred_element_type=jnp.float32)
                total[...] = total[...] * jnp.concatenate([shrink] * 2, axis=1) + update
                shift[...] = new
                return inner

            lax.fori_loop(0, (first_row + units - low + CHUNK_UNITS - 1) // CHUNK_UNITS, careful, 0)

        result = (total[:, :HD] / total[:, HD:]).astype(jnp.bfloat16)
        for head in range(heads):
            o_buf[piece, :, head * HD:(head + 1) * HD] = result[head * tokens:(head + 1) * tokens]

    if late:
        needed = [place(jnp.int32(piece))[1][0] < unseen for piece in range(pieces)]

        @pl.when(sum(need.astype(jnp.int32) for need in needed) > 0)
        def _():
            load()
            for piece in range(pieces):

                @pl.when(needed[piece])
                def _():
                    one_piece(piece)
                    copy = pltpu.make_async_copy(o_buf.at[piece], outs[piece], out_sem.at[piece])
                    copy.start()
                    copy.wait()
    else:
        if early:
            w_copy = pltpu.make_async_copy(w_from, w_to, out_sem.at[pieces])
            w_copy.start()
        load()

        def always(piece, carry):
            one_piece(piece)
            return carry

        lax.fori_loop(0, pieces, always, 0)
        run_copies([
            pltpu.make_async_copy(o_buf.at[piece], outs[piece], out_sem.at[piece]) for piece in range(pieces)
        ])
        if early:
            w_copy.wait()


def attend(mode, steps, doc_units, queries, keys, values, w_out=None, state=None, outs=None):
    pieces = len(steps)
    planes = len(keys)
    group = keys[0].shape[0] // queries[0].shape[0]
    tokens, width = queries[0].shape
    heads = width // HD
    plane_rows = keys[0].shape[0]
    rows = heads * tokens
    pad = (CHUNK_UNITS - 1) * UNIT
    scores = tokens * pieces * heads * plane_rows * (1 if mode == "late" else planes) // 2
    operands = [doc_units, *queries, *keys, *values]
    in_specs = [SMEM] + [HBM] * (len(operands) - 1)
    out_shape = [jax.ShapeDtypeStruct((tokens, width), jnp.bfloat16)] * pieces
    out_specs = [HBM] * pieces
    aliases = {}
    moved = 4 * tokens * pieces * width
    if mode == "early":
        operands += [w_out]
        in_specs += [HBM]
        out_shape += [pltpu.VMEM((pieces, rows, 2 * HD), jnp.float32), pltpu.VMEM(w_out.shape, w_out.dtype)]
        out_specs += [VMEM, VMEM]
        moved += 2 * w_out.size
    if mode == "late":
        aliases = {len(operands) + 1 + piece: piece for piece in range(pieces)}
        operands += [pltpu.with_memory_space_constraint(state, pltpu.VMEM), *outs]
        in_specs += [VMEM] + [HBM] * pieces
    return pl.pallas_call(
        partial(attention_kernel, mode, steps, group, planes, heads, doc_units.shape[0]),
        out_shape=out_shape,
        in_specs=in_specs,
        out_specs=out_specs,
        scratch_shapes=[
            pltpu.VMEM((pieces, tokens, width), jnp.bfloat16),
            pltpu.VMEM((pad + plane_rows * planes, HD), jnp.bfloat16),
            pltpu.VMEM((pad + plane_rows * planes, HD), jnp.bfloat16),
            pltpu.VMEM((pieces, tokens, width), jnp.bfloat16),
            pltpu.VMEM((rows, HD), jnp.float32),
            pltpu.VMEM((rows, 2 * HD), jnp.float32),
            pltpu.SemaphoreType.DMA((pieces + 2 * group * planes,)),
            pltpu.SemaphoreType.DMA((pieces + 1,)),
        ],
        input_output_aliases=aliases,
        compiler_params=params(),
        cost_estimate=pl.CostEstimate(flops=4 * HD * scores, transcendentals=scores, bytes_accessed=moved),
    )(*operands)


def project_kernel(group, first, tile, *refs):
    pieces = refs[:group]
    w_ref, give_ref, keep_ref, a_buf, sem = refs[group:]
    width = pieces[0].shape[1]
    member = lax.rem(lax.axis_index("ctx"), group)

    @pl.when(pl.program_id(0) == 0)
    def _():
        copies = []
        for step in range(group):
            start = pl.multiple_of((member ^ step) * width, width)
            copies.append(
                pltpu.make_async_copy(pieces[step], a_buf.at[:, pl.ds(start, width)], sem.at[step])
            )
        run_copies(copies)

    start = pl.multiple_of(first + pl.program_id(0) * tile, tile)
    product = jnp.dot(a_buf[...], w_ref[:, pl.ds(start, tile)], preferred_element_type=jnp.float32)
    product = product.astype(jnp.bfloat16)
    block = product.shape[0] // 2
    low_first = lax.axis_index("head") == 0
    keep_ref[...] = jnp.where(low_first, product[:block], product[block:])
    give_ref[...] = jnp.where(low_first, product[block:], product[:block])


def project(pieces, w_out, first, columns, tile):
    group = len(pieces)
    rows, width = pieces[0].shape
    depth = w_out.shape[0]
    half = jax.ShapeDtypeStruct((rows // 2, columns), jnp.bfloat16)
    spec = pl.BlockSpec((rows // 2, tile), lambda step: (0, step))
    return pl.pallas_call(
        partial(project_kernel, group, first, tile),
        out_shape=[half, half],
        grid=(columns // tile,),
        in_specs=[HBM] * group + [pl.BlockSpec(memory_space=pltpu.VMEM)],
        out_specs=[spec, spec],
        scratch_shapes=[pltpu.VMEM((rows, depth), jnp.bfloat16), pltpu.SemaphoreType.DMA((group,))],
        compiler_params=params(),
        cost_estimate=pl.CostEstimate(
            flops=2 * rows * depth * columns, transcendentals=0, bytes_accessed=4 * rows * columns
        ),
    )(*pieces, w_out)


def sum_kernel(*refs):
    out_ref = refs[-1]
    halves = (len(refs) - 1) // 2
    columns = refs[0].shape[1]
    for half in range(halves):
        summed = refs[half][...].astype(jnp.float32) + refs[halves + half][...].astype(jnp.float32)
        out_ref[:, half * columns:(half + 1) * columns] = summed.astype(jnp.bfloat16)


def shards(queries, key_heads, value_heads, doc_units, w_out):
    count = lax.axis_size("ctx")
    group = key_heads.shape[1] // HD
    hops = min(16, count // 2) // group
    tokens, depth = queries.shape
    width = depth // group
    rank = lax.axis_index("ctx")
    member = lax.rem(rank, group)

    def column_block(value, step, size):
        return lax.dynamic_slice(value, (0, (member ^ step) * size), (tokens, size))

    def swap(value, step):
        if step == 0:
            return value
        return lax.ppermute(value, "ctx", [(source, source ^ step) for source in range(count)])

    def next_plane(value):
        return lax.ppermute(value, "ctx", [(source, source + group) for source in range(count - group)])

    def own_plane(value):
        return jnp.concatenate([swap(column_block(value, step, HD), step) for step in range(group)], axis=0)

    keys, values = [own_plane(key_heads)], [own_plane(value_heads)]
    queries = lax.optimization_barrier((queries, keys, values))[0]
    query_pieces = [swap(column_block(queries, step, width), step) for step in range(group)]
    keys = [next_plane(keys[0])] + keys
    values = [next_plane(values[0])] + values
    if group > 1:
        keys, query_pieces[:-1] = lax.optimization_barrier((keys, query_pieces[:-1]))
        values, query_pieces[-1:] = lax.optimization_barrier((values, query_pieces[-1:]))
    for hop in range(hops - 1):
        keys = [next_plane(keys[0])] + keys
        values = [next_plane(values[0])] + values
    w_here = w_out
    attention = [None] * group
    far = tuple(range(group - 1, 0, -1))
    if far:
        far_queries = [query_pieces[step] for step in far]
        *partials, state, w_here = attend("early", far, doc_units, far_queries, keys[-2:], values[-2:], w_out=w_out)
        finals = attend("late", far, doc_units, far_queries, keys, values, state=state, outs=partials)
        for step, final in zip(far, finals):
            attention[step] = swap(final, step)
        query_pieces, finals = lax.optimization_barrier((query_pieces, finals))
    (attention[0],) = attend("full", (0,), doc_units, query_pieces[:1], keys, values)
    columns = w_out.shape[1]
    if lax.axis_size("head") == 2:
        w_here = pltpu.with_memory_space_constraint(w_here, pltpu.VMEM)
        size = columns // 2
        keeps, gots = [], []
        for half in range(2):
            give, keep = project(attention, w_here, half * size, size, 512)
            keeps.append(keep)
            gots.append(lax.ppermute(give, "head", [(0, 1), (1, 0)]))
        return pl.pallas_call(
            sum_kernel,
            out_shape=jax.ShapeDtypeStruct((tokens // 2, columns), jnp.bfloat16),
            compiler_params=params(),
        )(*keeps, *gots)
    product = sum(
        jnp.dot(
            attention[step],
            lax.dynamic_slice(w_out, ((member ^ step) * width, 0), (width, columns)),
            preferred_element_type=jnp.float32,
        )
        for step in range(group)
    )
    return lax.psum_scatter(product.astype(jnp.bfloat16), "head", scatter_dimension=0, tiled=True)


def solution(mesh):
    in_specs = (P("ctx", "head"), P("ctx", "head"), P("ctx", "head"), P(), P("head", None))
    out_specs = P(("ctx", "head"), None)
    return jax.shard_map(shards, mesh=mesh, in_specs=in_specs, out_specs=out_specs, check_vma=False)
```

```python
from functools import partial
import math

import jax
import jax.numpy as jnp
from jax import lax
from jax.experimental import pallas as pl
from jax.experimental.pallas import tpu as pltpu
from jax.sharding import PartitionSpec as P

HD = 128
UNIT = 128
CHUNK_UNITS = 4
LOW = -1e30
LARGE = 2.0**90
VMEM_LIMIT = 24 * 1024 * 1024
HBM = pl.BlockSpec(memory_space=pl.ANY)
SMEM = pl.BlockSpec(memory_space=pltpu.SMEM)
VMEM = pl.BlockSpec(memory_space=pltpu.VMEM)


def params():
    return pltpu.CompilerParams(vmem_limit_bytes=VMEM_LIMIT)


def run_copies(copies):
    for copy in copies:
        copy.start()
    for copy in copies:
        copy.wait()


def pack_kernel(group, *refs):
    packed = refs[group]
    rows = refs[0].shape[0]
    member = lax.rem(lax.axis_index("ctx"), group)
    for step in range(group):
        packed[pl.ds(pl.multiple_of((member ^ step) * rows, rows), rows), :] = refs[step][...]


def pack_rows(pieces):
    group = len(pieces)
    rows, columns = pieces[0].shape
    return pl.pallas_call(
        partial(pack_kernel, group),
        out_shape=jax.ShapeDtypeStruct((rows * group, columns), pieces[0].dtype),
        compiler_params=params(),
    )(*pieces)


def attention_kernel(mode, steps, group, regions, heads, docs, *refs):
    refs = list(refs)

    def take(number):
        taken = refs[:number]
        del refs[:number]
        return taken

    pieces = len(steps)
    early, late = mode == "early", mode == "late"
    (docs_ref,) = take(1)
    queries = take(pieces)
    keys = take(regions)
    values = take(regions)
    if early:
        (w_from,) = take(1)
    if late:
        (state,) = take(1)
        take(pieces)
    outs = take(pieces)
    if early:
        state, w_to = take(2)
    q_buf, o_buf, shift, total, in_sem, out_sem = refs
    tokens = queries[0].shape[0]
    units = tokens // UNIT
    sizes = [key.shape[0] // UNIT for key in keys]
    bases = [sum(sizes[:region]) for region in range(regions)]
    chunk_units = CHUNK_UNITS if sizes[0] % CHUNK_UNITS == 0 else units
    chunk = chunk_units * UNIT
    rank = lax.axis_index("ctx")
    member = lax.rem(rank, group)
    first_unit = (rank - member + group) * units - sum(sizes)
    unseen = 0 if early else bases[1] if late else None
    visited = keys[:1] if late else keys
    scale = math.log2(math.e) / math.sqrt(HD)

    def place(piece):
        here = (rank ^ (steps[0] - piece)) * units
        starts = []
        for unit in range(units):
            doc_first = jnp.int32(0)
            end = jnp.int32(0)
            for doc in range(docs):
                end = end + docs_ref[doc]
                doc_first = jnp.where(end <= here + unit, end, doc_first)
            starts.append(doc_first - first_unit)
        return here - first_unit, starts

    def load():
        run_copies([
            pltpu.make_async_copy(queries[piece], q_buf.at[piece], in_sem.at[piece]) for piece in range(pieces)
        ])

    def one_piece(piece):
        ones = jnp.ones((chunk, HD), jnp.bfloat16)
        square = jnp.ones((HD, HD), jnp.bfloat16)
        first_row, starts = place(piece)
        lows = [jnp.maximum(start, 0) for start in starts]
        low, high, stop = lows[0], lows[-1], first_row + units
        query = jnp.concatenate([q_buf[piece, :, head * HD:(head + 1) * HD] for head in range(heads)], axis=0)

        def scores_of(region, number, masked, query):
            begin_unit = bases[region] + number * chunk_units
            begin = pl.multiple_of(number * chunk, chunk)
            key = keys[region][pl.ds(begin, chunk), :]
            value = jnp.concatenate([values[region][pl.ds(begin, chunk), :], ones], axis=1)
            scores = lax.dot_general(query, key, (((1,), (1,)), ((), ())), preferred_element_type=jnp.float32)
            if masked:
                column = lax.broadcasted_iota(jnp.int32, (UNIT, chunk), 1)
                ahead = column - lax.broadcasted_iota(jnp.int32, (UNIT, chunk), 0)
                allowed = [
                    (column >= (lows[unit] - begin_unit) * UNIT) & (ahead <= (first_row + unit - begin_unit) * UNIT)
                    for unit in range(units)
                ]
                scores = jnp.concatenate([
                    jnp.where(allowed[part % units], scores[part * UNIT:(part + 1) * UNIT], LOW)
                    for part in range(query.shape[0] // UNIT)
                ], axis=0)
            return scores, value

        own_start = pl.multiple_of((first_row - bases[-1]) * UNIT, UNIT)
        own = query * jnp.concatenate([keys[-1][pl.ds(own_start, tokens), :]] * heads, axis=0)
        shift[...] = jnp.dot(own, square, preferred_element_type=jnp.float32) * scale
        if late:
            total[...] = state[piece]
        else:
            total[...] = jnp.zeros(total.shape, jnp.float32)

        def visit(region, number, masked):
            scores, value = scores_of(region, number, masked, query)
            shifts = jnp.concatenate([shift[...]] * chunk_units, axis=1)
            weights = jnp.exp2(scores * scale - shifts).astype(jnp.bfloat16)
            total[...] += jnp.dot(weights, value, preferred_element_type=jnp.float32)

        def span(region):
            count = sizes[region] // chunk_units
            first = jnp.clip((low - bases[region]) // chunk_units, 0, count)
            last = jnp.clip((stop - bases[region] + chunk_units - 1) // chunk_units, 0, count)
            return first, jnp.maximum(first, last)

        for region in range(len(visited)):
            first, last = span(region)
            inner = jnp.clip((high - bases[region] + chunk_units - 1) // chunk_units, first, last)
            outer = jnp.clip((first_row - bases[region]) // chunk_units, inner, last)

            def masked_visit(number, carry, region=region, first=first, inner=inner, outer=outer):
                at = first + number
                visit(region, jnp.where(at < inner, at, at - inner + outer), True)
                return carry

            def plain_visit(number, carry, region=region):
                visit(region, number, False)
                return carry

            lax.fori_loop(0, inner - first + last - outer, masked_visit, 0)
            lax.fori_loop(inner, outer, plain_visit, 0)

        overflow = jnp.logical_not(jnp.max(total[:, HD:]) < LARGE)
        if early:
            unfinished = starts[0] < unseen
            overflow = overflow & jnp.logical_not(unfinished)

            @pl.when(unfinished)
            def _():
                state[piece] = total[...]

        @pl.when(overflow)
        def _():
            shift[...] = jnp.full(shift.shape, LOW, jnp.float32)
            total[...] = jnp.zeros(total.shape, jnp.float32)

            for region in reversed(range(regions)):
                first, last = span(region)

                def careful(number, carry, region=region, first=first):
                    head = lax.rem(number, heads)
                    some = pl.ds(pl.multiple_of(head * tokens, tokens), tokens)
                    query = q_buf[piece, :, pl.ds(pl.multiple_of(head * HD, HD), HD)]
                    scores, value = scores_of(region, first + number // heads, True, query)
                    old = shift[some, :]
                    new = jnp.maximum(old, jnp.max(scores, axis=1, keepdims=True))
                    weights = jnp.exp2((scores - new[:, :1]) * scale).astype(jnp.bfloat16)
                    shrink = jnp.exp2((old - new) * scale)
                    update = jnp.dot(weights, value, preferred_element_type=jnp.float32)
                    total[some, :] = total[some, :] * jnp.concatenate([shrink] * 2, axis=1) + update
                    shift[some, :] = new
                    return carry

                lax.fori_loop(0, (last - first) * heads, careful, 0)

        result = (total[:, :HD] / total[:, HD:]).astype(jnp.bfloat16)
        for head in range(heads):
            o_buf[piece, :, head * HD:(head + 1) * HD] = result[head * tokens:(head + 1) * tokens]

    if late:
        def needs(piece):
            return place(piece)[1][0] < unseen

        @pl.when(sum(needs(jnp.int32(piece)).astype(jnp.int32) for piece in range(pieces)) > 0)
        def _():
            load()

            def maybe(piece, carry):
                @pl.when(needs(piece))
                def _():
                    one_piece(piece)

                return carry

            lax.fori_loop(0, pieces, maybe, 0)
            for piece in range(pieces):

                @pl.when(needs(jnp.int32(piece)))
                def _():
                    run_copies([pltpu.make_async_copy(o_buf.at[piece], outs[piece], out_sem.at[piece])])
    else:
        if early:
            w_copy = pltpu.make_async_copy(w_from, w_to, out_sem.at[pieces])
            w_copy.start()
        load()

        def always(piece, carry):
            one_piece(piece)
            return carry

        lax.fori_loop(0, pieces, always, 0)
        run_copies([
            pltpu.make_async_copy(o_buf.at[piece], outs[piece], out_sem.at[piece]) for piece in range(pieces)
        ])
        if early:
            w_copy.wait()


def attend(mode, steps, group, doc_units, queries, keys, values, w_out=None, state=None, outs=None):
    pieces = len(steps)
    regions = len(keys)
    tokens, width = queries[0].shape
    heads = width // HD
    rows = heads * tokens
    seen = sum(key.shape[0] for key in (keys[:1] if mode == "late" else keys))
    scores = rows * pieces * seen // 2
    operands = [doc_units, *queries, *keys, *values]
    in_specs = [SMEM] + [HBM] * pieces + [VMEM] * (2 * regions)
    out_shape = [jax.ShapeDtypeStruct((tokens, width), jnp.bfloat16)] * pieces
    out_specs = [HBM] * pieces
    aliases = {}
    moved = 4 * tokens * pieces * width
    if mode == "early":
        operands += [w_out]
        in_specs += [HBM]
        out_shape += [pltpu.VMEM((pieces, rows, 2 * HD), jnp.float32), pltpu.VMEM(w_out.shape, w_out.dtype)]
        out_specs += [VMEM, VMEM]
        moved += 2 * w_out.size
    if mode == "late":
        aliases = {len(operands) + 1 + piece: piece for piece in range(pieces)}
        operands += [pltpu.with_memory_space_constraint(state, pltpu.VMEM), *outs]
        in_specs += [VMEM] + [HBM] * pieces
    return pl.pallas_call(
        partial(attention_kernel, mode, steps, group, regions, heads, doc_units.shape[0]),
        out_shape=out_shape,
        in_specs=in_specs,
        out_specs=out_specs,
        scratch_shapes=[
            pltpu.VMEM((pieces, tokens, width), jnp.bfloat16),
            pltpu.VMEM((pieces, tokens, width), jnp.bfloat16),
            pltpu.VMEM((rows, HD), jnp.float32),
            pltpu.VMEM((rows, 2 * HD), jnp.float32),
            pltpu.SemaphoreType.DMA((pieces,)),
            pltpu.SemaphoreType.DMA((pieces + 1,)),
        ],
        input_output_aliases=aliases,
        compiler_params=params(),
        cost_estimate=pl.CostEstimate(flops=4 * HD * scores, transcendentals=scores, bytes_accessed=moved),
    )(*operands)


def project_kernel(group, first, tile, *refs):
    pieces = refs[:group]
    w_ref, give_ref, keep_ref, a_buf, sem = refs[group:]
    width = pieces[0].shape[1]
    member = lax.rem(lax.axis_index("ctx"), group)

    @pl.when(pl.program_id(0) == 0)
    def _():
        copies = []
        for step in range(group):
            start = pl.multiple_of((member ^ step) * width, width)
            copies.append(
                pltpu.make_async_copy(pieces[step], a_buf.at[:, pl.ds(start, width)], sem.at[step])
            )
        run_copies(copies)

    start = pl.multiple_of(first + pl.program_id(0) * tile, tile)
    product = jnp.dot(a_buf[...], w_ref[:, pl.ds(start, tile)], preferred_element_type=jnp.float32)
    product = product.astype(jnp.bfloat16)
    block = product.shape[0] // 2
    low_first = lax.axis_index("head") == 0
    keep_ref[...] = jnp.where(low_first, product[:block], product[block:])
    give_ref[...] = jnp.where(low_first, product[block:], product[:block])


def project(pieces, w_out, first, columns, tile):
    group = len(pieces)
    rows, width = pieces[0].shape
    depth = w_out.shape[0]
    half = jax.ShapeDtypeStruct((rows // 2, columns), jnp.bfloat16)
    spec = pl.BlockSpec((rows // 2, tile), lambda step: (0, step))
    return pl.pallas_call(
        partial(project_kernel, group, first, tile),
        out_shape=[half, half],
        grid=(columns // tile,),
        in_specs=[HBM] * group + [pl.BlockSpec(memory_space=pltpu.VMEM)],
        out_specs=[spec, spec],
        scratch_shapes=[pltpu.VMEM((rows, depth), jnp.bfloat16), pltpu.SemaphoreType.DMA((group,))],
        compiler_params=params(),
        cost_estimate=pl.CostEstimate(
            flops=2 * rows * depth * columns, transcendentals=0, bytes_accessed=4 * rows * columns
        ),
    )(*pieces, w_out)


def sum_kernel(*refs):
    out_ref = refs[-1]
    halves = (len(refs) - 1) // 2
    columns = refs[0].shape[1]
    for half in range(halves):
        summed = refs[half][...].astype(jnp.float32) + refs[halves + half][...].astype(jnp.float32)
        out_ref[:, half * columns:(half + 1) * columns] = summed.astype(jnp.bfloat16)


def shards(queries, key_heads, value_heads, doc_units, w_out):
    count = lax.axis_size("ctx")
    group = key_heads.shape[1] // HD
    hops = min(16, count // 2) // group
    tokens, depth = queries.shape
    width = depth // group
    rank = lax.axis_index("ctx")
    member = lax.rem(rank, group)

    def column_block(value, step, size):
        return lax.dynamic_slice(value, (0, (member ^ step) * size), (tokens, size))

    def swap(value, step):
        if step == 0:
            return value
        return lax.ppermute(value, "ctx", [(source, source ^ step) for source in range(count)])

    def next_plane(value):
        return lax.ppermute(value, "ctx", [(source, source + group) for source in range(count - group)])

    def own_plane(value):
        pieces = [swap(column_block(value, step, HD), step) for step in range(group)]
        return pack_rows(pieces) if group > 1 else pieces[0]

    keys, values = [own_plane(key_heads)], [own_plane(value_heads)]
    queries = lax.optimization_barrier((queries, keys, values))[0]
    query_pieces = [swap(column_block(queries, step, width), step) for step in range(group)]
    keys = [next_plane(keys[0])] + keys
    values = [next_plane(values[0])] + values
    if group > 1:
        keys, values, query_pieces[-1] = lax.optimization_barrier((keys, values, query_pieces[-1]))
    for hop in range(hops - 1):
        keys = [next_plane(keys[0])] + keys
        values = [next_plane(values[0])] + values
    if group == 1:
        keys, values = [jnp.concatenate(keys, axis=0)], [jnp.concatenate(values, axis=0)]

    def place_in_vmem(arrays):
        return [pltpu.with_memory_space_constraint(array, pltpu.VMEM) for array in arrays]

    keys, values = place_in_vmem(keys), place_in_vmem(values)
    w_here = w_out
    attention = [None] * group
    far = tuple(range(group - 1, 0, -1))
    if far:
        far_queries = [query_pieces[step] for step in far]
        *partials, state, w_here = attend("early", far, group, doc_units, far_queries, keys[-2:], values[-2:], w_out=w_out)
        finals = attend("late", far, group, doc_units, far_queries, keys, values, state=state, outs=partials)
        for step, final in zip(far, finals):
            attention[step] = swap(final, step)
        query_pieces, finals = lax.optimization_barrier((query_pieces, finals))
    (attention[0],) = attend("full", (0,), group, doc_units, query_pieces[:1], keys, values)
    columns = w_out.shape[1]
    if lax.axis_size("head") == 2:
        w_here = pltpu.with_memory_space_constraint(w_here, pltpu.VMEM)
        size = columns // 2
        keeps, gots = [], []
        for half in range(2):
            give, keep = project(attention, w_here, half * size, size, 512)
            keeps.append(keep)
            gots.append(lax.ppermute(give, "head", [(0, 1), (1, 0)]))
        return pl.pallas_call(
            sum_kernel,
            out_shape=jax.ShapeDtypeStruct((tokens // 2, columns), jnp.bfloat16),
            compiler_params=params(),
        )(*keeps, *gots)
    product = sum(
        jnp.dot(
            attention[step],
            lax.dynamic_slice(w_out, ((member ^ step) * width, 0), (width, columns)),
            preferred_element_type=jnp.float32,
        )
        for step in range(group)
    )
    return lax.psum_scatter(product.astype(jnp.bfloat16), "head", scatter_dimension=0, tiled=True)


def solution(mesh):
    in_specs = (P("ctx", "head"), P("ctx", "head"), P("ctx", "head"), P(), P("head", None))
    out_specs = P(("ctx", "head"), None)
    return jax.shard_map(shards, mesh=mesh, in_specs=in_specs, out_specs=out_specs, check_vma=False)
```

```python
from functools import partial
import math

import jax
import jax.numpy as jnp
from jax import lax
from jax.experimental import pallas as pl
from jax.experimental.pallas import tpu as pltpu
from jax.sharding import PartitionSpec as P

HD = 128
UNIT = 128
CHUNK_UNITS = 6
LOW = -1e30
LARGE = 2.0**90
VMEM_LIMIT = 24 * 1024 * 1024
HBM = pl.BlockSpec(memory_space=pl.ANY)
SMEM = pl.BlockSpec(memory_space=pltpu.SMEM)
VMEM = pl.BlockSpec(memory_space=pltpu.VMEM)


def params(limit=VMEM_LIMIT):
    return pltpu.CompilerParams(vmem_limit_bytes=limit)


def run_copies(copies):
    for copy in copies:
        copy.start()
    for copy in copies:
        copy.wait()


def pack_kernel(group, *refs):
    packed = refs[group]
    rows = refs[0].shape[0]
    member = lax.rem(lax.axis_index("ctx"), group)
    for step in range(group):
        packed[pl.ds(pl.multiple_of((member ^ step) * rows, rows), rows), :] = refs[step][...]


def pack_rows(pieces):
    group = len(pieces)
    rows, columns = pieces[0].shape
    return pl.pallas_call(
        partial(pack_kernel, group),
        out_shape=jax.ShapeDtypeStruct((rows * group, columns), pieces[0].dtype),
        compiler_params=params(),
    )(*pieces)


def attention_kernel(mode, steps, group, regions, heads, docs, *refs):
    refs = list(refs)

    def take(number):
        taken = refs[:number]
        del refs[:number]
        return taken

    pieces = len(steps)
    early, late = mode == "early", mode == "late"
    (docs_ref,) = take(1)
    queries = take(pieces)
    keys = take(regions)
    values = take(regions)
    if early:
        (w_from,) = take(1)
    if late:
        (state,) = take(1)
        take(pieces)
    outs = take(pieces)
    if early:
        state, w_to = take(2)
    q_buf, o_buf, shift, total, in_sem, out_sem = refs
    tokens = queries[0].shape[0]
    units = tokens // UNIT
    sizes = [key.shape[0] // UNIT for key in keys]
    bases = [sum(sizes[:region]) for region in range(regions)]
    chunk_units = CHUNK_UNITS if sizes[0] % CHUNK_UNITS == 0 else units
    chunk = chunk_units * UNIT
    rank = lax.axis_index("ctx")
    member = lax.rem(rank, group)
    first_unit = (rank - member + group) * units - sum(sizes)
    unseen = 0 if early else bases[1] if late else None
    visited = keys[:1] if late else keys
    scale = math.log2(math.e) / math.sqrt(HD)

    def place(piece):
        here = (rank ^ (steps[0] - piece)) * units
        starts = []
        for unit in range(units):
            doc_first = jnp.int32(0)
            end = jnp.int32(0)
            for doc in range(docs):
                end = end + docs_ref[doc]
                doc_first = jnp.where(end <= here + unit, end, doc_first)
            starts.append(doc_first - first_unit)
        return here - first_unit, starts

    def load():
        run_copies([
            pltpu.make_async_copy(queries[piece], q_buf.at[piece], in_sem.at[piece]) for piece in range(pieces)
        ])

    def one_piece(piece):
        ones = jnp.ones((chunk, HD), jnp.bfloat16)
        square = jnp.ones((HD, HD), jnp.bfloat16)
        first_row, starts = place(piece)
        lows = [jnp.maximum(start, 0) for start in starts]
        low, high, stop = lows[0], lows[-1], first_row + units
        query = jnp.concatenate([q_buf[piece, :, head * HD:(head + 1) * HD] for head in range(heads)], axis=0)

        def scores_of(region, number, masked, query):
            begin_unit = bases[region] + number * chunk_units
            begin = pl.multiple_of(number * chunk, chunk)
            key = keys[region][pl.ds(begin, chunk), :]
            value = jnp.concatenate([values[region][pl.ds(begin, chunk), :], ones], axis=1)
            scores = lax.dot_general(query, key, (((1,), (1,)), ((), ())), preferred_element_type=jnp.float32)
            if masked:
                column = lax.broadcasted_iota(jnp.int32, (UNIT, chunk), 1)
                ahead = column - lax.broadcasted_iota(jnp.int32, (UNIT, chunk), 0)
                allowed = [
                    (column >= (lows[unit] - begin_unit) * UNIT) & (ahead <= (first_row + unit - begin_unit) * UNIT)
                    for unit in range(units)
                ]
                scores = jnp.concatenate([
                    jnp.where(allowed[part % units], scores[part * UNIT:(part + 1) * UNIT], LOW)
                    for part in range(query.shape[0] // UNIT)
                ], axis=0)
            return scores, value

        own_start = pl.multiple_of((first_row - bases[-1]) * UNIT, UNIT)
        own = query * jnp.concatenate([keys[-1][pl.ds(own_start, tokens), :]] * heads, axis=0)
        shift[...] = jnp.dot(own, square, preferred_element_type=jnp.float32) * scale
        if late:
            total[...] = state[piece]
        else:
            total[...] = jnp.zeros(total.shape, jnp.float32)

        def visit(region, number, masked):
            scores, value = scores_of(region, number, masked, query)
            shifts = jnp.concatenate([shift[...]] * chunk_units, axis=1)
            weights = jnp.exp2(scores * scale - shifts).astype(jnp.bfloat16)
            total[...] += jnp.dot(weights, value, preferred_element_type=jnp.float32)

        def span(region):
            count = sizes[region] // chunk_units
            first = jnp.clip((low - bases[region]) // chunk_units, 0, count)
            last = jnp.clip((stop - bases[region] + chunk_units - 1) // chunk_units, 0, count)
            return first, jnp.maximum(first, last)

        for region in range(len(visited)):
            first, last = span(region)
            inner = jnp.clip((high - bases[region] + chunk_units - 1) // chunk_units, first, last)
            outer = jnp.clip((first_row - bases[region]) // chunk_units, inner, last)

            def masked_visit(number, carry, region=region, first=first, inner=inner, outer=outer):
                at = first + number
                visit(region, jnp.where(at < inner, at, at - inner + outer), True)
                return carry

            def plain_visit(number, carry, region=region):
                visit(region, number, False)
                return carry

            lax.fori_loop(0, inner - first + last - outer, masked_visit, 0)
            lax.fori_loop(inner, outer, plain_visit, 0)

        overflow = jnp.logical_not(jnp.max(total[:, HD:]) < LARGE)
        if early:
            unfinished = starts[0] < unseen
            overflow = overflow & jnp.logical_not(unfinished)

            @pl.when(unfinished)
            def _():
                state[piece] = total[...]

        @pl.when(overflow)
        def _():
            shift[...] = jnp.full(shift.shape, LOW, jnp.float32)
            total[...] = jnp.zeros(total.shape, jnp.float32)

            for region in reversed(range(regions)):
                first, last = span(region)

                def careful(number, carry, region=region, first=first):
                    head = lax.rem(number, heads)
                    some = pl.ds(pl.multiple_of(head * tokens, tokens), tokens)
                    query = q_buf[piece, :, pl.ds(pl.multiple_of(head * HD, HD), HD)]
                    scores, value = scores_of(region, first + number // heads, True, query)
                    old = shift[some, :]
                    new = jnp.maximum(old, jnp.max(scores, axis=1, keepdims=True))
                    weights = jnp.exp2((scores - new[:, :1]) * scale).astype(jnp.bfloat16)
                    shrink = jnp.exp2((old - new) * scale)
                    update = jnp.dot(weights, value, preferred_element_type=jnp.float32)
                    total[some, :] = total[some, :] * jnp.concatenate([shrink] * 2, axis=1) + update
                    shift[some, :] = new
                    return carry

                lax.fori_loop(0, (last - first) * heads, careful, 0)

        result = (total[:, :HD] / total[:, HD:]).astype(jnp.bfloat16)
        for head in range(heads):
            o_buf[piece, :, head * HD:(head + 1) * HD] = result[head * tokens:(head + 1) * tokens]

    if late:
        def needs(piece):
            return place(piece)[1][0] < unseen

        @pl.when(sum(needs(jnp.int32(piece)).astype(jnp.int32) for piece in range(pieces)) > 0)
        def _():
            load()

            def maybe(piece, carry):
                @pl.when(needs(piece))
                def _():
                    one_piece(piece)

                return carry

            lax.fori_loop(0, pieces, maybe, 0)
            for piece in range(pieces):

                @pl.when(needs(jnp.int32(piece)))
                def _():
                    run_copies([pltpu.make_async_copy(o_buf.at[piece], outs[piece], out_sem.at[piece])])
    else:
        if early:
            w_copy = pltpu.make_async_copy(w_from, w_to, out_sem.at[pieces])
            w_copy.start()
        load()

        def always(piece, carry):
            one_piece(piece)
            return carry

        lax.fori_loop(0, pieces, always, 0)
        run_copies([
            pltpu.make_async_copy(o_buf.at[piece], outs[piece], out_sem.at[piece]) for piece in range(pieces)
        ])
        if early:
            w_copy.wait()


def attend(mode, steps, group, doc_units, queries, keys, values, w_out=None, state=None, outs=None):
    pieces = len(steps)
    regions = len(keys)
    tokens, width = queries[0].shape
    heads = width // HD
    rows = heads * tokens
    seen = sum(key.shape[0] for key in (keys[:1] if mode == "late" else keys))
    scores = rows * pieces * seen // 2
    operands = [doc_units, *queries, *keys, *values]
    in_specs = [SMEM] + [HBM] * pieces + [VMEM] * (2 * regions)
    out_shape = [jax.ShapeDtypeStruct((tokens, width), jnp.bfloat16)] * pieces
    out_specs = [HBM] * pieces
    aliases = {}
    moved = 4 * tokens * pieces * width
    if mode == "early":
        operands += [w_out]
        in_specs += [HBM]
        out_shape += [pltpu.VMEM((pieces, rows, 2 * HD), jnp.float32), pltpu.VMEM(w_out.shape, w_out.dtype)]
        out_specs += [VMEM, VMEM]
        moved += 2 * w_out.size
    if mode == "late":
        aliases = {len(operands) + 1 + piece: piece for piece in range(pieces)}
        operands += [pltpu.with_memory_space_constraint(state, pltpu.VMEM), *outs]
        in_specs += [VMEM] + [HBM] * pieces
    return pl.pallas_call(
        partial(attention_kernel, mode, steps, group, regions, heads, doc_units.shape[0]),
        out_shape=out_shape,
        in_specs=in_specs,
        out_specs=out_specs,
        scratch_shapes=[
            pltpu.VMEM((pieces, tokens, width), jnp.bfloat16),
            pltpu.VMEM((pieces, tokens, width), jnp.bfloat16),
            pltpu.VMEM((rows, HD), jnp.float32),
            pltpu.VMEM((rows, 2 * HD), jnp.float32),
            pltpu.SemaphoreType.DMA((pieces,)),
            pltpu.SemaphoreType.DMA((pieces + 1,)),
        ],
        input_output_aliases=aliases,
        compiler_params=params(),
        cost_estimate=pl.CostEstimate(flops=4 * HD * scores, transcendentals=scores, bytes_accessed=moved),
    )(*operands)


def project_kernel(group, steps, first, tile, resumed, last, *refs):
    refs = list(refs)
    pieces = [refs.pop(0) for step in steps]
    w_ref = refs.pop(0)
    sums = [refs.pop(0)[:, pl.ds(pl.multiple_of(first + pl.program_id(0) * tile, tile), tile)]] if resumed else []
    width = pieces[0].shape[1]
    member = lax.rem(lax.axis_index("ctx"), group)
    start = pl.multiple_of(first + pl.program_id(0) * tile, tile)
    weights = jnp.concatenate(
        [w_ref[pl.ds(pl.multiple_of((member ^ step) * width, width), width), pl.ds(start, tile)] for step in steps],
        axis=0,
    )
    rows = jnp.concatenate([piece[...] for piece in pieces], axis=1)
    product = sum(sums, jnp.dot(rows, weights, preferred_element_type=jnp.float32))
    if not last:
        refs[0][:, pl.ds(start, tile)] = product
        return
    give_ref, keep_ref = refs
    product = product.astype(jnp.bfloat16)
    block = product.shape[0] // 2
    low_first = lax.axis_index("head") == 0
    keep_ref[...] = jnp.where(low_first, product[:block], product[block:])
    give_ref[...] = jnp.where(low_first, product[block:], product[:block])


def project(group, steps, pieces, w_out, first, columns, tile, sums=None, last=True):
    rows, width = pieces[0].shape
    depth = width * len(steps)
    if last:
        spec = pl.BlockSpec((rows // 2, tile), lambda step: (0, step))
        out_specs = [spec, spec]
        out_shape = [jax.ShapeDtypeStruct((rows // 2, columns), jnp.bfloat16)] * 2
    else:
        out_specs = VMEM
        out_shape = pltpu.VMEM((rows, columns), jnp.float32)
    operands = [*pieces, w_out]
    if sums is not None:
        operands.append(sums)
    return pl.pallas_call(
        partial(project_kernel, group, steps, first, tile, sums is not None, last),
        out_shape=out_shape,
        grid=(columns // tile,),
        in_specs=[VMEM] * len(operands),
        out_specs=out_specs,
        compiler_params=params(10 * 1024 * 1024),
        cost_estimate=pl.CostEstimate(
            flops=2 * rows * depth * columns, transcendentals=0, bytes_accessed=4 * rows * columns
        ),
    )(*operands)


def sum_kernel(*refs):
    out_ref = refs[-1]
    halves = (len(refs) - 1) // 2
    columns = refs[0].shape[1]
    for half in range(halves):
        summed = refs[half][...].astype(jnp.float32) + refs[halves + half][...].astype(jnp.float32)
        out_ref[:, half * columns:(half + 1) * columns] = summed.astype(jnp.bfloat16)


def shards(queries, key_heads, value_heads, doc_units, w_out):
    count = lax.axis_size("ctx")
    group = key_heads.shape[1] // HD
    hops = min(16, count // 2) // group
    tokens, depth = queries.shape
    width = depth // group
    rank = lax.axis_index("ctx")
    member = lax.rem(rank, group)

    def column_block(value, step, size):
        return lax.dynamic_slice(value, (0, (member ^ step) * size), (tokens, size))

    def swap(value, step):
        if step == 0:
            return value
        return lax.ppermute(value, "ctx", [(source, source ^ step) for source in range(count)])

    def next_plane(value):
        return lax.ppermute(value, "ctx", [(source, source + group) for source in range(count - group)])

    def own_plane(value):
        pieces = [swap(column_block(value, step, HD), step) for step in range(group)]
        return pack_rows(pieces) if group > 1 else pieces[0]

    keys, values = [own_plane(key_heads)], [own_plane(value_heads)]
    queries = lax.optimization_barrier((queries, keys, values))[0]
    query_pieces = [swap(column_block(queries, step, width), step) for step in range(group)]
    keys = [next_plane(keys[0])] + keys
    values = [next_plane(values[0])] + values
    if group > 1:
        keys, values, query_pieces[-1] = lax.optimization_barrier((keys, values, query_pieces[-1]))
    for hop in range(hops - 1):
        keys = [next_plane(keys[0])] + keys
        values = [next_plane(values[0])] + values
    if group == 1:
        keys, values = [jnp.concatenate(keys, axis=0)], [jnp.concatenate(values, axis=0)]

    def place_in_vmem(arrays):
        return [pltpu.with_memory_space_constraint(array, pltpu.VMEM) for array in arrays]

    keys, values = place_in_vmem(keys), place_in_vmem(values)
    w_here = w_out
    attention = [None] * group
    far = tuple(range(group - 1, 0, -1))
    if far:
        far_queries = [query_pieces[step] for step in far]
        *partials, state, w_here = attend("early", far, group, doc_units, far_queries, keys[-2:], values[-2:], w_out=w_out)
        finals = attend("late", far, group, doc_units, far_queries, keys, values, state=state, outs=partials)
        for step, final in zip(far, finals):
            attention[step] = swap(final, step)
        query_pieces, finals = lax.optimization_barrier((query_pieces, finals))
    (attention[0],) = attend("full", (0,), group, doc_units, query_pieces[:1], keys, values)
    columns = w_out.shape[1]
    if lax.axis_size("head") == 2:
        w_here = pltpu.with_memory_space_constraint(w_here, pltpu.VMEM)
        soon = (0,) + far[:1]
        rest = tuple(step for step in range(group) if step not in soon)
        sums = None
        if rest:
            sums = project(
                group, soon, [attention[step] for step in soon], w_here, 0, columns, 512, last=False
            )
            sums = pltpu.with_memory_space_constraint(sums, pltpu.VMEM)
        else:
            rest = soon
        size = columns // 2
        keeps, gots = [], []
        for half in range(2):
            give, keep = project(
                group, rest, [attention[step] for step in rest], w_here, half * size, size, 512, sums=sums
            )
            keeps.append(keep)
            gots.append(lax.ppermute(give, "head", [(0, 1), (1, 0)]))
        return pl.pallas_call(
            sum_kernel,
            out_shape=jax.ShapeDtypeStruct((tokens // 2, columns), jnp.bfloat16),
            compiler_params=params(),
        )(*keeps, *gots)
    product = sum(
        jnp.dot(
            attention[step],
            lax.dynamic_slice(w_out, ((member ^ step) * width, 0), (width, columns)),
            preferred_element_type=jnp.float32,
        )
        for step in range(group)
    )
    return lax.psum_scatter(product.astype(jnp.bfloat16), "head", scatter_dimension=0, tiled=True)


def solution(mesh):
    in_specs = (P("ctx", "head"), P("ctx", "head"), P("ctx", "head"), P(), P("head", None))
    out_specs = P(("ctx", "head"), None)
    return jax.shard_map(shards, mesh=mesh, in_specs=in_specs, out_specs=out_specs, check_vma=False)
```

```python
from functools import partial
import math

import jax
import jax.numpy as jnp
from jax import lax
from jax.experimental import pallas as pl
from jax.experimental.pallas import tpu as pltpu
from jax.sharding import PartitionSpec as P

HD = 128
UNIT = 128
CHUNK_UNITS = 6
LOW = -1e30
LARGE = 2.0**90
VMEM_LIMIT = 24 * 1024 * 1024
HBM = pl.BlockSpec(memory_space=pl.ANY)
SMEM = pl.BlockSpec(memory_space=pltpu.SMEM)
VMEM = pl.BlockSpec(memory_space=pltpu.VMEM)


def params(limit=VMEM_LIMIT):
    return pltpu.CompilerParams(vmem_limit_bytes=limit)


def run_copies(copies):
    for copy in copies:
        copy.start()
    for copy in copies:
        copy.wait()


def pack_kernel(group, *refs):
    packed = refs[group]
    rows = refs[0].shape[0]
    member = lax.rem(lax.axis_index("ctx"), group)
    for step in range(group):
        packed[pl.ds(pl.multiple_of((member ^ step) * rows, rows), rows), :] = refs[step][...]


def pack_rows(pieces):
    group = len(pieces)
    rows, columns = pieces[0].shape
    return pl.pallas_call(
        partial(pack_kernel, group),
        out_shape=jax.ShapeDtypeStruct((rows * group, columns), pieces[0].dtype),
        compiler_params=params(),
    )(*pieces)


def attention_kernel(mode, steps, group, regions, heads, docs, *refs):
    refs = list(refs)

    def take(number):
        taken = refs[:number]
        del refs[:number]
        return taken

    pieces = len(steps)
    early, late = mode == "early", mode == "late"
    (docs_ref,) = take(1)
    queries = take(pieces)
    keys = take(regions)
    values = take(regions)
    if early:
        (w_from,) = take(1)
    if late:
        (state,) = take(1)
        take(pieces)
    outs = take(pieces)
    if early:
        state, w_to = take(2)
    q_rows, o_buf, shift, total, out_sem = refs
    tokens = queries[0].shape[0]
    units = tokens // UNIT
    sizes = [key.shape[0] // UNIT for key in keys]
    bases = [sum(sizes[:region]) for region in range(regions)]
    chunk_units = CHUNK_UNITS if sizes[0] % CHUNK_UNITS == 0 else units
    chunk = chunk_units * UNIT
    rank = lax.axis_index("ctx")
    member = lax.rem(rank, group)
    first_unit = (rank - member + group) * units - sum(sizes)
    unseen = 0 if early else bases[1] if late else None
    visited = keys[:1] if late else keys
    scale = math.log2(math.e) / math.sqrt(HD)

    def place(piece):
        here = (rank ^ (steps[0] - piece)) * units
        starts = []
        for unit in range(units):
            doc_first = jnp.int32(0)
            end = jnp.int32(0)
            for doc in range(docs):
                end = end + docs_ref[doc]
                doc_first = jnp.where(end <= here + unit, end, doc_first)
            starts.append(doc_first - first_unit)
        return here - first_unit, starts

    def one_piece(piece):
        ones = jnp.ones((chunk, HD), jnp.bfloat16)
        square = jnp.ones((HD, HD), jnp.bfloat16)
        first_row, starts = place(piece)
        lows = [jnp.maximum(start, 0) for start in starts]
        low, high, stop = lows[0], lows[-1], first_row + units

        for number in range(pieces):

            @pl.when(piece == number)
            def _(number=number):
                for head in range(heads):
                    q_rows[head * tokens:(head + 1) * tokens, :] = queries[number][:, head * HD:(head + 1) * HD]

        query = q_rows[...]

        def scores_of(region, number, masked, query):
            begin_unit = bases[region] + number * chunk_units
            begin = pl.multiple_of(number * chunk, chunk)
            key = keys[region][pl.ds(begin, chunk), :]
            value = jnp.concatenate([values[region][pl.ds(begin, chunk), :], ones], axis=1)
            scores = lax.dot_general(query, key, (((1,), (1,)), ((), ())), preferred_element_type=jnp.float32)
            if masked:
                column = lax.broadcasted_iota(jnp.int32, (UNIT, chunk), 1)
                ahead = column - lax.broadcasted_iota(jnp.int32, (UNIT, chunk), 0)
                allowed = [
                    (column >= (lows[unit] - begin_unit) * UNIT) & (ahead <= (first_row + unit - begin_unit) * UNIT)
                    for unit in range(units)
                ]
                scores = jnp.concatenate([
                    jnp.where(allowed[part % units], scores[part * UNIT:(part + 1) * UNIT], LOW)
                    for part in range(query.shape[0] // UNIT)
                ], axis=0)
            return scores, value

        own_start = pl.multiple_of((first_row - bases[-1]) * UNIT, UNIT)
        own = query * jnp.concatenate([keys[-1][pl.ds(own_start, tokens), :]] * heads, axis=0)
        shift[...] = jnp.dot(own, square, preferred_element_type=jnp.float32) * scale
        if late:
            total[...] = state[piece]
        else:
            total[...] = jnp.zeros(total.shape, jnp.float32)

        def visit(region, number, masked):
            scores, value = scores_of(region, number, masked, query)
            shifts = jnp.concatenate([shift[...]] * chunk_units, axis=1)
            weights = jnp.exp2(scores * scale - shifts).astype(jnp.bfloat16)
            total[...] += jnp.dot(weights, value, preferred_element_type=jnp.float32)

        def span(region):
            count = sizes[region] // chunk_units
            first = jnp.clip((low - bases[region]) // chunk_units, 0, count)
            last = jnp.clip((stop - bases[region] + chunk_units - 1) // chunk_units, 0, count)
            return first, jnp.maximum(first, last)

        for region in range(len(visited)):
            first, last = span(region)
            inner = jnp.clip((high - bases[region] + chunk_units - 1) // chunk_units, first, last)
            outer = jnp.clip((first_row - bases[region]) // chunk_units, inner, last)

            def masked_visit(number, carry, region=region, first=first, inner=inner, outer=outer):
                at = first + number
                visit(region, jnp.where(at < inner, at, at - inner + outer), True)
                return carry

            def plain_visit(number, carry, region=region):
                visit(region, number, False)
                return carry

            lax.fori_loop(0, inner - first + last - outer, masked_visit, 0)
            lax.fori_loop(inner, outer, plain_visit, 0)

        overflow = jnp.logical_not(jnp.max(total[:, HD:]) < LARGE)
        if early:
            unfinished = starts[0] < unseen
            overflow = overflow & jnp.logical_not(unfinished)

            @pl.when(unfinished)
            def _():
                state[piece] = total[...]

        @pl.when(overflow)
        def _():
            shift[...] = jnp.full(shift.shape, LOW, jnp.float32)
            total[...] = jnp.zeros(total.shape, jnp.float32)

            for region in reversed(range(regions)):
                first, last = span(region)

                def careful(number, carry, region=region, first=first):
                    head = lax.rem(number, heads)
                    some = pl.ds(pl.multiple_of(head * tokens, tokens), tokens)
                    scores, value = scores_of(region, first + number // heads, True, q_rows[some, :])
                    old = shift[some, :]
                    new = jnp.maximum(old, jnp.max(scores, axis=1, keepdims=True))
                    weights = jnp.exp2((scores - new[:, :1]) * scale).astype(jnp.bfloat16)
                    shrink = jnp.exp2((old - new) * scale)
                    update = jnp.dot(weights, value, preferred_element_type=jnp.float32)
                    total[some, :] = total[some, :] * jnp.concatenate([shrink] * 2, axis=1) + update
                    shift[some, :] = new
                    return carry

                lax.fori_loop(0, (last - first) * heads, careful, 0)

        result = (total[:, :HD] / total[:, HD:]).astype(jnp.bfloat16)
        for head in range(heads):
            o_buf[piece, :, head * HD:(head + 1) * HD] = result[head * tokens:(head + 1) * tokens]

    if late:
        def needs(piece):
            return place(piece)[1][0] < unseen

        @pl.when(sum(needs(jnp.int32(piece)).astype(jnp.int32) for piece in range(pieces)) > 0)
        def _():
            def maybe(piece, carry):
                @pl.when(needs(piece))
                def _():
                    one_piece(piece)

                return carry

            lax.fori_loop(0, pieces, maybe, 0)
            for piece in range(pieces):

                @pl.when(needs(jnp.int32(piece)))
                def _():
                    run_copies([pltpu.make_async_copy(o_buf.at[piece], outs[piece], out_sem.at[piece])])
    else:
        if early:
            w_copy = pltpu.make_async_copy(w_from, w_to, out_sem.at[pieces])
            w_copy.start()
        def always(piece, carry):
            one_piece(piece)
            for number in range(pieces):

                @pl.when(piece == number)
                def _(number=number):
                    pltpu.make_async_copy(o_buf.at[number], outs[number], out_sem.at[number]).start()

            return carry

        lax.fori_loop(0, pieces, always, 0)
        for number in range(pieces):
            pltpu.make_async_copy(o_buf.at[number], outs[number], out_sem.at[number]).wait()
        if early:
            w_copy.wait()


def attend(mode, steps, group, doc_units, queries, keys, values, w_out=None, state=None, outs=None):
    pieces = len(steps)
    regions = len(keys)
    tokens, width = queries[0].shape
    heads = width // HD
    rows = heads * tokens
    seen = sum(key.shape[0] for key in (keys[:1] if mode == "late" else keys))
    scores = rows * pieces * seen // 2
    operands = [doc_units, *queries, *keys, *values]
    in_specs = [SMEM] + [VMEM] * (pieces + 2 * regions)
    out_shape = [jax.ShapeDtypeStruct((tokens, width), jnp.bfloat16)] * pieces
    out_specs = [HBM] * pieces
    aliases = {}
    moved = 4 * tokens * pieces * width
    if mode == "early":
        operands += [w_out]
        in_specs += [HBM]
        out_shape += [pltpu.VMEM((pieces, rows, 2 * HD), jnp.float32), pltpu.VMEM(w_out.shape, w_out.dtype)]
        out_specs += [VMEM, VMEM]
        moved += 2 * w_out.size
    if mode == "late":
        aliases = {len(operands) + 1 + piece: piece for piece in range(pieces)}
        operands += [pltpu.with_memory_space_constraint(state, pltpu.VMEM), *outs]
        in_specs += [VMEM] + [HBM] * pieces
    return pl.pallas_call(
        partial(attention_kernel, mode, steps, group, regions, heads, doc_units.shape[0]),
        out_shape=out_shape,
        in_specs=in_specs,
        out_specs=out_specs,
        scratch_shapes=[
            pltpu.VMEM((rows, HD), jnp.bfloat16),
            pltpu.VMEM((pieces, tokens, width), jnp.bfloat16),
            pltpu.VMEM((rows, HD), jnp.float32),
            pltpu.VMEM((rows, 2 * HD), jnp.float32),
            pltpu.SemaphoreType.DMA((pieces + 1,)),
        ],
        input_output_aliases=aliases,
        compiler_params=params(),
        cost_estimate=pl.CostEstimate(flops=4 * HD * scores, transcendentals=scores, bytes_accessed=moved),
    )(*operands)


def project_kernel(group, steps, first, tile, resumed, last, *refs):
    refs = list(refs)
    pieces = [refs.pop(0) for step in steps]
    w_ref = refs.pop(0)
    sums = [refs.pop(0)[:, pl.ds(pl.multiple_of(first + pl.program_id(0) * tile, tile), tile)]] if resumed else []
    width = pieces[0].shape[1]
    member = lax.rem(lax.axis_index("ctx"), group)
    start = pl.multiple_of(first + pl.program_id(0) * tile, tile)
    weights = jnp.concatenate(
        [w_ref[pl.ds(pl.multiple_of((member ^ step) * width, width), width), pl.ds(start, tile)] for step in steps],
        axis=0,
    )
    rows = jnp.concatenate([piece[...] for piece in pieces], axis=1)
    product = sum(sums, jnp.dot(rows, weights, preferred_element_type=jnp.float32))
    if not last:
        refs[0][:, pl.ds(start, tile)] = product
        return
    give_ref, keep_ref = refs
    product = product.astype(jnp.bfloat16)
    block = product.shape[0] // 2
    low_first = lax.axis_index("head") == 0
    keep_ref[...] = jnp.where(low_first, product[:block], product[block:])
    give_ref[...] = jnp.where(low_first, product[block:], product[:block])


def project(group, steps, pieces, w_out, first, columns, tile, sums=None, last=True):
    rows, width = pieces[0].shape
    depth = width * len(steps)
    if last:
        spec = pl.BlockSpec((rows // 2, tile), lambda step: (0, step))
        out_specs = [spec, spec]
        out_shape = [jax.ShapeDtypeStruct((rows // 2, columns), jnp.bfloat16)] * 2
    else:
        out_specs = VMEM
        out_shape = pltpu.VMEM((rows, columns), jnp.float32)
    operands = [*pieces, w_out]
    if sums is not None:
        operands.append(sums)
    return pl.pallas_call(
        partial(project_kernel, group, steps, first, tile, sums is not None, last),
        out_shape=out_shape,
        grid=(columns // tile,),
        in_specs=[VMEM] * len(operands),
        out_specs=out_specs,
        compiler_params=params(10 * 1024 * 1024),
        cost_estimate=pl.CostEstimate(
            flops=2 * rows * depth * columns, transcendentals=0, bytes_accessed=4 * rows * columns
        ),
    )(*operands)


def sum_kernel(*refs):
    out_ref = refs[-1]
    halves = (len(refs) - 1) // 2
    columns = refs[0].shape[1]
    for half in range(halves):
        summed = refs[half][...].astype(jnp.float32) + refs[halves + half][...].astype(jnp.float32)
        out_ref[:, half * columns:(half + 1) * columns] = summed.astype(jnp.bfloat16)


def shards(queries, key_heads, value_heads, doc_units, w_out):
    count = lax.axis_size("ctx")
    group = key_heads.shape[1] // HD
    hops = min(16, count // 2) // group
    tokens, depth = queries.shape
    width = depth // group
    rank = lax.axis_index("ctx")
    member = lax.rem(rank, group)

    def column_block(value, step, size):
        return lax.dynamic_slice(value, (0, (member ^ step) * size), (tokens, size))

    def swap(value, step):
        if step == 0:
            return value
        return lax.ppermute(value, "ctx", [(source, source ^ step) for source in range(count)])

    def next_plane(value):
        return lax.ppermute(value, "ctx", [(source, source + group) for source in range(count - group)])

    def own_plane(value):
        pieces = [swap(column_block(value, step, HD), step) for step in range(group)]
        return pack_rows(pieces) if group > 1 else pieces[0]

    keys, values = [own_plane(key_heads)], [own_plane(value_heads)]
    blocks = lax.optimization_barrier(([column_block(queries, step, width) for step in range(group)], keys))[0]
    query_pieces = [swap(blocks[step], step) for step in range(group)]
    keys = [next_plane(keys[0])] + keys
    values = [next_plane(values[0])] + values
    if group > 1:
        keys, values, query_pieces[-1] = lax.optimization_barrier((keys, values, query_pieces[-1]))
    for hop in range(hops - 1):
        keys = [next_plane(keys[0])] + keys
        values = [next_plane(values[0])] + values
    if group == 1:
        keys, values = [jnp.concatenate(keys, axis=0)], [jnp.concatenate(values, axis=0)]

    def place_in_vmem(arrays):
        return [pltpu.with_memory_space_constraint(array, pltpu.VMEM) for array in arrays]

    keys, values = place_in_vmem(keys), place_in_vmem(values)
    w_here = w_out
    attention = [None] * group
    far = tuple(range(group - 1, 0, -1))
    if far:
        far_queries = [query_pieces[step] for step in far]
        *partials, state, w_here = attend("early", far, group, doc_units, far_queries, keys[-2:], values[-2:], w_out=w_out)
        finals = attend("late", far, group, doc_units, far_queries, keys, values, state=state, outs=partials)
        for step, final in zip(far, finals):
            attention[step] = swap(final, step)
        query_pieces, finals = lax.optimization_barrier((query_pieces, finals))
    (attention[0],) = attend("full", (0,), group, doc_units, query_pieces[:1], keys, values)
    columns = w_out.shape[1]
    if lax.axis_size("head") == 2:
        w_here = pltpu.with_memory_space_constraint(w_here, pltpu.VMEM)
        soon = (0,) + far[:1]
        rest = tuple(step for step in range(group) if step not in soon)
        sums = None
        if rest:
            sums = project(
                group, soon, [attention[step] for step in soon], w_here, 0, columns, 512, last=False
            )
            sums = pltpu.with_memory_space_constraint(sums, pltpu.VMEM)
        else:
            rest = soon
        size = columns // 2
        keeps, gots = [], []
        for half in range(2):
            give, keep = project(
                group, rest, [attention[step] for step in rest], w_here, half * size, size, 512, sums=sums
            )
            keeps.append(keep)
            gots.append(lax.ppermute(give, "head", [(0, 1), (1, 0)]))
        return pl.pallas_call(
            sum_kernel,
            out_shape=jax.ShapeDtypeStruct((tokens // 2, columns), jnp.bfloat16),
            compiler_params=params(),
        )(*keeps, *gots)
    product = sum(
        jnp.dot(
            attention[step],
            lax.dynamic_slice(w_out, ((member ^ step) * width, 0), (width, columns)),
            preferred_element_type=jnp.float32,
        )
        for step in range(group)
    )
    return lax.psum_scatter(product.astype(jnp.bfloat16), "head", scatter_dimension=0, tiled=True)


def solution(mesh):
    in_specs = (P("ctx", "head"), P("ctx", "head"), P("ctx", "head"), P(), P("head", None))
    out_specs = P(("ctx", "head"), None)
    return jax.shard_map(shards, mesh=mesh, in_specs=in_specs, out_specs=out_specs, check_vma=False)
```

```python
from functools import partial
import math

import jax
import jax.numpy as jnp
from jax import lax
from jax.experimental import pallas as pl
from jax.experimental.pallas import tpu as pltpu
from jax.sharding import PartitionSpec as P

HD = 128
UNIT = 128
CHUNK_UNITS = 6
LOW = -1e30
LARGE = 2.0**90
VMEM_LIMIT = 24 * 1024 * 1024
HBM = pl.BlockSpec(memory_space=pl.ANY)
SMEM = pl.BlockSpec(memory_space=pltpu.SMEM)
VMEM = pl.BlockSpec(memory_space=pltpu.VMEM)


def params(limit=VMEM_LIMIT):
    return pltpu.CompilerParams(vmem_limit_bytes=limit)


def run_copies(copies):
    for copy in copies:
        copy.start()
    for copy in copies:
        copy.wait()


def pack_kernel(group, *refs):
    packed = refs[group]
    rows = refs[0].shape[0]
    member = lax.rem(lax.axis_index("ctx"), group)
    for step in range(group):
        packed[pl.ds(pl.multiple_of((member ^ step) * rows, rows), rows), :] = refs[step][...]


def pack_rows(pieces):
    group = len(pieces)
    rows, columns = pieces[0].shape
    return pl.pallas_call(
        partial(pack_kernel, group),
        out_shape=jax.ShapeDtypeStruct((rows * group, columns), pieces[0].dtype),
        compiler_params=params(),
    )(*pieces)


def attention_kernel(mode, steps, group, regions, heads, docs, *refs):
    refs = list(refs)

    def take(number):
        taken = refs[:number]
        del refs[:number]
        return taken

    pieces = len(steps)
    early, late = mode == "early", mode == "late"
    (docs_ref,) = take(1)
    queries = take(pieces)
    keys = take(regions)
    values = take(regions)
    if early:
        (w_from,) = take(1)
    if late:
        (state,) = take(1)
        take(pieces)
    outs = take(pieces)
    if early:
        state, w_to = take(2)
    q_rows, o_buf, shift, total, out_sem = refs
    tokens = queries[0].shape[0]
    units = tokens // UNIT
    sizes = [key.shape[0] // UNIT for key in keys]
    bases = [sum(sizes[:region]) for region in range(regions)]
    chunk_units = CHUNK_UNITS if sizes[0] % CHUNK_UNITS == 0 else units
    chunk = chunk_units * UNIT
    rank = lax.axis_index("ctx")
    member = lax.rem(rank, group)
    first_unit = (rank - member + group) * units - sum(sizes)
    unseen = 0 if early else bases[1] if late else None
    visited = keys[:1] if late else keys
    scale = math.log2(math.e) / math.sqrt(HD)

    def place(piece):
        here = (rank ^ (steps[0] - piece)) * units
        starts = []
        for unit in range(units):
            doc_first = jnp.int32(0)
            end = jnp.int32(0)
            for doc in range(docs):
                end = end + docs_ref[doc]
                doc_first = jnp.where(end <= here + unit, end, doc_first)
            starts.append(doc_first - first_unit)
        return here - first_unit, starts

    def one_piece(piece):
        ones = jnp.ones((chunk, HD), jnp.bfloat16)
        square = jnp.ones((HD, HD), jnp.bfloat16)
        first_row, starts = place(piece)
        lows = [jnp.maximum(start, 0) for start in starts]
        low, high, stop = lows[0], lows[-1], first_row + units

        for number in range(pieces):

            @pl.when(piece == number)
            def _(number=number):
                for head in range(heads):
                    q_rows[head * tokens:(head + 1) * tokens, :] = queries[number][:, head * HD:(head + 1) * HD]

        query = q_rows[...]

        def scores_of(region, number, masked, query):
            begin_unit = bases[region] + number * chunk_units
            begin = pl.multiple_of(number * chunk, chunk)
            key = keys[region][pl.ds(begin, chunk), :]
            value = jnp.concatenate([values[region][pl.ds(begin, chunk), :], ones], axis=1)
            scores = lax.dot_general(query, key, (((1,), (1,)), ((), ())), preferred_element_type=jnp.float32)
            if masked:
                column = lax.broadcasted_iota(jnp.int32, (UNIT, chunk), 1)
                ahead = column - lax.broadcasted_iota(jnp.int32, (UNIT, chunk), 0)
                allowed = [
                    (column >= (lows[unit] - begin_unit) * UNIT) & (ahead <= (first_row + unit - begin_unit) * UNIT)
                    for unit in range(units)
                ]
                scores = jnp.concatenate([
                    jnp.where(allowed[part % units], scores[part * UNIT:(part + 1) * UNIT], LOW)
                    for part in range(query.shape[0] // UNIT)
                ], axis=0)
            return scores, value

        own_start = pl.multiple_of((first_row - bases[-1]) * UNIT, UNIT)
        own = query * jnp.concatenate([keys[-1][pl.ds(own_start, tokens), :]] * heads, axis=0)
        shift[...] = jnp.dot(own, square, preferred_element_type=jnp.float32) * scale
        if late:
            total[...] = state[piece]
        else:
            total[...] = jnp.zeros(total.shape, jnp.float32)

        def visit(region, number, masked):
            scores, value = scores_of(region, number, masked, query)
            shifts = jnp.concatenate([shift[...]] * chunk_units, axis=1)
            weights = jnp.exp2(scores * scale - shifts).astype(jnp.bfloat16)
            total[...] += jnp.dot(weights, value, preferred_element_type=jnp.float32)

        def span(region):
            count = sizes[region] // chunk_units
            first = jnp.clip((low - bases[region]) // chunk_units, 0, count)
            last = jnp.clip((stop - bases[region] + chunk_units - 1) // chunk_units, 0, count)
            return first, jnp.maximum(first, last)

        for region in range(len(visited)):
            first, last = span(region)
            inner = jnp.clip((high - bases[region] + chunk_units - 1) // chunk_units, first, last)
            outer = jnp.clip((first_row - bases[region]) // chunk_units, inner, last)

            def masked_visit(number, carry, region=region, first=first, inner=inner, outer=outer):
                at = first + number
                visit(region, jnp.where(at < inner, at, at - inner + outer), True)
                return carry

            def plain_visit(number, carry, region=region):
                visit(region, number, False)
                return carry

            lax.fori_loop(0, inner - first + last - outer, masked_visit, 0)
            lax.fori_loop(inner, outer, plain_visit, 0)

        overflow = jnp.logical_not(jnp.max(total[:, HD:]) < LARGE)
        if early:
            unfinished = starts[0] < unseen
            overflow = overflow & jnp.logical_not(unfinished)

            @pl.when(unfinished)
            def _():
                state[piece] = total[...]

        @pl.when(overflow)
        def _():
            shift[...] = jnp.full(shift.shape, LOW, jnp.float32)
            total[...] = jnp.zeros(total.shape, jnp.float32)

            for region in reversed(range(regions)):
                first, last = span(region)

                def careful(number, carry, region=region, first=first):
                    head = lax.rem(number, heads)
                    some = pl.ds(pl.multiple_of(head * tokens, tokens), tokens)
                    scores, value = scores_of(region, first + number // heads, True, q_rows[some, :])
                    old = shift[some, :]
                    new = jnp.maximum(old, jnp.max(scores, axis=1, keepdims=True))
                    weights = jnp.exp2((scores - new[:, :1]) * scale).astype(jnp.bfloat16)
                    shrink = jnp.exp2((old - new) * scale)
                    update = jnp.dot(weights, value, preferred_element_type=jnp.float32)
                    total[some, :] = total[some, :] * jnp.concatenate([shrink] * 2, axis=1) + update
                    shift[some, :] = new
                    return carry

                lax.fori_loop(0, (last - first) * heads, careful, 0)

        result = (total[:, :HD] / total[:, HD:]).astype(jnp.bfloat16)
        for head in range(heads):
            o_buf[piece, :, head * HD:(head + 1) * HD] = result[head * tokens:(head + 1) * tokens]

    if late:
        def needs(piece):
            return place(piece)[1][0] < unseen

        @pl.when(sum(needs(jnp.int32(piece)).astype(jnp.int32) for piece in range(pieces)) > 0)
        def _():
            def maybe(piece, carry):
                @pl.when(needs(piece))
                def _():
                    one_piece(piece)

                return carry

            lax.fori_loop(0, pieces, maybe, 0)
            for piece in range(pieces):

                @pl.when(needs(jnp.int32(piece)))
                def _():
                    run_copies([pltpu.make_async_copy(o_buf.at[piece], outs[piece], out_sem.at[piece])])
    else:
        if early:
            w_copy = pltpu.make_async_copy(w_from, w_to, out_sem.at[pieces])
            w_copy.start()
        def always(piece, carry):
            one_piece(piece)
            for number in range(pieces):

                @pl.when(piece == number)
                def _(number=number):
                    pltpu.make_async_copy(o_buf.at[number], outs[number], out_sem.at[number]).start()

            return carry

        lax.fori_loop(0, pieces, always, 0)
        for number in range(pieces):
            pltpu.make_async_copy(o_buf.at[number], outs[number], out_sem.at[number]).wait()
        if early:
            w_copy.wait()


def attend(mode, steps, group, doc_units, queries, keys, values, w_out=None, state=None, outs=None):
    pieces = len(steps)
    regions = len(keys)
    tokens, width = queries[0].shape
    heads = width // HD
    rows = heads * tokens
    seen = sum(key.shape[0] for key in (keys[:1] if mode == "late" else keys))
    scores = rows * pieces * seen // 2
    operands = [doc_units, *queries, *keys, *values]
    in_specs = [SMEM] + [VMEM] * (pieces + 2 * regions)
    out_shape = [jax.ShapeDtypeStruct((tokens, width), jnp.bfloat16)] * pieces
    out_specs = [HBM] * pieces
    aliases = {}
    moved = 4 * tokens * pieces * width
    if mode == "early":
        operands += [w_out]
        in_specs += [HBM]
        out_shape += [pltpu.VMEM((pieces, rows, 2 * HD), jnp.float32), pltpu.VMEM(w_out.shape, w_out.dtype)]
        out_specs += [VMEM, VMEM]
        moved += 2 * w_out.size
    if mode == "late":
        aliases = {len(operands) + 1 + piece: piece for piece in range(pieces)}
        operands += [pltpu.with_memory_space_constraint(state, pltpu.VMEM), *outs]
        in_specs += [VMEM] + [HBM] * pieces
    return pl.pallas_call(
        partial(attention_kernel, mode, steps, group, regions, heads, doc_units.shape[0]),
        out_shape=out_shape,
        in_specs=in_specs,
        out_specs=out_specs,
        scratch_shapes=[
            pltpu.VMEM((rows, HD), jnp.bfloat16),
            pltpu.VMEM((pieces, tokens, width), jnp.bfloat16),
            pltpu.VMEM((rows, HD), jnp.float32),
            pltpu.VMEM((rows, 2 * HD), jnp.float32),
            pltpu.SemaphoreType.DMA((pieces + 1,)),
        ],
        input_output_aliases=aliases,
        compiler_params=params(),
        cost_estimate=pl.CostEstimate(flops=4 * HD * scores, transcendentals=scores, bytes_accessed=moved),
    )(*operands)


def project_kernel(group, steps, first, tile, resumed, last, *refs):
    refs = list(refs)
    pieces = [refs.pop(0) for step in steps]
    w_ref = refs.pop(0)
    sums = [refs.pop(0)[:, pl.ds(pl.multiple_of(first + pl.program_id(0) * tile, tile), tile)]] if resumed else []
    width = pieces[0].shape[1]
    member = lax.rem(lax.axis_index("ctx"), group)
    start = pl.multiple_of(first + pl.program_id(0) * tile, tile)
    weights = jnp.concatenate(
        [w_ref[pl.ds(pl.multiple_of((member ^ step) * width, width), width), pl.ds(start, tile)] for step in steps],
        axis=0,
    )
    rows = jnp.concatenate([piece[...] for piece in pieces], axis=1)
    product = sum(sums, jnp.dot(rows, weights, preferred_element_type=jnp.float32))
    if not last:
        refs[0][:, pl.ds(start, tile)] = product
        return
    give_ref, keep_ref = refs
    product = product.astype(jnp.bfloat16)
    block = product.shape[0] // 2
    low_first = lax.axis_index("head") == 0
    keep_ref[...] = jnp.where(low_first, product[:block], product[block:])
    give_ref[...] = jnp.where(low_first, product[block:], product[:block])


def project(group, steps, pieces, w_out, first, columns, tile, sums=None, last=True):
    rows, width = pieces[0].shape
    depth = width * len(steps)
    if last:
        spec = pl.BlockSpec((rows // 2, tile), lambda step: (0, step))
        out_specs = [spec, spec]
        out_shape = [jax.ShapeDtypeStruct((rows // 2, columns), jnp.bfloat16)] * 2
    else:
        out_specs = VMEM
        out_shape = pltpu.VMEM((rows, columns), jnp.float32)
    operands = [*pieces, w_out]
    if sums is not None:
        operands.append(sums)
    return pl.pallas_call(
        partial(project_kernel, group, steps, first, tile, sums is not None, last),
        out_shape=out_shape,
        grid=(columns // tile,),
        in_specs=[VMEM] * len(operands),
        out_specs=out_specs,
        compiler_params=params(10 * 1024 * 1024),
        cost_estimate=pl.CostEstimate(
            flops=2 * rows * depth * columns, transcendentals=0, bytes_accessed=4 * rows * columns
        ),
    )(*operands)


def sum_kernel(*refs):
    out_ref = refs[-1]
    halves = (len(refs) - 1) // 2
    columns = refs[0].shape[1]
    for half in range(halves):
        summed = refs[half][...].astype(jnp.float32) + refs[halves + half][...].astype(jnp.float32)
        out_ref[:, half * columns:(half + 1) * columns] = summed.astype(jnp.bfloat16)


def shards(queries, key_heads, value_heads, doc_units, w_out):
    count = lax.axis_size("ctx")
    group = key_heads.shape[1] // HD
    hops = min(16, count // 2) // group
    tokens, depth = queries.shape
    width = depth // group
    rank = lax.axis_index("ctx")
    member = lax.rem(rank, group)

    def column_block(value, step, size):
        return lax.dynamic_slice(value, (0, (member ^ step) * size), (tokens, size))

    def swap(value, step):
        if step == 0:
            return value
        return lax.ppermute(value, "ctx", [(source, source ^ step) for source in range(count)])

    def next_plane(value):
        return lax.ppermute(value, "ctx", [(source, source + group) for source in range(count - group)])

    def own_plane(value):
        pieces = [swap(column_block(value, step, HD), step) for step in range(group)]
        return pack_rows(pieces) if group > 1 else pieces[0]

    keys, values = [own_plane(key_heads)], [own_plane(value_heads)]
    queries = lax.optimization_barrier((queries, keys, values))[0]
    query_pieces = [swap(column_block(queries, step, width), step) for step in range(group)]
    keys = [next_plane(keys[0])] + keys
    values = [next_plane(values[0])] + values
    if group > 1:
        keys, values, query_pieces[-1] = lax.optimization_barrier((keys, values, query_pieces[-1]))
    for hop in range(hops - 1):
        keys = [next_plane(keys[0])] + keys
        values = [next_plane(values[0])] + values
    if group == 1:
        keys, values = [jnp.concatenate(keys, axis=0)], [jnp.concatenate(values, axis=0)]

    def place_in_vmem(arrays):
        return [pltpu.with_memory_space_constraint(array, pltpu.VMEM) for array in arrays]

    keys, values = place_in_vmem(keys), place_in_vmem(values)
    w_here = w_out
    attention = [None] * group
    far = tuple(range(group - 1, 0, -1))
    if far:
        far_queries = [query_pieces[step] for step in far]
        *partials, state, w_here = attend("early", far, group, doc_units, far_queries, keys[-2:], values[-2:], w_out=w_out)
        finals = attend("late", far, group, doc_units, far_queries, keys, values, state=state, outs=partials)
        for step, final in zip(far, finals):
            attention[step] = swap(final, step)
        query_pieces, finals = lax.optimization_barrier((query_pieces, finals))
    (attention[0],) = attend("full", (0,), group, doc_units, query_pieces[:1], keys, values)
    columns = w_out.shape[1]
    if lax.axis_size("head") == 2:
        w_here = pltpu.with_memory_space_constraint(w_here, pltpu.VMEM)
        soon = (0,) + far[:1]
        rest = tuple(step for step in range(group) if step not in soon)
        sums = None
        if rest:
            sums = project(
                group, soon, [attention[step] for step in soon], w_here, 0, columns, 512, last=False
            )
            sums = pltpu.with_memory_space_constraint(sums, pltpu.VMEM)
        else:
            rest = soon
        size = columns // 2
        keeps, gots = [], []
        for half in range(2):
            give, keep = project(
                group, rest, [attention[step] for step in rest], w_here, half * size, size, 512, sums=sums
            )
            keeps.append(keep)
            gots.append(lax.ppermute(give, "head", [(0, 1), (1, 0)]))
        return pl.pallas_call(
            sum_kernel,
            out_shape=jax.ShapeDtypeStruct((tokens // 2, columns), jnp.bfloat16),
            compiler_params=params(),
        )(*keeps, *gots)
    product = sum(
        jnp.dot(
            attention[step],
            lax.dynamic_slice(w_out, ((member ^ step) * width, 0), (width, columns)),
            preferred_element_type=jnp.float32,
        )
        for step in range(group)
    )
    return lax.psum_scatter(product.astype(jnp.bfloat16), "head", scatter_dimension=0, tiled=True)


def solution(mesh):
    in_specs = (P("ctx", "head"), P("ctx", "head"), P("ctx", "head"), P(), P("head", None))
    out_specs = P(("ctx", "head"), None)
    return jax.shard_map(shards, mesh=mesh, in_specs=in_specs, out_specs=out_specs, check_vma=False)
```

```python
from functools import partial
import math

import jax
import jax.numpy as jnp
from jax import lax
from jax.experimental import pallas as pl
from jax.experimental.pallas import tpu as pltpu
from jax.sharding import PartitionSpec as P

HD = 128
UNIT = 128
CHUNK_UNITS = 6
LOW = -1e30
LARGE = 2.0**90
VMEM_LIMIT = 24 * 1024 * 1024
HBM = pl.BlockSpec(memory_space=pl.ANY)
SMEM = pl.BlockSpec(memory_space=pltpu.SMEM)
VMEM = pl.BlockSpec(memory_space=pltpu.VMEM)


def params(limit=VMEM_LIMIT):
    return pltpu.CompilerParams(vmem_limit_bytes=limit)


def run_copies(copies):
    for copy in copies:
        copy.start()
    for copy in copies:
        copy.wait()


def pack_kernel(group, *refs):
    packed = refs[group]
    rows = refs[0].shape[0]
    member = lax.rem(lax.axis_index("ctx"), group)
    for step in range(group):
        packed[pl.ds(pl.multiple_of((member ^ step) * rows, rows), rows), :] = refs[step][...]


def pack_rows(pieces):
    group = len(pieces)
    rows, columns = pieces[0].shape
    return pl.pallas_call(
        partial(pack_kernel, group),
        out_shape=jax.ShapeDtypeStruct((rows * group, columns), pieces[0].dtype),
        compiler_params=params(),
    )(*pieces)


def attention_kernel(mode, steps, group, regions, heads, docs, *refs):
    refs = list(refs)

    def take(number):
        taken = refs[:number]
        del refs[:number]
        return taken

    pieces = len(steps)
    early, late = mode == "early", mode == "late"
    (docs_ref,) = take(1)
    queries = take(pieces)
    keys = take(regions)
    values = take(regions)
    if early:
        (w_from,) = take(1)
    if late:
        (state,) = take(1)
        take(pieces)
    outs = take(pieces)
    if early:
        state, w_to = take(2)
    q_rows, o_buf, shift, total, out_sem = refs
    tokens = queries[0].shape[0]
    units = tokens // UNIT
    sizes = [key.shape[0] // UNIT for key in keys]
    bases = [sum(sizes[:region]) for region in range(regions)]
    chunk_units = CHUNK_UNITS if sizes[0] % CHUNK_UNITS == 0 and not late else units
    chunk = chunk_units * UNIT
    rank = lax.axis_index("ctx")
    member = lax.rem(rank, group)
    first_unit = (rank - member + group) * units - sum(sizes)
    unseen = 0 if early else bases[1] if late else None
    visited = keys[:1] if late else keys
    scale = math.log2(math.e) / math.sqrt(HD)

    def place(piece):
        here = (rank ^ (steps[0] - piece)) * units
        starts = []
        for unit in range(units):
            doc_first = jnp.int32(0)
            end = jnp.int32(0)
            for doc in range(docs):
                end = end + docs_ref[doc]
                doc_first = jnp.where(end <= here + unit, end, doc_first)
            starts.append(doc_first - first_unit)
        return here - first_unit, starts

    def one_piece(piece):
        ones = jnp.ones((chunk, HD), jnp.bfloat16)
        square = jnp.ones((HD, HD), jnp.bfloat16)
        first_row, starts = place(piece)
        lows = [jnp.maximum(start, 0) for start in starts]
        low, high, stop = lows[0], lows[-1], first_row + units

        for number in range(pieces):

            @pl.when(piece == number)
            def _(number=number):
                for head in range(heads):
                    q_rows[head * tokens:(head + 1) * tokens, :] = queries[number][:, head * HD:(head + 1) * HD]

        query = q_rows[...]

        def scores_of(region, number, masked, query):
            begin_unit = bases[region] + number * chunk_units
            begin = pl.multiple_of(number * chunk, chunk)
            key = keys[region][pl.ds(begin, chunk), :]
            value = jnp.concatenate([values[region][pl.ds(begin, chunk), :], ones], axis=1)
            scores = lax.dot_general(query, key, (((1,), (1,)), ((), ())), preferred_element_type=jnp.float32)
            if masked:
                column = lax.broadcasted_iota(jnp.int32, (UNIT, chunk), 1)
                ahead = column - lax.broadcasted_iota(jnp.int32, (UNIT, chunk), 0)
                allowed = [
                    (column >= (lows[unit] - begin_unit) * UNIT) & (ahead <= (first_row + unit - begin_unit) * UNIT)
                    for unit in range(units)
                ]
                scores = jnp.concatenate([
                    jnp.where(allowed[part % units], scores[part * UNIT:(part + 1) * UNIT], LOW)
                    for part in range(query.shape[0] // UNIT)
                ], axis=0)
            return scores, value

        own_start = pl.multiple_of((first_row - bases[-1]) * UNIT, UNIT)
        own = query * jnp.concatenate([keys[-1][pl.ds(own_start, tokens), :]] * heads, axis=0)
        shift[...] = jnp.dot(own, square, preferred_element_type=jnp.float32) * scale
        if late:
            total[...] = state[piece]
        else:
            total[...] = jnp.zeros(total.shape, jnp.float32)

        def visit(region, number, masked):
            scores, value = scores_of(region, number, masked, query)
            shifts = jnp.concatenate([shift[...]] * chunk_units, axis=1)
            weights = jnp.exp2(scores * scale - shifts).astype(jnp.bfloat16)
            total[...] += jnp.dot(weights, value, preferred_element_type=jnp.float32)

        def span(region):
            count = sizes[region] // chunk_units
            first = jnp.clip((low - bases[region]) // chunk_units, 0, count)
            last = jnp.clip((stop - bases[region] + chunk_units - 1) // chunk_units, 0, count)
            return first, jnp.maximum(first, last)

        for region in range(len(visited)):
            first, last = span(region)
            inner = jnp.clip((high - bases[region] + chunk_units - 1) // chunk_units, first, last)
            outer = jnp.clip((first_row - bases[region]) // chunk_units, inner, last)

            def masked_visit(number, carry, region=region, first=first, inner=inner, outer=outer):
                at = first + number
                visit(region, jnp.where(at < inner, at, at - inner + outer), True)
                return carry

            def plain_visit(number, carry, region=region):
                visit(region, number, False)
                return carry

            lax.fori_loop(0, inner - first + last - outer, masked_visit, 0)
            lax.fori_loop(inner, outer, plain_visit, 0)

        overflow = jnp.logical_not(jnp.max(total[:, HD:]) < LARGE)
        if early:
            unfinished = starts[0] < unseen
            overflow = overflow & jnp.logical_not(unfinished)

            @pl.when(unfinished)
            def _():
                state[piece] = total[...]

        @pl.when(overflow)
        def _():
            shift[...] = jnp.full(shift.shape, LOW, jnp.float32)
            total[...] = jnp.zeros(total.shape, jnp.float32)

            for region in reversed(range(regions)):
                first, last = span(region)

                def careful(number, carry, region=region, first=first):
                    head = lax.rem(number, heads)
                    some = pl.ds(pl.multiple_of(head * tokens, tokens), tokens)
                    scores, value = scores_of(region, first + number // heads, True, q_rows[some, :])
                    old = shift[some, :]
                    new = jnp.maximum(old, jnp.max(scores, axis=1, keepdims=True))
                    weights = jnp.exp2((scores - new[:, :1]) * scale).astype(jnp.bfloat16)
                    shrink = jnp.exp2((old - new) * scale)
                    update = jnp.dot(weights, value, preferred_element_type=jnp.float32)
                    total[some, :] = total[some, :] * jnp.concatenate([shrink] * 2, axis=1) + update
                    shift[some, :] = new
                    return carry

                lax.fori_loop(0, (last - first) * heads, careful, 0)

        result = (total[:, :HD] / total[:, HD:]).astype(jnp.bfloat16)
        for head in range(heads):
            o_buf[piece, :, head * HD:(head + 1) * HD] = result[head * tokens:(head + 1) * tokens]

    if late:
        def needs(piece):
            return place(piece)[1][0] < unseen

        @pl.when(sum(needs(jnp.int32(piece)).astype(jnp.int32) for piece in range(pieces)) > 0)
        def _():
            def maybe(piece, carry):
                @pl.when(needs(piece))
                def _():
                    one_piece(piece)

                return carry

            lax.fori_loop(0, pieces, maybe, 0)
            for piece in range(pieces):

                @pl.when(needs(jnp.int32(piece)))
                def _():
                    run_copies([pltpu.make_async_copy(o_buf.at[piece], outs[piece], out_sem.at[piece])])
    else:
        if early:
            w_copy = pltpu.make_async_copy(w_from, w_to, out_sem.at[pieces])
            w_copy.start()
        def always(piece, carry):
            one_piece(piece)
            for number in range(pieces):

                @pl.when(piece == number)
                def _(number=number):
                    pltpu.make_async_copy(o_buf.at[number], outs[number], out_sem.at[number]).start()

            return carry

        lax.fori_loop(0, pieces, always, 0)
        for number in range(pieces):
            pltpu.make_async_copy(o_buf.at[number], outs[number], out_sem.at[number]).wait()
        if early:
            w_copy.wait()


def attend(mode, steps, group, doc_units, queries, keys, values, w_out=None, state=None, outs=None):
    pieces = len(steps)
    regions = len(keys)
    tokens, width = queries[0].shape
    heads = width // HD
    rows = heads * tokens
    seen = sum(key.shape[0] for key in (keys[:1] if mode == "late" else keys))
    scores = rows * pieces * seen // 2
    operands = [doc_units, *queries, *keys, *values]
    in_specs = [SMEM] + [VMEM] * (pieces + 2 * regions)
    out_shape = [jax.ShapeDtypeStruct((tokens, width), jnp.bfloat16)] * pieces
    out_specs = [HBM] * pieces
    aliases = {}
    moved = 4 * tokens * pieces * width
    if mode == "early":
        operands += [w_out]
        in_specs += [HBM]
        out_shape += [pltpu.VMEM((pieces, rows, 2 * HD), jnp.float32), pltpu.VMEM(w_out.shape, w_out.dtype)]
        out_specs += [VMEM, VMEM]
        moved += 2 * w_out.size
    if mode == "late":
        aliases = {len(operands) + 1 + piece: piece for piece in range(pieces)}
        operands += [pltpu.with_memory_space_constraint(state, pltpu.VMEM), *outs]
        in_specs += [VMEM] + [HBM] * pieces
    return pl.pallas_call(
        partial(attention_kernel, mode, steps, group, regions, heads, doc_units.shape[0]),
        out_shape=out_shape,
        in_specs=in_specs,
        out_specs=out_specs,
        scratch_shapes=[
            pltpu.VMEM((rows, HD), jnp.bfloat16),
            pltpu.VMEM((pieces, tokens, width), jnp.bfloat16),
            pltpu.VMEM((rows, HD), jnp.float32),
            pltpu.VMEM((rows, 2 * HD), jnp.float32),
            pltpu.SemaphoreType.DMA((pieces + 1,)),
        ],
        input_output_aliases=aliases,
        compiler_params=params(),
        cost_estimate=pl.CostEstimate(flops=4 * HD * scores, transcendentals=scores, bytes_accessed=moved),
    )(*operands)


def project_kernel(group, steps, first, tile, resumed, last, *refs):
    refs = list(refs)
    pieces = [refs.pop(0) for step in steps]
    w_ref = refs.pop(0)
    sums = [refs.pop(0)[:, pl.ds(pl.multiple_of(first + pl.program_id(0) * tile, tile), tile)]] if resumed else []
    width = pieces[0].shape[1]
    member = lax.rem(lax.axis_index("ctx"), group)
    start = pl.multiple_of(first + pl.program_id(0) * tile, tile)
    weights = jnp.concatenate(
        [w_ref[pl.ds(pl.multiple_of((member ^ step) * width, width), width), pl.ds(start, tile)] for step in steps],
        axis=0,
    )
    rows = jnp.concatenate([piece[...] for piece in pieces], axis=1)
    product = sum(sums, jnp.dot(rows, weights, preferred_element_type=jnp.float32))
    if not last:
        refs[0][:, pl.ds(start, tile)] = product
        return
    give_ref, keep_ref = refs
    product = product.astype(jnp.bfloat16)
    block = product.shape[0] // 2
    low_first = lax.axis_index("head") == 0
    keep_ref[...] = jnp.where(low_first, product[:block], product[block:])
    give_ref[...] = jnp.where(low_first, product[block:], product[:block])


def project(group, steps, pieces, w_out, first, columns, tile, sums=None, last=True):
    rows, width = pieces[0].shape
    depth = width * len(steps)
    if last:
        spec = pl.BlockSpec((rows // 2, tile), lambda step: (0, step))
        out_specs = [spec, spec]
        out_shape = [jax.ShapeDtypeStruct((rows // 2, columns), jnp.bfloat16)] * 2
    else:
        out_specs = VMEM
        out_shape = pltpu.VMEM((rows, columns), jnp.float32)
    operands = [*pieces, w_out]
    if sums is not None:
        operands.append(sums)
    return pl.pallas_call(
        partial(project_kernel, group, steps, first, tile, sums is not None, last),
        out_shape=out_shape,
        grid=(columns // tile,),
        in_specs=[VMEM] * len(operands),
        out_specs=out_specs,
        compiler_params=params(10 * 1024 * 1024),
        cost_estimate=pl.CostEstimate(
            flops=2 * rows * depth * columns, transcendentals=0, bytes_accessed=4 * rows * columns
        ),
    )(*operands)


def sum_kernel(*refs):
    out_ref = refs[-1]
    halves = (len(refs) - 1) // 2
    columns = refs[0].shape[1]
    for half in range(halves):
        summed = refs[half][...].astype(jnp.float32) + refs[halves + half][...].astype(jnp.float32)
        out_ref[:, half * columns:(half + 1) * columns] = summed.astype(jnp.bfloat16)


def shards(queries, key_heads, value_heads, doc_units, w_out):
    count = lax.axis_size("ctx")
    group = key_heads.shape[1] // HD
    hops = min(16, count // 2) // group
    tokens, depth = queries.shape
    width = depth // group
    rank = lax.axis_index("ctx")
    member = lax.rem(rank, group)

    def column_block(value, step, size):
        return lax.dynamic_slice(value, (0, (member ^ step) * size), (tokens, size))

    def swap(value, step):
        if step == 0:
            return value
        return lax.ppermute(value, "ctx", [(source, source ^ step) for source in range(count)])

    def next_plane(value):
        return lax.ppermute(value, "ctx", [(source, source + group) for source in range(count - group)])

    def own_plane(value):
        pieces = [swap(column_block(value, step, HD), step) for step in range(group)]
        return pack_rows(pieces) if group > 1 else pieces[0]

    keys, values = [own_plane(key_heads)], [own_plane(value_heads)]
    queries = lax.optimization_barrier((queries, keys, values))[0]
    query_pieces = [swap(column_block(queries, step, width), step) for step in range(group)]
    keys = [next_plane(keys[0])] + keys
    values = [next_plane(values[0])] + values
    if group > 1:
        keys, values, query_pieces[-1] = lax.optimization_barrier((keys, values, query_pieces[-1]))
    for hop in range(hops - 1):
        keys = [next_plane(keys[0])] + keys
        values = [next_plane(values[0])] + values
    if group == 1:
        keys, values = [jnp.concatenate(keys, axis=0)], [jnp.concatenate(values, axis=0)]

    def place_in_vmem(arrays):
        return [pltpu.with_memory_space_constraint(array, pltpu.VMEM) for array in arrays]

    keys, values = place_in_vmem(keys), place_in_vmem(values)
    w_here = w_out
    attention = [None] * group
    far = tuple(range(group - 1, 0, -1))
    if far:
        far_queries = [query_pieces[step] for step in far]
        *partials, state, w_here = attend("early", far, group, doc_units, far_queries, keys[-2:], values[-2:], w_out=w_out)
        finals = attend("late", far, group, doc_units, far_queries, keys, values, state=state, outs=partials)
        for step, final in zip(far, finals):
            attention[step] = swap(final, step)
        query_pieces, finals = lax.optimization_barrier((query_pieces, finals))
    (attention[0],) = attend("full", (0,), group, doc_units, query_pieces[:1], keys, values)
    columns = w_out.shape[1]
    if lax.axis_size("head") == 2:
        w_here = pltpu.with_memory_space_constraint(w_here, pltpu.VMEM)
        soon = (0,) + far[:1]
        rest = tuple(step for step in range(group) if step not in soon)
        sums = None
        if rest:
            sums = project(
                group, soon, [attention[step] for step in soon], w_here, 0, columns, 512, last=False
            )
            sums = pltpu.with_memory_space_constraint(sums, pltpu.VMEM)
        else:
            rest = soon
        size = columns // 2
        keeps, gots = [], []
        for half in range(2):
            give, keep = project(
                group, rest, [attention[step] for step in rest], w_here, half * size, size, 512, sums=sums
            )
            keeps.append(keep)
            gots.append(lax.ppermute(give, "head", [(0, 1), (1, 0)]))
        return pl.pallas_call(
            sum_kernel,
            out_shape=jax.ShapeDtypeStruct((tokens // 2, columns), jnp.bfloat16),
            compiler_params=params(),
        )(*keeps, *gots)
    product = sum(
        jnp.dot(
            attention[step],
            lax.dynamic_slice(w_out, ((member ^ step) * width, 0), (width, columns)),
            preferred_element_type=jnp.float32,
        )
        for step in range(group)
    )
    return lax.psum_scatter(product.astype(jnp.bfloat16), "head", scatter_dimension=0, tiled=True)


def solution(mesh):
    in_specs = (P("ctx", "head"), P("ctx", "head"), P("ctx", "head"), P(), P("head", None))
    out_specs = P(("ctx", "head"), None)
    return jax.shard_map(shards, mesh=mesh, in_specs=in_specs, out_specs=out_specs, check_vma=False)
```

```python
from functools import partial
import math

import jax
import jax.numpy as jnp
from jax import lax
from jax.experimental import pallas as pl
from jax.experimental.pallas import tpu as pltpu
from jax.sharding import PartitionSpec as P

HD = 128
UNIT = 128
CHUNK_UNITS = 6
LOW = -1e30
LARGE = 2.0**90
VMEM_LIMIT = 24 * 1024 * 1024
HBM = pl.BlockSpec(memory_space=pl.ANY)
SMEM = pl.BlockSpec(memory_space=pltpu.SMEM)
VMEM = pl.BlockSpec(memory_space=pltpu.VMEM)


def params(limit=VMEM_LIMIT):
    return pltpu.CompilerParams(vmem_limit_bytes=limit)


def pack_kernel(group, *refs):
    packed = refs[group]
    rows = refs[0].shape[0]
    member = lax.rem(lax.axis_index("ctx"), group)
    for step in range(group):
        packed[pl.ds(pl.multiple_of((member ^ step) * rows, rows), rows), :] = refs[step][...]


def pack_rows(pieces):
    group = len(pieces)
    rows, columns = pieces[0].shape
    return pl.pallas_call(
        partial(pack_kernel, group),
        out_shape=jax.ShapeDtypeStruct((rows * group, columns), pieces[0].dtype),
        compiler_params=params(),
    )(*pieces)


def attention_kernel(mode, steps, group, regions, heads, docs, *refs):
    refs = list(refs)

    def take(number):
        taken = refs[:number]
        del refs[:number]
        return taken

    pieces = len(steps)
    early, late = mode == "early", mode == "late"
    (docs_ref,) = take(1)
    queries = take(pieces)
    keys = take(regions)
    values = take(regions)
    if early:
        (w_from,) = take(1)
    if late:
        (state,) = take(1)
        take(pieces)
    outs = take(pieces)
    if early:
        state, w_to = take(2)
    q_rows, o_buf, shift, total, out_sem = refs
    tokens = queries[0].shape[0]
    units = tokens // UNIT
    sizes = [key.shape[0] // UNIT for key in keys]
    bases = [sum(sizes[:region]) for region in range(regions)]
    chunk_units = CHUNK_UNITS if sizes[0] % CHUNK_UNITS == 0 and not late else units
    chunk = chunk_units * UNIT
    rank = lax.axis_index("ctx")
    member = lax.rem(rank, group)
    first_unit = (rank - member + group) * units - sum(sizes)
    unseen = 0 if early else bases[1] if late else None
    visited = keys[:1] if late else keys
    scale = math.log2(math.e) / math.sqrt(HD)

    def place(piece):
        here = (rank ^ (steps[0] - piece)) * units
        starts = []
        for unit in range(units):
            doc_first = jnp.int32(0)
            end = jnp.int32(0)
            for doc in range(docs):
                end = end + docs_ref[doc]
                doc_first = jnp.where(end <= here + unit, end, doc_first)
            starts.append(doc_first - first_unit)
        return here - first_unit, starts

    def one_piece(piece):
        ones = jnp.ones((chunk, HD), jnp.bfloat16)
        square = jnp.ones((HD, HD), jnp.bfloat16)
        first_row, starts = place(piece)
        lows = [jnp.maximum(start, 0) for start in starts]
        low, high, stop = lows[0], lows[-1], first_row + units

        for number in range(pieces):

            @pl.when(piece == number)
            def _(number=number):
                for head in range(heads):
                    q_rows[head * tokens:(head + 1) * tokens, :] = queries[number][:, head * HD:(head + 1) * HD]

        query = q_rows[...]

        def scores_of(region, number, masked, query):
            begin_unit = bases[region] + number * chunk_units
            begin = pl.multiple_of(number * chunk, chunk)
            key = keys[region][pl.ds(begin, chunk), :]
            value = jnp.concatenate([values[region][pl.ds(begin, chunk), :], ones], axis=1)
            scores = lax.dot_general(query, key, (((1,), (1,)), ((), ())), preferred_element_type=jnp.float32)
            if masked:
                column = lax.broadcasted_iota(jnp.int32, (UNIT, chunk), 1)
                ahead = column - lax.broadcasted_iota(jnp.int32, (UNIT, chunk), 0)
                allowed = [
                    (column >= (lows[unit] - begin_unit) * UNIT) & (ahead <= (first_row + unit - begin_unit) * UNIT)
                    for unit in range(units)
                ]
                scores = jnp.concatenate([
                    jnp.where(allowed[part % units], scores[part * UNIT:(part + 1) * UNIT], LOW)
                    for part in range(query.shape[0] // UNIT)
                ], axis=0)
            return scores, value

        own_start = pl.multiple_of((first_row - bases[-1]) * UNIT, UNIT)
        own = query * jnp.concatenate([keys[-1][pl.ds(own_start, tokens), :]] * heads, axis=0)
        shift[...] = jnp.dot(own, square, preferred_element_type=jnp.float32) * scale
        if late:
            total[...] = state[piece]
        else:
            total[...] = jnp.zeros(total.shape, jnp.float32)

        def visit(region, number, masked):
            scores, value = scores_of(region, number, masked, query)
            shifts = jnp.concatenate([shift[...]] * chunk_units, axis=1)
            weights = jnp.exp2(scores * scale - shifts).astype(jnp.bfloat16)
            total[...] += jnp.dot(weights, value, preferred_element_type=jnp.float32)

        def span(region):
            count = sizes[region] // chunk_units
            first = jnp.clip((low - bases[region]) // chunk_units, 0, count)
            last = jnp.clip((stop - bases[region] + chunk_units - 1) // chunk_units, 0, count)
            return first, jnp.maximum(first, last)

        for region in range(len(visited)):
            first, last = span(region)
            inner = jnp.clip((high - bases[region] + chunk_units - 1) // chunk_units, first, last)
            outer = jnp.clip((first_row - bases[region]) // chunk_units, inner, last)

            def masked_visit(number, carry, region=region, first=first, inner=inner, outer=outer):
                at = first + number
                visit(region, jnp.where(at < inner, at, at - inner + outer), True)
                return carry

            def plain_visit(number, carry, region=region):
                visit(region, number, False)
                return carry

            lax.fori_loop(0, inner - first + last - outer, masked_visit, 0)
            lax.fori_loop(inner, outer, plain_visit, 0)

        overflow = jnp.logical_not(jnp.max(total[:, HD:]) < LARGE)
        if early:
            unfinished = starts[0] < unseen
            overflow = overflow & jnp.logical_not(unfinished)

            @pl.when(unfinished)
            def _():
                state[piece] = total[...]

        @pl.when(overflow)
        def _():
            shift[...] = jnp.full(shift.shape, LOW, jnp.float32)
            total[...] = jnp.zeros(total.shape, jnp.float32)

            for region in reversed(range(regions)):
                first, last = span(region)

                def careful(number, carry, region=region, first=first):
                    head = lax.rem(number, heads)
                    some = pl.ds(pl.multiple_of(head * tokens, tokens), tokens)
                    scores, value = scores_of(region, first + number // heads, True, q_rows[some, :])
                    old = shift[some, :]
                    new = jnp.maximum(old, jnp.max(scores, axis=1, keepdims=True))
                    weights = jnp.exp2((scores - new[:, :1]) * scale).astype(jnp.bfloat16)
                    shrink = jnp.exp2((old - new) * scale)
                    update = jnp.dot(weights, value, preferred_element_type=jnp.float32)
                    total[some, :] = total[some, :] * jnp.concatenate([shrink] * 2, axis=1) + update
                    shift[some, :] = new
                    return carry

                lax.fori_loop(0, (last - first) * heads, careful, 0)

        result = (total[:, :HD] / total[:, HD:]).astype(jnp.bfloat16)
        for head in range(heads):
            o_buf[piece, :, head * HD:(head + 1) * HD] = result[head * tokens:(head + 1) * tokens]

    if late:
        def needs(piece):
            return place(piece)[1][0] < unseen

        @pl.when(sum(needs(jnp.int32(piece)).astype(jnp.int32) for piece in range(pieces)) > 0)
        def _():
            def maybe(piece, carry):
                @pl.when(needs(piece))
                def _():
                    one_piece(piece)
                    for number in range(pieces):

                        @pl.when(piece == number)
                        def _(number=number):
                            pltpu.make_async_copy(o_buf.at[number], outs[number], out_sem.at[number]).start()

                return carry

            lax.fori_loop(0, pieces, maybe, 0)
            for number in range(pieces):

                @pl.when(needs(jnp.int32(number)))
                def _(number=number):
                    pltpu.make_async_copy(o_buf.at[number], outs[number], out_sem.at[number]).wait()
    else:
        if early:
            w_copy = pltpu.make_async_copy(w_from, w_to, out_sem.at[pieces])
            w_copy.start()
        def always(piece, carry):
            one_piece(piece)
            for number in range(pieces):

                @pl.when(piece == number)
                def _(number=number):
                    pltpu.make_async_copy(o_buf.at[number], outs[number], out_sem.at[number]).start()

            return carry

        lax.fori_loop(0, pieces, always, 0)
        for number in range(pieces):
            pltpu.make_async_copy(o_buf.at[number], outs[number], out_sem.at[number]).wait()
        if early:
            w_copy.wait()


def attend(mode, steps, group, doc_units, queries, keys, values, w_out=None, state=None, outs=None):
    pieces = len(steps)
    regions = len(keys)
    tokens, width = queries[0].shape
    heads = width // HD
    rows = heads * tokens
    seen = sum(key.shape[0] for key in (keys[:1] if mode == "late" else keys))
    scores = rows * pieces * seen // 2
    operands = [doc_units, *queries, *keys, *values]
    in_specs = [SMEM] + [VMEM] * (pieces + 2 * regions)
    out_shape = [jax.ShapeDtypeStruct((tokens, width), jnp.bfloat16)] * pieces
    out_specs = [HBM] * pieces
    aliases = {}
    moved = 4 * tokens * pieces * width
    if mode == "early":
        operands += [w_out]
        in_specs += [HBM]
        out_shape += [pltpu.VMEM((pieces, rows, 2 * HD), jnp.float32), pltpu.VMEM(w_out.shape, w_out.dtype)]
        out_specs += [VMEM, VMEM]
        moved += 2 * w_out.size
    if mode == "late":
        aliases = {len(operands) + 1 + piece: piece for piece in range(pieces)}
        operands += [pltpu.with_memory_space_constraint(state, pltpu.VMEM), *outs]
        in_specs += [VMEM] + [HBM] * pieces
    return pl.pallas_call(
        partial(attention_kernel, mode, steps, group, regions, heads, doc_units.shape[0]),
        out_shape=out_shape,
        in_specs=in_specs,
        out_specs=out_specs,
        scratch_shapes=[
            pltpu.VMEM((rows, HD), jnp.bfloat16),
            pltpu.VMEM((pieces, tokens, width), jnp.bfloat16),
            pltpu.VMEM((rows, HD), jnp.float32),
            pltpu.VMEM((rows, 2 * HD), jnp.float32),
            pltpu.SemaphoreType.DMA((pieces + 1,)),
        ],
        input_output_aliases=aliases,
        compiler_params=params(),
        cost_estimate=pl.CostEstimate(flops=4 * HD * scores, transcendentals=scores, bytes_accessed=moved),
    )(*operands)


def project_kernel(group, steps, first, tile, resumed, last, *refs):
    refs = list(refs)
    pieces = [refs.pop(0) for step in steps]
    w_ref = refs.pop(0)
    sums = [refs.pop(0)[:, pl.ds(pl.multiple_of(first + pl.program_id(0) * tile, tile), tile)]] if resumed else []
    width = pieces[0].shape[1]
    member = lax.rem(lax.axis_index("ctx"), group)
    start = pl.multiple_of(first + pl.program_id(0) * tile, tile)
    weights = jnp.concatenate(
        [w_ref[pl.ds(pl.multiple_of((member ^ step) * width, width), width), pl.ds(start, tile)] for step in steps],
        axis=0,
    )
    rows = jnp.concatenate([piece[...] for piece in pieces], axis=1)
    product = sum(sums, jnp.dot(rows, weights, preferred_element_type=jnp.float32))
    if not last:
        refs[0][:, pl.ds(start, tile)] = product
        return
    give_ref, keep_ref = refs
    product = product.astype(jnp.bfloat16)
    block = product.shape[0] // 2
    low_first = lax.axis_index("head") == 0
    keep_ref[...] = jnp.where(low_first, product[:block], product[block:])
    give_ref[...] = jnp.where(low_first, product[block:], product[:block])


def project(group, steps, pieces, w_out, first, columns, tile, sums=None, last=True):
    rows, width = pieces[0].shape
    depth = width * len(steps)
    if last:
        spec = pl.BlockSpec((rows // 2, tile), lambda step: (0, step))
        out_specs = [spec, spec]
        out_shape = [jax.ShapeDtypeStruct((rows // 2, columns), jnp.bfloat16)] * 2
    else:
        out_specs = VMEM
        out_shape = pltpu.VMEM((rows, columns), jnp.float32)
    operands = [*pieces, w_out]
    if sums is not None:
        operands.append(sums)
    return pl.pallas_call(
        partial(project_kernel, group, steps, first, tile, sums is not None, last),
        out_shape=out_shape,
        grid=(columns // tile,),
        in_specs=[VMEM] * len(operands),
        out_specs=out_specs,
        compiler_params=params(10 * 1024 * 1024),
        cost_estimate=pl.CostEstimate(
            flops=2 * rows * depth * columns, transcendentals=0, bytes_accessed=4 * rows * columns
        ),
    )(*operands)


def sum_kernel(*refs):
    summed = refs[0][...].astype(jnp.float32) + refs[1][...].astype(jnp.float32)
    refs[-1][...] = summed.astype(jnp.bfloat16)


def sum_half(keep, got, half, columns, total):
    rows, size = keep.shape
    operands = [keep, got] + ([] if total is None else [total])
    return pl.pallas_call(
        sum_kernel,
        out_shape=jax.ShapeDtypeStruct((rows, columns), jnp.bfloat16),
        grid=(1,),
        in_specs=[pl.BlockSpec((rows, size), lambda step: (0, 0))] * 2 + [HBM] * (len(operands) - 2),
        out_specs=pl.BlockSpec((rows, size), lambda step: (0, half)),
        input_output_aliases={} if total is None else {2: 0},
        compiler_params=params(10 * 1024 * 1024),
    )(*operands)


def shards(queries, key_heads, value_heads, doc_units, w_out):
    count = lax.axis_size("ctx")
    group = key_heads.shape[1] // HD
    hops = min(16, count // 2) // group
    tokens, depth = queries.shape
    width = depth // group
    rank = lax.axis_index("ctx")
    member = lax.rem(rank, group)

    def column_block(value, step, size):
        return lax.dynamic_slice(value, (0, (member ^ step) * size), (tokens, size))

    def swap(value, step):
        if step == 0:
            return value
        return lax.ppermute(value, "ctx", [(source, source ^ step) for source in range(count)])

    def next_plane(value):
        return lax.ppermute(value, "ctx", [(source, source + group) for source in range(count - group)])

    def own_plane(value):
        pieces = [swap(column_block(value, step, HD), step) for step in range(group)]
        return pack_rows(pieces) if group > 1 else pieces[0]

    keys, values = [own_plane(key_heads)], [own_plane(value_heads)]
    queries = lax.optimization_barrier((queries, keys, values))[0]
    query_pieces = [swap(column_block(queries, step, width), step) for step in range(group)]
    keys = [next_plane(keys[0])] + keys
    values = [next_plane(values[0])] + values
    if group > 1:
        keys, values, query_pieces[-1] = lax.optimization_barrier((keys, values, query_pieces[-1]))
    for hop in range(hops - 1):
        keys = [next_plane(keys[0])] + keys
        values = [next_plane(values[0])] + values
    if group == 1:
        keys, values = [jnp.concatenate(keys, axis=0)], [jnp.concatenate(values, axis=0)]

    def place_in_vmem(arrays):
        return [pltpu.with_memory_space_constraint(array, pltpu.VMEM) for array in arrays]

    keys, values = place_in_vmem(keys), place_in_vmem(values)
    w_here = w_out
    attention = [None] * group
    far = tuple(range(group - 1, 0, -1))
    if far:
        far_queries = [query_pieces[step] for step in far]
        *partials, state, w_here = attend("early", far, group, doc_units, far_queries, keys[-2:], values[-2:], w_out=w_out)
        finals = attend("late", far, group, doc_units, far_queries, keys, values, state=state, outs=partials)
        for step, final in zip(far, finals):
            attention[step] = swap(final, step)
        query_pieces, finals = lax.optimization_barrier((query_pieces, finals))
    (attention[0],) = attend("full", (0,), group, doc_units, query_pieces[:1], keys, values)
    columns = w_out.shape[1]
    if lax.axis_size("head") == 2:
        w_here = pltpu.with_memory_space_constraint(w_here, pltpu.VMEM)
        soon = (0,) + far[:1]
        rest = tuple(step for step in range(group) if step not in soon)
        sums = None
        if rest:
            sums = project(
                group, soon, [attention[step] for step in soon], w_here, 0, columns, 512, last=False
            )
            sums = pltpu.with_memory_space_constraint(sums, pltpu.VMEM)
        else:
            rest = soon
        size = columns // 2
        keeps, gots = [], []
        for half in range(2):
            give, keep = project(
                group, rest, [attention[step] for step in rest], w_here, half * size, size, 512, sums=sums
            )
            keeps.append(keep)
            gots.append(lax.ppermute(give, "head", [(0, 1), (1, 0)]))
        total = None
        for half in range(2):
            total = sum_half(keeps[half], gots[half], half, columns, total)
        return total
    product = sum(
        jnp.dot(
            attention[step],
            lax.dynamic_slice(w_out, ((member ^ step) * width, 0), (width, columns)),
            preferred_element_type=jnp.float32,
        )
        for step in range(group)
    )
    return lax.psum_scatter(product.astype(jnp.bfloat16), "head", scatter_dimension=0, tiled=True)


def solution(mesh):
    in_specs = (P("ctx", "head"), P("ctx", "head"), P("ctx", "head"), P(), P("head", None))
    out_specs = P(("ctx", "head"), None)
    return jax.shard_map(shards, mesh=mesh, in_specs=in_specs, out_specs=out_specs, check_vma=False)
```

```python
from functools import partial
import math

import jax
import jax.numpy as jnp
from jax import lax
from jax.experimental import pallas as pl
from jax.experimental.pallas import tpu as pltpu
from jax.sharding import PartitionSpec as P

HD = 128
UNIT = 128
CHUNK_UNITS = 6
LOW = -1e30
LARGE = 2.0**90
VMEM_LIMIT = 24 * 1024 * 1024
HBM = pl.BlockSpec(memory_space=pl.ANY)
SMEM = pl.BlockSpec(memory_space=pltpu.SMEM)
VMEM = pl.BlockSpec(memory_space=pltpu.VMEM)


def params(limit=VMEM_LIMIT):
    return pltpu.CompilerParams(vmem_limit_bytes=limit)


def pack_kernel(group, *refs):
    packed = refs[group]
    rows = refs[0].shape[0]
    member = lax.rem(lax.axis_index("ctx"), group)
    for step in range(group):
        packed[pl.ds(pl.multiple_of((member ^ step) * rows, rows), rows), :] = refs[step][...]


def pack_rows(pieces):
    group = len(pieces)
    rows, columns = pieces[0].shape
    return pl.pallas_call(
        partial(pack_kernel, group),
        out_shape=jax.ShapeDtypeStruct((rows * group, columns), pieces[0].dtype),
        compiler_params=params(),
    )(*pieces)


def attention_kernel(mode, steps, group, regions, heads, docs, *refs):
    refs = list(refs)

    def take(number):
        taken = refs[:number]
        del refs[:number]
        return taken

    pieces = len(steps)
    early, late = mode == "early", mode == "late"
    (docs_ref,) = take(1)
    queries = take(pieces)
    keys = take(regions)
    values = take(regions)
    if early:
        (w_from,) = take(1)
    if late:
        (state,) = take(1)
        take(pieces)
    outs = take(pieces)
    if early:
        state, w_to = take(2)
    q_rows, o_buf, shift, total, out_sem = refs
    tokens = queries[0].shape[0]
    units = tokens // UNIT
    sizes = [key.shape[0] // UNIT for key in keys]
    bases = [sum(sizes[:region]) for region in range(regions)]
    chunk_units = CHUNK_UNITS if sizes[0] % CHUNK_UNITS == 0 and not late else units
    chunk = chunk_units * UNIT
    rank = lax.axis_index("ctx")
    member = lax.rem(rank, group)
    first_unit = (rank - member + group) * units - sum(sizes)
    unseen = 0 if early else bases[1] if late else None
    visited = keys[:1] if late else keys
    scale = math.log2(math.e) / math.sqrt(HD)

    def place(piece):
        here = (rank ^ (steps[0] - piece)) * units
        starts = []
        for unit in range(units):
            doc_first = jnp.int32(0)
            end = jnp.int32(0)
            for doc in range(docs):
                end = end + docs_ref[doc]
                doc_first = jnp.where(end <= here + unit, end, doc_first)
            starts.append(doc_first - first_unit)
        return here - first_unit, starts

    def one_piece(piece):
        ones = jnp.ones((chunk, HD), jnp.bfloat16)
        square = jnp.ones((HD, HD), jnp.bfloat16)
        first_row, starts = place(piece)
        lows = [jnp.maximum(start, 0) for start in starts]
        low, high, stop = lows[0], lows[-1], first_row + units

        for number in range(pieces):

            @pl.when(piece == number)
            def _(number=number):
                for head in range(heads):
                    q_rows[head * tokens:(head + 1) * tokens, :] = queries[number][:, head * HD:(head + 1) * HD]

        query = q_rows[...]

        def scores_of(region, number, masked, query):
            begin_unit = bases[region] + number * chunk_units
            begin = pl.multiple_of(number * chunk, chunk)
            key = keys[region][pl.ds(begin, chunk), :]
            value = jnp.concatenate([values[region][pl.ds(begin, chunk), :], ones], axis=1)
            scores = lax.dot_general(query, key, (((1,), (1,)), ((), ())), preferred_element_type=jnp.float32)
            if masked:
                column = lax.broadcasted_iota(jnp.int32, (UNIT, chunk), 1)
                ahead = column - lax.broadcasted_iota(jnp.int32, (UNIT, chunk), 0)
                allowed = [
                    (column >= (lows[unit] - begin_unit) * UNIT) & (ahead <= (first_row + unit - begin_unit) * UNIT)
                    for unit in range(units)
                ]
                scores = jnp.concatenate([
                    jnp.where(allowed[part % units], scores[part * UNIT:(part + 1) * UNIT], LOW)
                    for part in range(query.shape[0] // UNIT)
                ], axis=0)
            return scores, value

        own_start = pl.multiple_of((first_row - bases[-1]) * UNIT, UNIT)
        own = query * jnp.concatenate([keys[-1][pl.ds(own_start, tokens), :]] * heads, axis=0)
        shift[...] = jnp.dot(own, square, preferred_element_type=jnp.float32) * scale
        if late:
            total[...] = state[piece]
        else:
            total[...] = jnp.zeros(total.shape, jnp.float32)

        def visit(region, number, masked):
            scores, value = scores_of(region, number, masked, query)
            shifts = jnp.concatenate([shift[...]] * chunk_units, axis=1)
            weights = jnp.exp2(scores * scale - shifts).astype(jnp.bfloat16)
            total[...] += jnp.dot(weights, value, preferred_element_type=jnp.float32)

        def span(region):
            count = sizes[region] // chunk_units
            first = jnp.clip((low - bases[region]) // chunk_units, 0, count)
            last = jnp.clip((stop - bases[region] + chunk_units - 1) // chunk_units, 0, count)
            return first, jnp.maximum(first, last)

        for region in range(len(visited)):
            first, last = span(region)
            inner = jnp.clip((high - bases[region] + chunk_units - 1) // chunk_units, first, last)
            outer = jnp.clip((first_row - bases[region]) // chunk_units, inner, last)

            def masked_visit(number, carry, region=region, first=first, inner=inner, outer=outer):
                at = first + number
                visit(region, jnp.where(at < inner, at, at - inner + outer), True)
                return carry

            def plain_visit(number, carry, region=region):
                visit(region, number, False)
                return carry

            lax.fori_loop(0, inner - first + last - outer, masked_visit, 0)
            lax.fori_loop(inner, outer, plain_visit, 0)

        overflow = jnp.logical_not(jnp.max(total[:, HD:]) < LARGE)
        if early:
            unfinished = starts[0] < unseen
            overflow = overflow & jnp.logical_not(unfinished)

            @pl.when(unfinished)
            def _():
                state[piece] = total[...]

        @pl.when(overflow)
        def _():
            shift[...] = jnp.full(shift.shape, LOW, jnp.float32)
            total[...] = jnp.zeros(total.shape, jnp.float32)

            for region in reversed(range(regions)):
                first, last = span(region)

                def careful(number, carry, region=region, first=first):
                    head = lax.rem(number, heads)
                    some = pl.ds(pl.multiple_of(head * tokens, tokens), tokens)
                    scores, value = scores_of(region, first + number // heads, True, q_rows[some, :])
                    old = shift[some, :]
                    new = jnp.maximum(old, jnp.max(scores, axis=1, keepdims=True))
                    weights = jnp.exp2((scores - new[:, :1]) * scale).astype(jnp.bfloat16)
                    shrink = jnp.exp2((old - new) * scale)
                    update = jnp.dot(weights, value, preferred_element_type=jnp.float32)
                    total[some, :] = total[some, :] * jnp.concatenate([shrink] * 2, axis=1) + update
                    shift[some, :] = new
                    return carry

                lax.fori_loop(0, (last - first) * heads, careful, 0)

        result = (total[:, :HD] / total[:, HD:]).astype(jnp.bfloat16)
        for head in range(heads):
            o_buf[piece, :, head * HD:(head + 1) * HD] = result[head * tokens:(head + 1) * tokens]

    if late:
        def needs(piece):
            return place(piece)[1][0] < unseen

        @pl.when(sum(needs(jnp.int32(piece)).astype(jnp.int32) for piece in range(pieces)) > 0)
        def _():
            def maybe(piece, carry):
                @pl.when(needs(piece))
                def _():
                    one_piece(piece)
                    for number in range(pieces):

                        @pl.when(piece == number)
                        def _(number=number):
                            pltpu.make_async_copy(o_buf.at[number], outs[number], out_sem.at[number]).start()

                return carry

            lax.fori_loop(0, pieces, maybe, 0)
            for number in range(pieces):

                @pl.when(needs(jnp.int32(number)))
                def _(number=number):
                    pltpu.make_async_copy(o_buf.at[number], outs[number], out_sem.at[number]).wait()
    else:
        if early:
            w_copy = pltpu.make_async_copy(w_from, w_to, out_sem.at[pieces])
            w_copy.start()
        def always(piece, carry):
            one_piece(piece)
            for number in range(pieces):

                @pl.when(piece == number)
                def _(number=number):
                    pltpu.make_async_copy(o_buf.at[number], outs[number], out_sem.at[number]).start()

            return carry

        lax.fori_loop(0, pieces, always, 0)
        for number in range(pieces):
            pltpu.make_async_copy(o_buf.at[number], outs[number], out_sem.at[number]).wait()
        if early:
            w_copy.wait()


def attend(mode, steps, group, doc_units, queries, keys, values, w_out=None, state=None, outs=None):
    pieces = len(steps)
    regions = len(keys)
    tokens, width = queries[0].shape
    heads = width // HD
    rows = heads * tokens
    seen = sum(key.shape[0] for key in (keys[:1] if mode == "late" else keys))
    scores = rows * pieces * seen // 2
    operands = [doc_units, *queries, *keys, *values]
    in_specs = [SMEM] + [VMEM] * (pieces + 2 * regions)
    out_shape = [jax.ShapeDtypeStruct((tokens, width), jnp.bfloat16)] * pieces
    out_specs = [HBM] * pieces
    aliases = {}
    moved = 4 * tokens * pieces * width
    if mode == "early":
        operands += [w_out]
        in_specs += [HBM]
        out_shape += [pltpu.VMEM((pieces, rows, 2 * HD), jnp.float32), pltpu.VMEM(w_out.shape, w_out.dtype)]
        out_specs += [VMEM, VMEM]
        moved += 2 * w_out.size
    if mode == "late":
        aliases = {len(operands) + 1 + piece: piece for piece in range(pieces)}
        operands += [pltpu.with_memory_space_constraint(state, pltpu.VMEM), *outs]
        in_specs += [VMEM] + [HBM] * pieces
    return pl.pallas_call(
        partial(attention_kernel, mode, steps, group, regions, heads, doc_units.shape[0]),
        out_shape=out_shape,
        in_specs=in_specs,
        out_specs=out_specs,
        scratch_shapes=[
            pltpu.VMEM((rows, HD), jnp.bfloat16),
            pltpu.VMEM((pieces, tokens, width), jnp.bfloat16),
            pltpu.VMEM((rows, HD), jnp.float32),
            pltpu.VMEM((rows, 2 * HD), jnp.float32),
            pltpu.SemaphoreType.DMA((pieces + 1,)),
        ],
        input_output_aliases=aliases,
        compiler_params=params(),
        cost_estimate=pl.CostEstimate(flops=4 * HD * scores, transcendentals=scores, bytes_accessed=moved),
    )(*operands)


def project_kernel(group, steps, first, tile, resumed, last, *refs):
    refs = list(refs)
    pieces = [refs.pop(0) for step in steps]
    w_ref = refs.pop(0)
    sums = [refs.pop(0)[:, pl.ds(pl.multiple_of(first + pl.program_id(0) * tile, tile), tile)]] if resumed else []
    width = pieces[0].shape[1]
    member = lax.rem(lax.axis_index("ctx"), group)
    start = pl.multiple_of(first + pl.program_id(0) * tile, tile)
    weights = jnp.concatenate(
        [w_ref[pl.ds(pl.multiple_of((member ^ step) * width, width), width), pl.ds(start, tile)] for step in steps],
        axis=0,
    )
    rows = jnp.concatenate([piece[...] for piece in pieces], axis=1)
    product = sum(sums, jnp.dot(rows, weights, preferred_element_type=jnp.float32))
    if not last:
        refs[0][:, pl.ds(start, tile)] = product
        return
    give_ref, keep_ref = refs
    product = product.astype(jnp.bfloat16)
    block = product.shape[0] // 2
    low_first = lax.axis_index("head") == 0
    keep_ref[...] = jnp.where(low_first, product[:block], product[block:])
    give_ref[...] = jnp.where(low_first, product[block:], product[:block])


def project(group, steps, pieces, w_out, first, columns, tile, sums=None, last=True):
    rows, width = pieces[0].shape
    depth = width * len(steps)
    if last:
        spec = pl.BlockSpec((rows // 2, tile), lambda step: (0, step))
        out_specs = [spec, spec]
        out_shape = [jax.ShapeDtypeStruct((rows // 2, columns), jnp.bfloat16)] * 2
    else:
        out_specs = VMEM
        out_shape = pltpu.VMEM((rows, columns), jnp.float32)
    operands = [*pieces, w_out]
    if sums is not None:
        operands.append(sums)
    return pl.pallas_call(
        partial(project_kernel, group, steps, first, tile, sums is not None, last),
        out_shape=out_shape,
        grid=(columns // tile,),
        in_specs=[VMEM] * len(operands),
        out_specs=out_specs,
        compiler_params=params(10 * 1024 * 1024),
        cost_estimate=pl.CostEstimate(
            flops=2 * rows * depth * columns, transcendentals=0, bytes_accessed=4 * rows * columns
        ),
    )(*operands)


def sum_kernel(*refs):
    summed = refs[0][...].astype(jnp.float32) + refs[1][...].astype(jnp.float32)
    refs[-1][...] = summed.astype(jnp.bfloat16)


def sum_half(keep, got, half, columns, total):
    rows, size = keep.shape
    operands = [keep, got] + ([] if total is None else [total])
    return pl.pallas_call(
        sum_kernel,
        out_shape=jax.ShapeDtypeStruct((rows, columns), jnp.bfloat16),
        grid=(1,),
        in_specs=[pl.BlockSpec((rows, size), lambda step: (0, 0))] * 2 + [HBM] * (len(operands) - 2),
        out_specs=pl.BlockSpec((rows, size), lambda step: (0, half)),
        input_output_aliases={} if total is None else {2: 0},
        compiler_params=params(10 * 1024 * 1024),
    )(*operands)


def shards(queries, key_heads, value_heads, doc_units, w_out):
    count = lax.axis_size("ctx")
    group = key_heads.shape[1] // HD
    hops = min(16, count // 2) // group
    tokens, depth = queries.shape
    width = depth // group
    rank = lax.axis_index("ctx")
    member = lax.rem(rank, group)

    def column_block(value, step, size):
        return lax.dynamic_slice(value, (0, (member ^ step) * size), (tokens, size))

    def swap(value, step):
        if step == 0:
            return value
        return lax.ppermute(value, "ctx", [(source, source ^ step) for source in range(count)])

    def next_plane(value):
        return lax.ppermute(value, "ctx", [(source, source + group) for source in range(count - group)])

    def own_plane(value):
        pieces = [swap(column_block(value, step, HD), step) for step in range(group)]
        return pack_rows(pieces) if group > 1 else pieces[0]

    keys, values = [own_plane(key_heads)], [own_plane(value_heads)]
    queries = lax.optimization_barrier((queries, keys, values))[0]
    query_pieces = [swap(column_block(queries, step, width), step) for step in range(group)]
    keys = [next_plane(keys[0])] + keys
    values = [next_plane(values[0])] + values
    if group > 1:
        keys, values, query_pieces[-1] = lax.optimization_barrier((keys, values, query_pieces[-1]))
    for hop in range(hops - 1):
        keys = [next_plane(keys[0])] + keys
        values = [next_plane(values[0])] + values
    if group == 1:
        keys, values = [jnp.concatenate(keys, axis=0)], [jnp.concatenate(values, axis=0)]

    def place_in_vmem(arrays):
        return [pltpu.with_memory_space_constraint(array, pltpu.VMEM) for array in arrays]

    keys, values = place_in_vmem(keys), place_in_vmem(values)
    w_here = w_out
    attention = [None] * group
    far = tuple(range(group - 1, 0, -1))
    if far:
        far_queries = [query_pieces[step] for step in far]
        *partials, state, w_here = attend("early", far, group, doc_units, far_queries, keys[-2:], values[-2:], w_out=w_out)
        finals = attend("late", far, group, doc_units, far_queries, keys, values, state=state, outs=partials)
        for step, final in zip(far, finals):
            attention[step] = swap(final, step)
        query_pieces, finals = lax.optimization_barrier((query_pieces, finals))
    (attention[0],) = attend("full", (0,), group, doc_units, query_pieces[:1], keys, values)
    columns = w_out.shape[1]
    if lax.axis_size("head") == 2:
        w_here = pltpu.with_memory_space_constraint(w_here, pltpu.VMEM)
        soon = (0,) + far[:1]
        rest = tuple(step for step in range(group) if step not in soon)
        sums = None
        if rest:
            sums = project(
                group, soon, [attention[step] for step in soon], w_here, 0, columns, 1024, last=False
            )
            sums = pltpu.with_memory_space_constraint(sums, pltpu.VMEM)
        else:
            rest = soon
        size = columns // 2
        keeps, gots = [], []
        for half in range(2):
            give, keep = project(
                group, rest, [attention[step] for step in rest], w_here, half * size, size, 1024, sums=sums
            )
            keeps.append(keep)
            gots.append(lax.ppermute(give, "head", [(0, 1), (1, 0)]))
        total = None
        for half in range(2):
            total = sum_half(keeps[half], gots[half], half, columns, total)
        return total
    product = sum(
        jnp.dot(
            attention[step],
            lax.dynamic_slice(w_out, ((member ^ step) * width, 0), (width, columns)),
            preferred_element_type=jnp.float32,
        )
        for step in range(group)
    )
    return lax.psum_scatter(product.astype(jnp.bfloat16), "head", scatter_dimension=0, tiled=True)


def solution(mesh):
    in_specs = (P("ctx", "head"), P("ctx", "head"), P("ctx", "head"), P(), P("head", None))
    out_specs = P(("ctx", "head"), None)
    return jax.shard_map(shards, mesh=mesh, in_specs=in_specs, out_specs=out_specs, check_vma=False)
```
